128 devices in a mesh: ag: 16 (over y, z_lo, core), tm: 8 (over z_hi, x).
Axes of the slice: x: 4, y: 4, z: 4 (z_hi: 2, z_lo: 2; z = z_hi * 2 + z_lo), core: 2. Of those that a mesh axis runs over, the one named last changes fastest.
Arguments:
- tokens: bfloat16 [1, 256, 128, 1024], P(None, 'ag', 'tm'), may hold values from -6 to 6
- cotangent: bfloat16 [1, 256, 128, 1024], P(None, 'ag', 'tm'), may hold values from -6 to 6
- observed: int32 [1, 256, 128], replicated, may hold values from 0 to 1, as said below
- time_qkv: bfloat16 [1024, 3072], replicated, may hold values from -12 to 12
- time_out: bfloat16 [1024, 1024], replicated, may hold values from -0.1875 to 0.1875
- agent_qkv: bfloat16 [1024, 3072], replicated, may hold values from -12 to 12
- agent_out: bfloat16 [1024, 1024], replicated, may hold values from -0.1875 to 0.1875
Outputs:
- grad_tokens: bfloat16 [1, 256, 128, 1024], P(None, 'ag', 'tm')
- grad_time_qkv: float32 [1024, 3072], P(('ag', 'tm'))
- grad_time_out: float32 [1024, 1024], P(('ag', 'tm'))
- grad_agent_qkv: float32 [1024, 3072], P(('ag', 'tm'))
- grad_agent_out: float32 [1024, 1024], P(('ag', 'tm'))
The draws below stay inside these ranges and needn't reach their ends.
Inputs may be any that keep to these rules, and one draw needn't show every extreme that they name: 1 marks an observed step of a present agent; each scene's present agents come first, each observed over one run of steps.
All inputs are finite; a program needn't handle non-finite values.
Results may differ from the reference program's by a relative error of at most 0.012.
Values may be sent and summed in bfloat16 or wider, within the bound.
A program may use at most 192 MiB of HBM per device.

```python
import math
import jax
import jax.numpy as jnp
from jax import lax

D = 1024
H = 16
HD = 64
SCENES = 1
A = 256
STEPS = 128


def draw_observed(key, part):
    first_key, second_key, third_key = jax.random.split(jax.random.fold_in(key, 7), 3)
    present = jax.random.randint(first_key, (SCENES, 1, 1), A // 2, A + 1)
    begin = jax.random.randint(second_key, (SCENES, A, 1), 0, STEPS // 2)
    span = jax.random.randint(third_key, (SCENES, A, 1), STEPS // 4, STEPS + 1)
    agent_ids = jnp.arange(A)[None, :, None]
    step_ids = jnp.arange(STEPS)[None, None, :]
    keep = (agent_ids < present) & (step_ids >= begin) & (step_ids < begin + span)
    return keep.astype(jnp.int32)


def projection_weight(key):
    bound = 6.0 / math.sqrt(D)
    matrix = jnp.clip(jax.random.normal(key, (D, 3 * D), jnp.float32) / math.sqrt(D), -bound, bound)
    return jnp.clip(matrix, -12.0, 12.0).astype(jnp.bfloat16)


def draw_time_qkv(key, part):
    return projection_weight(jax.random.fold_in(key, 11))


def draw_agent_qkv(key, part):
    return projection_weight(jax.random.fold_in(key, 12))


def shard_levels(own_key, dims, cuts, low, top_value):
    def one(axis_at, parts):
        steps = jax.random.uniform(jax.random.fold_in(jax.random.fold_in(own_key, 6), axis_at), (parts,), jnp.float32, low / len(cuts), top_value / len(cuts))
        return jnp.repeat(jnp.exp(steps), dims[axis_at] // parts).reshape((-1,) + (1,) * (len(dims) - axis_at - 1))

    gain = one(*cuts[0])
    for cut in cuts[1:]:
        gain = gain * one(*cut)
    return gain


def bell_draw(own_key, dims, width, most, cuts=(), dtype=jnp.bfloat16):
    values = jax.random.normal(own_key, dims, jnp.float32) * width
    if len(cuts) > 0:
        values = shard_levels(own_key, dims, cuts, -0.22, 0.18) * values
    return jnp.clip(values, min=-most, max=most).astype(dtype)


def setup_inputs(seed: int = 0) -> dict:
    keys = jax.random.split(jax.random.key(seed), 8)
    tokens = bell_draw(keys[0], (SCENES, A, STEPS, D), 1.0, 6.0, ((1, 16), (2, 8)))
    cotangent = bell_draw(keys[1], (SCENES, A, STEPS, D), 1.0, 6.0, ((1, 16), (2, 8)))
    observed = draw_observed(jax.random.fold_in(keys[7], 71), 0)
    time_qkv = draw_time_qkv(jax.random.fold_in(keys[7], 71), 0)
    time_out = bell_draw(keys[4], (D, D), D ** -0.5, 0.1875)
    agent_qkv = draw_agent_qkv(jax.random.fold_in(keys[7], 71), 0)
    agent_out = bell_draw(keys[6], (D, D), D ** -0.5, 0.1875)
    return dict(tokens=tokens, cotangent=cotangent, observed=observed, time_qkv=time_qkv, time_out=time_out, agent_qkv=agent_qkv, agent_out=agent_out)


epsilon = 1e-06
masked_score = -1e+30

def normalize(token_rows):
    widened = token_rows.astype(jnp.float32)
    inverse = lax.rsqrt(lax.optimization_barrier(jnp.mean(widened * widened, axis=-1, keepdims=True)) + epsilon)
    return (widened * inverse, inverse)

def head_split(merged_qkv, which_part):
    batch_size, length, across = merged_qkv.shape[:3]
    member = merged_qkv[..., which_part * D:(which_part + 1) * D]
    return member.reshape(batch_size, length, across, H, HD).astype(jnp.float32)

def allowed_pairs(observed):
    key_seen = jnp.transpose(observed, (0, 2, 1))[:, :, None, :] > 0
    length = observed.shape[1]
    same_slot = jnp.arange(length)[:, None] == jnp.arange(length)[None, :]
    return key_seen | same_slot

def attention_probs(merged_qkv, allowed):
    queries = head_split(merged_qkv, 0)
    keys_part = head_split(merged_qkv, 1)
    scores = jnp.einsum('bqche,bkche->bchqk', queries, keys_part) * HD ** (-0.5)
    scores = jnp.where(allowed[:, :, None], scores, masked_score)
    shifted = jnp.exp(scores - lax.optimization_barrier(jnp.max(scores, axis=-1, keepdims=True)))
    return shifted / lax.optimization_barrier(jnp.sum(shifted, axis=-1, keepdims=True))

def attention_forward(merged_qkv, allowed):
    probability = attention_probs(merged_qkv, allowed)
    rounded = lax.optimization_barrier(probability.astype(jnp.bfloat16)).astype(jnp.float32)
    values_part = head_split(merged_qkv, 2)
    mixed_heads = jnp.einsum('bchqk,bkche->bqche', rounded, values_part)
    batch_size, length, across = merged_qkv.shape[:3]
    return mixed_heads.reshape(batch_size, length, across, D).astype(jnp.bfloat16)

def attention_backward(merged_qkv, allowed, grad_mixed):
    probability = attention_probs(merged_qkv, allowed)
    rounded = lax.optimization_barrier(probability.astype(jnp.bfloat16)).astype(jnp.float32)
    queries = head_split(merged_qkv, 0)
    keys_part = head_split(merged_qkv, 1)
    values_part = head_split(merged_qkv, 2)
    batch_size, length, across = merged_qkv.shape[:3]
    grad_heads = grad_mixed.reshape(batch_size, length, across, H, HD).astype(jnp.float32)
    grad_probs = jnp.einsum('bqche,bkche->bchqk', grad_heads, values_part)
    grad_values = jnp.einsum('bchqk,bqche->bkche', rounded, grad_heads)
    grad_scores = probability * (grad_probs - lax.optimization_barrier(jnp.sum(grad_probs * probability, axis=-1, keepdims=True))) * HD ** (-0.5)
    grad_scores = lax.optimization_barrier(grad_scores.astype(jnp.bfloat16)).astype(jnp.float32)
    grad_queries = jnp.einsum('bchqk,bkche->bqche', grad_scores, keys_part)
    grad_keys = jnp.einsum('bchqk,bqche->bkche', grad_scores, queries)
    joined = jnp.concatenate([member.reshape(batch_size, length, across, D) for member in (grad_queries, grad_keys, grad_values)], axis=-1)
    return joined.astype(jnp.bfloat16)

def project_in(tokens_view, weight_qkv):
    normed, inverse = normalize(tokens_view)
    unit_rows = normed.astype(jnp.bfloat16)
    merged_qkv = jnp.dot(unit_rows.reshape(-1, D), weight_qkv, preferred_element_type=jnp.float32).astype(jnp.bfloat16)
    return (normed, inverse, unit_rows, merged_qkv.reshape(tokens_view.shape[:3] + (3 * D,)))

def sublayer_forward(tokens_view, weight_qkv, weight_out, allowed):
    normed, inverse, unit_rows, merged_qkv = project_in(tokens_view, weight_qkv)
    mixed_heads = attention_forward(merged_qkv, allowed)
    update = jnp.dot(mixed_heads.reshape(-1, D), weight_out, preferred_element_type=jnp.float32).reshape(tokens_view.shape)
    return (tokens_view.astype(jnp.float32) + update).astype(jnp.bfloat16)

def sublayer_backward(tokens_view, weight_qkv, weight_out, allowed, upstream):
    normed, inverse, unit_rows, merged_qkv = project_in(tokens_view, weight_qkv)
    mixed_heads = attention_forward(merged_qkv, allowed)
    flat_up = upstream.reshape(-1, D)
    grad_mixed = jnp.dot(flat_up, weight_out.T, preferred_element_type=jnp.float32).astype(jnp.bfloat16).reshape(tokens_view.shape)
    grad_out = jnp.dot(mixed_heads.reshape(-1, D).T, flat_up, preferred_element_type=jnp.float32)
    grad_merged = attention_backward(merged_qkv, allowed, grad_mixed).reshape(-1, 3 * D)
    grad_qkv = jnp.dot(unit_rows.reshape(-1, D).T, grad_merged, preferred_element_type=jnp.float32)
    grad_unit = jnp.dot(grad_merged, weight_qkv.T, preferred_element_type=jnp.float32).reshape(tokens_view.shape)
    grad_rows = inverse * (grad_unit - normed * lax.optimization_barrier(jnp.mean(grad_unit * normed, axis=-1, keepdims=True)))
    grad_input = (upstream.astype(jnp.float32) + grad_rows).astype(jnp.bfloat16)
    return (grad_input, grad_qkv, grad_out)

def reference(tokens, cotangent, observed, time_qkv, time_out, agent_qkv, agent_out):
    seq_block = 16
    time_blocks = SCENES * A // seq_block
    time_tokens = tokens.reshape(time_blocks, seq_block, STEPS, 1, D)
    time_seen = observed.reshape(time_blocks, seq_block, STEPS, 1)

    def time_forward(block_args):
        return sublayer_forward(block_args[0], time_qkv, time_out, allowed_pairs(block_args[1]))
    first_out = lax.map(time_forward, (time_tokens, time_seen)).reshape(SCENES, A, STEPS, D)
    step_block = 8
    agent_blocks = STEPS // step_block
    agent_first = jnp.moveaxis(first_out.reshape(SCENES, A, agent_blocks, step_block, D), 2, 0)
    agent_up = jnp.moveaxis(cotangent.reshape(SCENES, A, agent_blocks, step_block, D), 2, 0)
    agent_seen = jnp.moveaxis(observed.reshape(SCENES, A, agent_blocks, step_block), 2, 0)
    zero_qkv = jnp.zeros((D, 3 * D), jnp.float32)
    zero_out = jnp.zeros((D, D), jnp.float32)

    def agent_step(running, block_args):
        grad_input, grad_qkv, grad_out = sublayer_backward(block_args[0], agent_qkv, agent_out, allowed_pairs(block_args[2]), block_args[1])
        return ((running[0] + grad_qkv, running[1] + grad_out), grad_input)
    agent_sums, grad_first = lax.scan(agent_step, (zero_qkv, zero_out), (agent_first, agent_up, agent_seen))
    grad_first = jnp.moveaxis(grad_first, 0, 2).reshape(time_blocks, seq_block, STEPS, 1, D)

    def time_step(running, block_args):
        grad_input, grad_qkv, grad_out = sublayer_backward(block_args[0], time_qkv, time_out, allowed_pairs(block_args[2]), block_args[1])
        return ((running[0] + grad_qkv, running[1] + grad_out), grad_input)
    time_sums, grad_input = lax.scan(time_step, (zero_qkv, zero_out), (time_tokens, grad_first, time_seen))
    grad_tokens = grad_input.reshape(SCENES, A, STEPS, D)
    return (grad_tokens, time_sums[0], time_sums[1], agent_sums[0], agent_sums[1])
```

```python
import functools

import jax
import jax.numpy as jnp
from jax import lax
from jax.experimental import pallas as pl
from jax.experimental.pallas import tpu as pltpu
from jax.sharding import PartitionSpec as P


MESH = pl.DeviceIdType.MESH
BF = jnp.bfloat16
F32 = jnp.float32
NT = (((1,), (1,)), ((), ()))
TN = (((0,), (0,)), ((), ()))

STREAMS = ((0, 1408, "xyz"), (1408, 2816, "yzx"), (2816, 4096, "zyx"))


def matmul(left, right, dims=(((1,), (0,)), ((), ()))):
    return lax.dot_general(left, right, dims, preferred_element_type=F32)


class Place:
    def __init__(self):
        self.ag = lax.axis_index("ag")
        self.tm = lax.axis_index("tm")
        self.y = self.ag // 4
        self.zlo = (self.ag // 2) % 2
        self.core = self.ag % 2
        self.zhi = self.tm // 4
        self.x = self.tm % 4
        self.z = self.zhi * 2 + self.zlo

    def at(self, axis):
        return {"x": self.x, "y": self.y, "z": self.z}[axis]

    def ring(self, axis, step):
        if axis == "x":
            return (self.ag, self.zhi * 4 + (self.x + step) % 4)
        if axis == "y":
            return (((self.y + step) % 4) * 4 + self.ag % 4, self.tm)
        z = (self.z + step) % 4
        return (self.y * 4 + (z % 2) * 2 + self.core, (z // 2) * 4 + self.x)

    def twin(self):
        return (self.ag + 1 - 2 * self.core, self.tm)


def remote(src, dst, send, recv, device):
    return pltpu.make_async_remote_copy(
        src_ref=src, dst_ref=dst, send_sem=send, recv_sem=recv, device_id=device, device_id_type=MESH
    )


def greet(devices):
    barrier = pltpu.get_barrier_semaphore()
    for device in devices:
        pl.semaphore_signal(barrier, inc=1, device_id=device, device_id_type=MESH)
    pl.semaphore_wait(barrier, len(devices))


def selector(core, x_first):
    at = lax.broadcasted_iota(jnp.int32, (128, 256), 0)
    row = lax.broadcasted_iota(jnp.int32, (128, 256), 1)
    high, low = at // 32, (at // 8) % 4
    x, z = (high, low) if x_first else (low, high)
    wanted = (z % 2) * 128 + core * 64 + (z // 2) * 32 + x * 8 + at % 8
    return jnp.where(row == wanted, 1.0, 0.0).astype(BF)


class Twin:
    def __init__(self, place, send, recv):
        self.place, self.send, self.recv = place, send, recv

    def copy(self, slot, ref, cols=None):
        cols = slice(None) if cols is None else cols
        return remote(
            ref.at[0:256, cols], ref.at[256:512, cols], self.send.at[slot], self.recv.at[slot], self.place.twin()
        )


class Scatter:
    def __init__(self, place, bufs, send, recv):
        self.place = place
        self.g, self.own, self.r1, self.s2, self.r2, self.s3, self.r3 = bufs
        self.send, self.recv = send, recv

    def copy(self, stream, phase, step):
        lo, hi, axes = STREAMS[stream]
        cols = slice(lo, hi)
        axis = axes[phase]
        to = (self.place.at(axis) + step) % 4
        slot = step - 1
        if phase == 0:
            src, dst = self.g.at[slot, :, cols], self.r1.at[slot, :, cols]
        elif phase == 1:
            src = self.s2.at[pl.ds(pl.multiple_of(to * 32, 32), 32), cols]
            dst = self.r2.at[slot, :, cols]
        else:
            src = self.s3.at[pl.ds(pl.multiple_of(to * 8, 8), 8), cols]
            dst = self.r3.at[slot, :, cols]
        return remote(
            src,
            dst,
            self.send.at[stream, phase, slot],
            self.recv.at[stream, phase, slot],
            self.place.ring(axis, step),
        )

    def product(self, stream, ut, ut_mixed, gm, g, block):
        lo, hi, _ = STREAMS[stream]
        rows = pl.ds(pl.multiple_of(block * 128, 128), 128)
        if stream < 2:
            return [(lo, hi, matmul(ut[stream, rows, :], gm[:, lo:hi]))]
        return [
            (lo, 3072, matmul(ut[2, rows, :], gm[:, lo:3072])),
            (3072, 4096, matmul(ut_mixed[rows, :], g[...])),
        ]

    def start(self, stream, ut, ut_mixed, gm, g):
        at = self.place.at(STREAMS[stream][2][0])

        def one(step, carry):
            for lo, hi, part in self.product(stream, ut, ut_mixed, gm, g, (at + step) % 4):
                self.g[step - 1, :, lo:hi] = part.astype(BF)
            self.copy(stream, 0, step).start()
            return carry

        lax.fori_loop(1, 4, one, 0)
        for lo, hi, part in self.product(stream, ut, ut_mixed, gm, g, at):
            self.own[:, lo:hi] = part

    def second(self, stream):
        lo, hi, _ = STREAMS[stream]
        for step in (1, 2, 3):
            self.copy(stream, 0, step).wait_recv()

        def one(q, carry):
            rows = pl.ds(pl.multiple_of(q * 32, 32), 32)
            total = self.own[rows, lo:hi]
            for slot in range(3):
                total = total + self.r1[slot, rows, lo:hi].astype(F32)
            self.own[rows, lo:hi] = total
            self.s2[rows, lo:hi] = total.astype(BF)
            return carry

        lax.fori_loop(0, 4, one, 0)
        for step in (1, 2, 3):
            self.copy(stream, 1, step).start()

    def third(self, stream):
        lo, hi, axes = STREAMS[stream]
        for step in (1, 2, 3):
            self.copy(stream, 1, step).wait_recv()
        total = self.own[pl.ds(pl.multiple_of(self.place.at(axes[1]) * 32, 32), 32), lo:hi]
        for slot in range(3):
            total = total + self.r2[slot, :, lo:hi].astype(F32)
        self.s3[:, lo:hi] = total
        for step in (1, 2, 3):
            self.copy(stream, 2, step).start()

    def last(self, stream, qkv_ref, out_ref):
        lo, hi, axes = STREAMS[stream]
        for step in (1, 2, 3):
            self.copy(stream, 2, step).wait_recv()
        total = self.s3[pl.ds(pl.multiple_of(self.place.at(axes[2]) * 8, 8), 8), lo:hi]
        for slot in range(3):
            total = total + self.r3[slot, :, lo:hi]
        top = min(hi, 3072)
        qkv_ref[:, lo:top] = total[:, : top - lo]
        if hi > 3072:
            out_ref[...] = total[:, 3072 - lo :]

    def drain(self):
        for stream in range(3):
            for phase in range(3):
                for step in (1, 2, 3):
                    self.copy(stream, phase, step).wait_send()


def scatter_bufs():
    return [
        pltpu.VMEM((3, 128, 4096), BF),
        pltpu.VMEM((128, 4096), F32),
        pltpu.VMEM((3, 128, 4096), BF),
        pltpu.VMEM((128, 4096), BF),
        pltpu.VMEM((3, 32, 4096), BF),
        pltpu.VMEM((32, 4096), F32),
        pltpu.VMEM((3, 8, 4096), F32),
    ]


def transposed(place, unit, mixed, ut, ut_mixed):
    sel_x = selector(place.core, True)
    sel_z = selector(place.core, False)
    for y in range(4):
        cols = slice(y * 256, y * 256 + 256)
        part = matmul(sel_x, unit[:, cols], NT).astype(BF)
        for x in range(4):
            ut[0, x * 128 + y * 32 : x * 128 + y * 32 + 32, :] = part[x * 32 : x * 32 + 32]
        part = matmul(sel_z, unit[:, cols], NT).astype(BF)
        ut[1, y * 128 : y * 128 + 128, :] = part
        for z in range(4):
            ut[2, z * 128 + y * 32 : z * 128 + y * 32 + 32, :] = part[z * 32 : z * 32 + 32]
        part = matmul(sel_z, mixed[:, cols], NT).astype(BF)
        for z in range(4):
            ut_mixed[z * 128 + y * 32 : z * 128 + y * 32 + 32, :] = part[z * 32 : z * 32 + 32]


def scatter_kernel(
    t_unit, t_gm, t_mixed, t_g, a_unit, a_gm, a_mixed, a_g,
    tq_ref, to_ref, aq_ref, ao_ref,
    units, gms, mixeds, gs, ut, ut_mixed, *rest,
):
    bufs = (rest[:7], rest[7:14])
    twin_send, twin_recv, sc_send, sc_recv = rest[14:]
    place = Place()
    greet([place.twin()] + [place.ring(axis, step) for axis in "xyz" for step in (1, 2, 3)])
    scatters = []
    twins = []
    for s, ins in enumerate(((a_unit, a_gm, a_mixed, a_g), (t_unit, t_gm, t_mixed, t_g))):
        twin = Twin(place, twin_send.at[s], twin_recv.at[s])
        pair = (units.at[s], gms.at[s], mixeds.at[s], gs.at[s])
        for slot, (src, dst) in enumerate(zip(ins, pair)):
            dst[0:256, :] = src[...]
            twin.copy(slot, dst).start()
        twins.append((twin, pair))
    for s in range(2):
        twin, pair = twins[s]
        for slot in range(4):
            twin.copy(slot, pair[slot]).wait_recv()
        unit, gm, mixed, g = pair
        transposed(place, unit, mixed, ut, ut_mixed)
        scatter = Scatter(place, bufs[s], sc_send.at[s], sc_recv.at[s])
        for stream in range(3):
            scatter.start(stream, ut, ut_mixed, gm, g)
        scatters.append(scatter)
    for s in range(2):
        for stream in range(3):
            scatters[s].second(stream)
    for s in range(2):
        for stream in range(3):
            scatters[s].third(stream)
    outs = ((aq_ref, ao_ref), (tq_ref, to_ref))
    for s in range(2):
        for stream in range(3):
            scatters[s].last(stream, *outs[s])
    for s in range(2):
        scatters[s].drain()
        twin, pair = twins[s]
        for slot in range(4):
            twin.copy(slot, pair[slot]).wait_send()


def scatter_grads(time_terms, agent_terms):
    (t_unit, t_gm), (t_mixed, t_g) = time_terms
    (a_unit, a_gm), (a_mixed, a_g) = agent_terms
    return pl.pallas_call(
        scatter_kernel,
        out_shape=[
            jax.ShapeDtypeStruct((8, 3072), F32),
            jax.ShapeDtypeStruct((8, 1024), F32),
            jax.ShapeDtypeStruct((8, 3072), F32),
            jax.ShapeDtypeStruct((8, 1024), F32),
        ],
        in_specs=[pl.BlockSpec(memory_space=pltpu.VMEM)] * 8,
        out_specs=[pl.BlockSpec(memory_space=pltpu.VMEM)] * 4,
        scratch_shapes=[
            pltpu.VMEM((2, 512, 1024), BF),
            pltpu.VMEM((2, 512, 3072), BF),
            pltpu.VMEM((2, 512, 1024), BF),
            pltpu.VMEM((2, 512, 1024), BF),
            pltpu.VMEM((3, 512, 512), BF),
            pltpu.VMEM((512, 512), BF),
        ]
        + scatter_bufs()
        + scatter_bufs()
        + [
            pltpu.SemaphoreType.DMA((2, 4)),
            pltpu.SemaphoreType.DMA((2, 4)),
            pltpu.SemaphoreType.DMA((2, 3, 3, 3)),
            pltpu.SemaphoreType.DMA((2, 3, 3, 3)),
        ],
        compiler_params=pltpu.CompilerParams(
            collective_id=0, has_side_effects=True, vmem_limit_bytes=56 * 1024 * 1024
        ),
    )(t_unit, t_gm, t_mixed, t_g, a_unit, a_gm, a_mixed, a_g)


D = 1024
H = 16
HD = 64


epsilon = 1e-06
masked_score = -1e30


def normalize(flat_rows):
    widened = flat_rows.astype(jnp.float32)
    inverse = lax.rsqrt(jnp.mean(widened * widened, axis=-1, keepdims=True) + epsilon)
    return (widened * inverse, inverse)


def head_split(merged_qkv, which_part):
    batch_size, length, across = merged_qkv.shape[:3]
    member = merged_qkv[..., which_part * D : (which_part + 1) * D]
    return member.reshape(batch_size, length, across, H, HD)


def allowed_pairs(observed):
    key_seen = jnp.transpose(observed, (0, 2, 1))[:, :, None, :] > 0
    length = observed.shape[1]
    same_slot = jnp.arange(length)[:, None] == jnp.arange(length)[None, :]
    return key_seen | same_slot


def attention_forward(merged_qkv, allowed):
    queries = head_split(merged_qkv, 0)
    keys_part = head_split(merged_qkv, 1)
    values_part = head_split(merged_qkv, 2)
    scores = jnp.einsum(
        "bqche,bkche->bchqk", queries, keys_part, preferred_element_type=jnp.float32
    ) * HD ** (-0.5)
    scores = jnp.where(allowed[:, :, None], scores, masked_score)
    shifted = jnp.exp(scores - jnp.max(scores, axis=-1, keepdims=True))
    probability = shifted / jnp.sum(shifted, axis=-1, keepdims=True)
    rounded = probability.astype(jnp.bfloat16)
    mixed_heads = jnp.einsum(
        "bchqk,bkche->bqche", rounded, values_part, preferred_element_type=jnp.float32
    )
    batch_size, length, across = merged_qkv.shape[:3]
    return (
        probability,
        rounded,
        mixed_heads.reshape(batch_size, length, across, D).astype(jnp.bfloat16),
    )


def attention_backward(merged_qkv, probability, rounded, grad_mixed):
    queries = head_split(merged_qkv, 0)
    keys_part = head_split(merged_qkv, 1)
    values_part = head_split(merged_qkv, 2)
    batch_size, length, across = merged_qkv.shape[:3]
    grad_heads = grad_mixed.reshape(batch_size, length, across, H, HD)
    grad_probs = jnp.einsum(
        "bqche,bkche->bchqk", grad_heads, values_part, preferred_element_type=jnp.float32
    )
    grad_values = jnp.einsum(
        "bchqk,bqche->bkche", rounded, grad_heads, preferred_element_type=jnp.float32
    )
    grad_scores = (
        probability
        * (grad_probs - jnp.sum(grad_probs * probability, axis=-1, keepdims=True))
        * HD ** (-0.5)
    )
    grad_scores = grad_scores.astype(jnp.bfloat16)
    grad_queries = jnp.einsum(
        "bchqk,bkche->bqche", grad_scores, keys_part, preferred_element_type=jnp.float32
    )
    grad_keys = jnp.einsum(
        "bchqk,bqche->bkche", grad_scores, queries, preferred_element_type=jnp.float32
    )
    joined = jnp.concatenate(
        [
            member.reshape(batch_size, length, across, D)
            for member in (grad_queries, grad_keys, grad_values)
        ],
        axis=-1,
    )
    return joined.astype(jnp.bfloat16)


def forward_parts(tokens_view, weight_qkv, allowed):
    normed, inverse = normalize(tokens_view.reshape(-1, D))
    unit_rows = normed.astype(jnp.bfloat16)
    merged_qkv = jnp.dot(unit_rows, weight_qkv, preferred_element_type=jnp.float32).astype(
        jnp.bfloat16
    )
    merged_qkv = merged_qkv.reshape(tokens_view.shape[:3] + (3 * D,))
    probability, rounded, mixed_heads = attention_forward(merged_qkv, allowed)
    return (
        normed,
        inverse,
        unit_rows,
        merged_qkv,
        probability,
        rounded,
        mixed_heads.reshape(-1, D),
    )


def residual_output(tokens_view, mixed_rows, weight_out):
    update = jnp.dot(mixed_rows, weight_out, preferred_element_type=jnp.float32)
    return (
        (tokens_view.reshape(-1, D).astype(jnp.float32) + update)
        .astype(jnp.bfloat16)
        .reshape(tokens_view.shape)
    )


def backward_parts(tokens_view, upstream, weight_qkv, weight_out, saved_parts):
    normed, inverse, unit_rows, merged_qkv, probability, rounded, mixed_rows = saved_parts
    flat_up = upstream.reshape(-1, D)
    grad_mixed = jnp.dot(flat_up, weight_out.T, preferred_element_type=jnp.float32).astype(
        jnp.bfloat16
    )
    grad_merged = attention_backward(
        merged_qkv, probability, rounded, grad_mixed.reshape(tokens_view.shape)
    ).reshape(-1, 3 * D)
    grad_unit = jnp.dot(grad_merged, weight_qkv.T, preferred_element_type=jnp.float32)
    grad_rows = inverse * (
        grad_unit - normed * jnp.mean(grad_unit * normed, axis=-1, keepdims=True)
    )
    grad_input = (
        (flat_up.astype(jnp.float32) + grad_rows).astype(jnp.bfloat16).reshape(tokens_view.shape)
    )
    return (grad_input, ((unit_rows, grad_merged), (mixed_rows, flat_up)))


def local(tokens, cotangent, observed, time_qkv, time_out, agent_qkv, agent_out):
    agent_devices = lax.axis_size("ag")
    time_devices = lax.axis_size("tm")
    agent_index = lax.axis_index("ag")
    time_index = lax.axis_index("tm")
    scenes, agent_rows, step_rows = tokens.shape[:3]
    time_agents = agent_rows // time_devices
    agent_steps = step_rows // agent_devices
    whole_steps = step_rows * time_devices
    upstream_agent = lax.all_to_all(cotangent, "ag", split_axis=2, concat_axis=1, tiled=True)
    time_tokens = lax.all_to_all(tokens, "tm", split_axis=1, concat_axis=2, tiled=True)
    agent_start = agent_index * agent_rows + time_index * time_agents
    time_seen = lax.dynamic_slice_in_dim(observed, agent_start, time_agents, 1)
    time_allowed = allowed_pairs(time_seen.reshape(scenes * time_agents, whole_steps, 1))
    time_view = time_tokens.reshape(scenes * time_agents, whole_steps, 1, D)
    time_saved = forward_parts(time_view, time_qkv, time_allowed)
    first_time = residual_output(time_view, time_saved[6], time_out).reshape(
        scenes, time_agents, whole_steps, D
    )
    first_home = lax.all_to_all(first_time, "tm", split_axis=2, concat_axis=1, tiled=True)
    first_agent = lax.all_to_all(first_home, "ag", split_axis=2, concat_axis=1, tiled=True)
    step_start = time_index * step_rows + agent_index * agent_steps
    agent_seen = lax.dynamic_slice_in_dim(observed, step_start, agent_steps, 2)
    agent_saved = forward_parts(first_agent, agent_qkv, allowed_pairs(agent_seen))
    grad_first_agent, agent_terms = backward_parts(
        first_agent, upstream_agent, agent_qkv, agent_out, agent_saved
    )
    back_home = lax.all_to_all(grad_first_agent, "ag", split_axis=1, concat_axis=2, tiled=True)
    back_time = lax.all_to_all(back_home, "tm", split_axis=1, concat_axis=2, tiled=True)
    grad_view = back_time.reshape(time_view.shape)
    grad_time_view, time_terms = backward_parts(
        time_view, grad_view, time_qkv, time_out, time_saved
    )
    grad_tokens = lax.all_to_all(
        grad_time_view.reshape(scenes, time_agents, whole_steps, D),
        "tm",
        split_axis=2,
        concat_axis=1,
        tiled=True,
    )
    return (grad_tokens, *scatter_grads(time_terms, agent_terms))


def solution(mesh):
    in_specs = (P(None, "ag", "tm", None), P(None, "ag", "tm", None), P(), P(), P(), P(), P())
    out_specs = (
        P(None, "ag", "tm", None),
        P(("ag", "tm"), None),
        P(("ag", "tm"), None),
        P(("ag", "tm"), None),
        P(("ag", "tm"), None),
    )
    return jax.shard_map(local, mesh=mesh, in_specs=in_specs, out_specs=out_specs, check_vma=False)
```

```python
import functools

import jax
import jax.numpy as jnp
from jax import lax
from jax.experimental import pallas as pl
from jax.experimental.pallas import tpu as pltpu
from jax.sharding import PartitionSpec as P

D = 1024
H = 16
HD = 64
STEPS = 128
epsilon = 1e-06
masked_score = -1e30

MESH = pl.DeviceIdType.MESH
BF = jnp.bfloat16
F32 = jnp.float32
NT = (((1,), (1,)), ((), ()))
TN = (((0,), (0,)), ((), ()))

STREAMS = ((0, 1408, "xyz"), (1408, 2816, "yzx"), (2816, 4096, "zyx"))


def matmul(left, right, dims=(((1,), (0,)), ((), ()))):
    return lax.dot_general(left, right, dims, preferred_element_type=F32)


class Place:
    def __init__(self):
        self.ag = lax.axis_index("ag")
        self.tm = lax.axis_index("tm")
        self.y = self.ag // 4
        self.zlo = (self.ag // 2) % 2
        self.core = self.ag % 2
        self.zhi = self.tm // 4
        self.x = self.tm % 4
        self.z = self.zhi * 2 + self.zlo

    def at(self, axis):
        return {"x": self.x, "y": self.y, "z": self.z}[axis]

    def ring(self, axis, step):
        if axis == "x":
            return (self.ag, self.zhi * 4 + (self.x + step) % 4)
        if axis == "y":
            return (((self.y + step) % 4) * 4 + self.ag % 4, self.tm)
        z = (self.z + step) % 4
        return (self.y * 4 + (z % 2) * 2 + self.core, (z // 2) * 4 + self.x)

    def twin(self):
        return (self.ag + 1 - 2 * self.core, self.tm)


def remote(src, dst, send, recv, device):
    return pltpu.make_async_remote_copy(
        src_ref=src, dst_ref=dst, send_sem=send, recv_sem=recv, device_id=device, device_id_type=MESH
    )


def greet(devices):
    barrier = pltpu.get_barrier_semaphore()
    for device in devices:
        pl.semaphore_signal(barrier, inc=1, device_id=device, device_id_type=MESH)
    pl.semaphore_wait(barrier, len(devices))


def selector(core, x_first):
    at = lax.broadcasted_iota(jnp.int32, (128, 256), 0)
    row = lax.broadcasted_iota(jnp.int32, (128, 256), 1)
    high, low = at // 32, (at // 8) % 4
    x, z = (high, low) if x_first else (low, high)
    wanted = (z % 2) * 128 + core * 64 + (z // 2) * 32 + x * 8 + at % 8
    return jnp.where(row == wanted, 1.0, 0.0).astype(BF)


class Twin:
    def __init__(self, place, send, recv):
        self.place, self.send, self.recv = place, send, recv

    def copy(self, slot, ref, cols=None):
        cols = slice(None) if cols is None else cols
        return remote(
            ref.at[0:256, cols], ref.at[256:512, cols], self.send.at[slot], self.recv.at[slot], self.place.twin()
        )

    def copy_rows(self, slot, ref):
        return remote(ref.at[0:2], ref.at[2:4], self.send.at[slot], self.recv.at[slot], self.place.twin())


class Scatter:
    def __init__(self, place, block, bufs, send, recv):
        self.place = place
        self.block, (self.own, self.r1, self.s2, self.r2, self.s3, self.r3) = block, bufs
        self.send, self.recv = send, recv

    def copy(self, stream, phase, step):
        lo, hi, axes = STREAMS[stream]
        cols = slice(lo, hi)
        axis = axes[phase]
        to = (self.place.at(axis) + step) % 4
        slot = step - 1
        if phase == 0:
            src, dst = self.block(stream, slot), self.r1.at[slot, :, cols]
        elif phase == 1:
            src = self.s2.at[pl.ds(pl.multiple_of(to * 32, 32), 32), cols]
            dst = self.r2.at[slot, :, cols]
        else:
            src = self.s3.at[pl.ds(pl.multiple_of(to * 8, 8), 8), cols]
            dst = self.r3.at[slot, :, cols]
        return remote(
            src,
            dst,
            self.send.at[stream, phase, slot],
            self.recv.at[stream, phase, slot],
            self.place.ring(axis, step),
        )

    def product(self, stream, ut, ut_mixed, gm, g, block):
        lo, hi, _ = STREAMS[stream]
        rows = pl.ds(pl.multiple_of(block * 128, 128), 128)
        if stream < 2:
            return [(lo, hi, matmul(ut[stream, rows, :], gm[:, lo:hi]))]
        return [
            (lo, 3072, matmul(ut[2, rows, :], gm[:, lo:3072])),
            (3072, 4096, matmul(ut_mixed[rows, :], g[...].reshape(512, D))),
        ]

    def start(self, stream, ut, ut_mixed, gm, g):
        first, _, axes = STREAMS[stream]
        at = self.place.at(axes[0])

        def one(step, carry):
            for lo, hi, part in self.product(stream, ut, ut_mixed, gm, g, (at + step) % 4):
                self.block(stream, step - 1)[:, lo - first : hi - first] = part.astype(BF)
            self.copy(stream, 0, step).start()
            return carry

        lax.fori_loop(1, 4, one, 0)
        for lo, hi, part in self.product(stream, ut, ut_mixed, gm, g, at):
            self.own[:, lo:hi] = part

    def second(self, stream):
        lo, hi, _ = STREAMS[stream]
        for step in (1, 2, 3):
            self.copy(stream, 0, step).wait_recv()

        def one(q, carry):
            rows = pl.ds(pl.multiple_of(q * 32, 32), 32)
            total = self.own[rows, lo:hi]
            for slot in range(3):
                total = total + self.r1[slot, rows, lo:hi].astype(F32)
            self.own[rows, lo:hi] = total
            self.s2[rows, lo:hi] = total.astype(BF)
            return carry

        lax.fori_loop(0, 4, one, 0)
        for step in (1, 2, 3):
            self.copy(stream, 1, step).start()

    def third(self, stream):
        lo, hi, axes = STREAMS[stream]
        for step in (1, 2, 3):
            self.copy(stream, 1, step).wait_recv()
        total = self.own[pl.ds(pl.multiple_of(self.place.at(axes[1]) * 32, 32), 32), lo:hi]
        for slot in range(3):
            total = total + self.r2[slot, :, lo:hi].astype(F32)
        self.s3[:, lo:hi] = total
        for step in (1, 2, 3):
            self.copy(stream, 2, step).start()

    def last(self, stream, qkv_ref, out_ref):
        lo, hi, axes = STREAMS[stream]
        for step in (1, 2, 3):
            self.copy(stream, 2, step).wait_recv()
        total = self.s3[pl.ds(pl.multiple_of(self.place.at(axes[2]) * 8, 8), 8), lo:hi]
        for slot in range(3):
            total = total + self.r3[slot, :, lo:hi]
        top = min(hi, 3072)
        qkv_ref[:, lo:top] = total[:, : top - lo]
        if hi > 3072:
            out_ref[...] = total[:, 3072 - lo :]

    def drain(self):
        for stream in range(3):
            for phase in range(3):
                for step in (1, 2, 3):
                    self.copy(stream, phase, step).wait_send()


def scatter_bufs():
    return [
        pltpu.VMEM((128, 4096), F32),
        pltpu.VMEM((3, 128, 4096), BF),
        pltpu.VMEM((128, 4096), BF),
        pltpu.VMEM((3, 32, 4096), BF),
        pltpu.VMEM((32, 4096), F32),
        pltpu.VMEM((3, 8, 4096), F32),
    ]


def transposed(place, unit, mixed, ut, ut_mixed):
    sel_x = selector(place.core, True)
    sel_z = selector(place.core, False)
    for y in range(4):
        cols = slice(y * 256, y * 256 + 256)
        part = matmul(sel_x, unit[:, cols], NT).astype(BF)
        for x in range(4):
            ut[0, x * 128 + y * 32 : x * 128 + y * 32 + 32, :] = part[x * 32 : x * 32 + 32]
        part = matmul(sel_z, unit[:, cols], NT).astype(BF)
        ut[1, y * 128 : y * 128 + 128, :] = part
        for z in range(4):
            ut[2, z * 128 + y * 32 : z * 128 + y * 32 + 32, :] = part[z * 32 : z * 32 + 32]
        part = matmul(sel_z, mixed[:, cols], NT).astype(BF)
        for z in range(4):
            ut_mixed[z * 128 + y * 32 : z * 128 + y * 32 + 32, :] = part[z * 32 : z * 32 + 32]


def normal(x_ref):
    x = x_ref[...].reshape(256, D).astype(F32)
    inverse = lax.rsqrt(jnp.mean(x * x, axis=-1, keepdims=True) + epsilon)
    return x * inverse, inverse


def span(start, size):
    return pl.ds(pl.multiple_of(start * size, size), size)


def project(x_ref, unit, w, merged):
    unit[0:256, :] = normal(x_ref)[0].astype(BF)

    def one(n, carry):
        cols = span(n, 512)
        merged[:, cols] = matmul(unit[0:256, :], w[:, cols]).astype(BF)
        return carry

    lax.fori_loop(0, 6, one, 0)


def halves():
    lane = lax.broadcasted_iota(jnp.int32, (1, 128), 1)
    low = jnp.where(lane < HD, 1.0, 0.0)
    return low.astype(BF), (1.0 - low).astype(BF)


def pair_parts(merged, rows, pair):
    q = merged[rows, span(pair, 128)] * BF(HD**-0.5)
    k = merged[rows, pl.ds(pl.multiple_of(D + pair * 128, 128), 128)]
    v = merged[rows, pl.ds(pl.multiple_of(2 * D + pair * 128, 128), 128)]
    return q, k, v


def prob_of(q, k, bias):
    scores = matmul(q, k, NT) + bias
    shifted = jnp.exp(scores - jnp.max(scores, axis=-1, keepdims=True))
    return shifted * (1.0 / jnp.sum(shifted, axis=-1, keepdims=True))


def attend(merged, mixed, rows, bias_ref):
    def one(pair, carry):
        q, k, v = pair_parts(merged, rows, pair)
        total = None
        for half in halves():
            part = matmul(prob_of(q * half, k, bias_ref[...]).astype(BF), v * half)
            total = part if total is None else total + part
        mixed[rows, span(pair, 128)] = total.astype(BF)
        return carry

    lax.fori_loop(0, H // 2, one, 0)


def attend_back(merged, gmix, mixed, gm, rows, bias_ref):
    def one(pair, carry):
        q, k, v = pair_parts(merged, rows, pair)
        go = gmix[rows, span(pair, 128)]
        sums = [None] * 4
        for half in halves():
            prob = prob_of(q * half, k, bias_ref[...])
            rounded = prob.astype(BF)
            go_half = go * half
            gp = matmul(go_half, v, NT)
            gs = (prob * (gp - jnp.sum(gp * prob, axis=-1, keepdims=True))).astype(BF)
            parts = [
                matmul(gs, k * half),
                matmul(gs, q * half, TN),
                matmul(rounded, go_half, TN),
                None if mixed is None else matmul(rounded, v * half),
            ]
            sums = [p if s is None else s + p for s, p in zip(sums, parts)]
        gm[rows, span(pair, 128)] = (sums[0] * HD**-0.5).astype(BF)
        gm[rows, pl.ds(pl.multiple_of(D + pair * 128, 128), 128)] = sums[1].astype(BF)
        gm[rows, pl.ds(pl.multiple_of(2 * D + pair * 128, 128), 128)] = sums[2].astype(BF)
        if mixed is not None:
            mixed[rows, span(pair, 128)] = sums[3].astype(BF)
        return carry

    lax.fori_loop(0, H // 2, one, 0)


def add_residual(x_ref, mixed, w, out_ref, shape):
    for n in range(2):
        cols = slice(n * 512, n * 512 + 512)
        x = x_ref[..., cols].reshape(256, 512).astype(F32)
        out = x + matmul(mixed[0:256, :], w[:, cols])
        out_ref[..., cols] = out.astype(BF).reshape(shape + (512,))


def grad_of_mixed(g, w, gmix):
    def one(n, carry):
        rows = span(n, 256)
        gmix[:, rows] = matmul(g[...].reshape(256, D), w[rows, :], NT).astype(BF)
        return carry

    lax.fori_loop(0, 4, one, 0)


def grad_of_input(x_ref, g, gm, w, gu, out_ref, shape):
    def one(n, carry):
        rows = span(n, 256)
        gu[:, rows] = matmul(gm[0:256, :], w[rows, :], NT)
        return carry

    lax.fori_loop(0, 4, one, 0)
    normed, inverse = normal(x_ref)
    grad_unit = gu[...]
    rows = inverse * (grad_unit - normed * jnp.mean(grad_unit * normed, axis=-1, keepdims=True))
    out_ref[...] = (g[...].reshape(256, D).astype(F32) + rows).astype(BF).reshape(shape + (D,))


def swap_rows(src, dst):
    at = lax.broadcasted_iota(jnp.int32, (256, 256), 0)
    row = lax.broadcasted_iota(jnp.int32, (256, 256), 1)
    swap = jnp.where(row == (at % 16) * 16 + at // 16, 1.0, 0.0).astype(BF)
    for n in range(2):
        cols = slice(n * 512, n * 512 + 512)
        out = matmul(swap, src[..., cols].reshape(256, 512)).astype(BF)
        dst[..., cols] = out.reshape(dst.shape[:-1] + (512,))


class Swap:
    def __init__(self, place, axis, send, recv, source, target):
        self.place, self.axis, self.send, self.recv = place, axis, send, recv
        self.source, self.target = source, target
        self.size = 8 if axis == "tm" else 16
        self.me = place.tm if axis == "tm" else place.ag

    def copy(self, step):
        to = (self.me + step) % self.size
        device = (self.place.ag, to) if self.axis == "tm" else (to, self.place.tm)
        return remote(self.source(to), self.target(self.me), self.send.at[step], self.recv.at[step], device)

    def local(self):
        return pltpu.make_async_copy(self.source(self.me), self.target(self.me), self.recv.at[0])

    def start(self):
        def one(step, carry):
            self.copy(step).start()
            return carry

        lax.fori_loop(1, self.size, one, 0)
        self.local().start()

    def wait(self):
        def one(step, carry):
            self.copy(step).wait_recv()
            return carry

        lax.fori_loop(1, self.size, one, 0)
        self.local().wait()

    def drain(self):
        def one(step, carry):
            self.copy(step).wait_send()
            return carry

        lax.fori_loop(1, self.size, one, 0)


def block_kernel(
    tokens, cotangent, observed, time_qkv, time_out, agent_qkv, agent_out,
    grad_tokens, tq_ref, to_ref, aq_ref, ao_ref,
    w_tq, w_to, w_aq, w_ao,
    x_time, made, home, turned, x_agent, cot, back,
    merged_t, merged_a, gmix, gu, bias_t, bias_a,
    units, gms, mixeds, g_time, g_agent, ut, ut_mixed,
    *rest,
):
    grad_a = rest[0]
    bufs = (rest[1:7], rest[7:13])
    load, swap_send, swap_recv, twin_send, twin_recv, sc_send, sc_recv = rest[13:]
    place = Place()
    loads = [
        pltpu.make_async_copy(src, dst, load.at[i])
        for i, (src, dst) in enumerate(
            (
                (cotangent, cot),
                (time_qkv, w_tq),
                (time_out, w_to),
                (agent_out, w_ao),
                (agent_qkv, w_aq),
            )
        )
    ]
    for copy in loads:
        copy.start()
    far = [
        (place.y * 4 + (1 - place.zlo) * 2 + place.core, (1 - place.zhi) * 4 + place.x),
    ]
    greet(
        [((place.ag + step) % 16, place.tm) for step in range(1, 16)]
        + [(place.ag, (place.tm + step) % 8) for step in range(1, 8)]
        + far
    )

    def swap(slot, axis, source, target):
        return Swap(place, axis, swap_send.at[slot], swap_recv.at[slot], source, target)

    def two(ref):
        return lambda i: ref.at[pl.ds(i * 2, 2)]

    def sixteen(ref):
        return lambda i: ref.at[0:2, span(i, 16), :]

    def rows16(ref):
        return lambda i: ref.at[span(i, 16), :]

    tokens_in = swap(0, "tm", two(tokens), sixteen(x_time))
    cot_in = swap(1, "ag", rows16(turned), rows16(g_agent))
    first_home = swap(2, "tm", sixteen(made), two(home))
    first_agent = swap(3, "ag", rows16(turned), rows16(x_agent))
    back_home = swap(4, "ag", rows16(cot), rows16(back))
    back_time = swap(5, "tm", two(home), sixteen(g_time))
    tokens_out = swap(6, "tm", sixteen(made), two(grad_tokens))
    twins = [Twin(place, twin_send.at[s], twin_recv.at[s]) for s in range(2)]

    def block_a(stream, slot):
        lo, hi, _ = STREAMS[stream]
        return grad_a.at[slot, :, lo:hi]

    def block_t(stream, slot):
        lo, hi, _ = STREAMS[stream]
        if stream < 2:
            return w_aq.at[span(slot, 128), lo:hi]
        return w_aq.at[span(slot + 4, 128), 0 : hi - lo]

    scatters = [Scatter(place, (block_a, block_t)[s], bufs[s], sc_send.at[s], sc_recv.at[s]) for s in range(2)]
    unit_a, unit_t = units.at[0], units.at[1]
    gm_a, gm_t = gms.at[0], gms.at[1]
    mixed_a, mixed_t = mixeds.at[0], mixeds.at[1]
    seqs = [slice(0, 128), slice(128, 256)]

    with jax.named_scope("tokens_to_agents"):
        tokens_in.start()
        loads[0].wait()
        swap_rows(cot, turned)
        cot_in.start()
        self_t = lax.broadcasted_iota(jnp.int32, (128, 128), 0) == lax.broadcasted_iota(jnp.int32, (128, 128), 1)
        for a in range(2):
            row = observed[pl.ds(place.ag * 16 + place.tm * 2 + a, 1), :]
            bias_t[a] = jnp.where((row > 0) | self_t, 0.0, masked_score)
        at_step = lax.broadcasted_iota(jnp.int32, (8, STEPS), 1) == place.tm * 16 + place.ag
        seen = matmul(jnp.where(at_step, 1.0, 0.0).astype(BF), observed[...].astype(F32).astype(BF), NT)
        self_a = lax.broadcasted_iota(jnp.int32, (256, 256), 0) == lax.broadcasted_iota(jnp.int32, (256, 256), 1)
        bias_a[...] = jnp.where((seen[0:1, :] > 0.5) | self_a, 0.0, masked_score)
        loads[1].wait()
        tokens_in.wait()
    with jax.named_scope("time_forward"):
        project(x_time, unit_t, w_tq, merged_t)
        twins[1].copy(0, unit_t).start()
        for a in range(2):
            attend(merged_t, mixed_t, seqs[a], bias_t.at[a])
        twins[1].copy(2, mixed_t).start()
        loads[2].wait()
        add_residual(x_time, mixed_t, w_to, made, (2, 128))
        first_home.start()
    with jax.named_scope("first_to_steps"):
        cot_in.wait()
        twins[0].copy(3, g_agent).start()
        loads[3].wait()
        grad_of_mixed(g_agent.at[0:256, :], w_ao, gmix)
        cot_in.drain()
        first_home.wait()
        swap_rows(home, turned)
        first_agent.start()
        loads[4].wait()
        first_agent.wait()
    with jax.named_scope("agent_backward"):
        project(x_agent, unit_a, w_aq, merged_a)
        twins[0].copy(0, unit_a).start()
        attend_back(merged_a, gmix, mixed_a, gm_a, slice(0, 256), bias_a)
        twins[0].copy(2, mixed_a).start()
        twins[0].copy(1, gm_a).start()
        grad_of_input(x_agent, g_agent.at[0:256, :], gm_a, w_aq, gu, cot, (256,))
        back_home.start()
    with jax.named_scope("agent_weights"):
        for slot, ref in enumerate((unit_a, gm_a, mixed_a, g_agent)):
            twins[0].copy(slot, ref).wait_recv()
        transposed(place, unit_a, mixed_a, ut, ut_mixed)
        for stream in range(3):
            scatters[0].start(stream, ut, ut_mixed, gm_a, g_agent)
    with jax.named_scope("grad_first_to_agents"):
        back_home.wait()
        swap_rows(back, home)
        back_time.start()
        back_time.wait()
        twins[1].copy_rows(3, g_time).start()
    with jax.named_scope("time_backward"):
        g_own = g_time.at[0:2]
        grad_of_mixed(g_own, w_to, gmix)
        for a in range(2):
            attend_back(merged_t, gmix, None, gm_t, seqs[a], bias_t.at[a])
        twins[1].copy(1, gm_t).start()
        first_home.drain()
        grad_of_input(x_time, g_own, gm_t, w_tq, gu, made, (2, 128))
        tokens_out.start()
    with jax.named_scope("time_weights"):
        for slot, ref in enumerate((unit_t, gm_t, mixed_t)):
            twins[1].copy(slot, ref).wait_recv()
        twins[1].copy_rows(3, g_time).wait_recv()
        transposed(place, unit_t, mixed_t, ut, ut_mixed)
        for stream in range(3):
            scatters[1].start(stream, ut, ut_mixed, gm_t, g_time)
    with jax.named_scope("rings"):
        outs = ((aq_ref, ao_ref), (tq_ref, to_ref))
        for stream in range(3):
            scatters[0].second(stream)
        for stream in range(3):
            scatters[0].third(stream)
        for stream in range(3):
            scatters[1].second(stream)
        for stream in range(3):
            scatters[0].last(stream, *outs[0])
        for stream in range(3):
            scatters[1].third(stream)
        for stream in range(3):
            scatters[1].last(stream, *outs[1])
        tokens_out.wait()
    with jax.named_scope("drain"):
        for s in range(2):
            scatters[s].drain()
        for slot, ref in enumerate((unit_a, gm_a, mixed_a, g_agent)):
            twins[0].copy(slot, ref).wait_send()
        for slot, ref in enumerate((unit_t, gm_t, mixed_t)):
            twins[1].copy(slot, ref).wait_send()
        twins[1].copy_rows(3, g_time).wait_send()
        for moved in (tokens_in, first_agent, back_home, back_time, tokens_out):
            moved.drain()


def local(tokens, cotangent, observed, time_qkv, time_out, agent_qkv, agent_out):
    shape = jax.ShapeDtypeStruct
    grad_tokens, *grads = pl.pallas_call(
        block_kernel,
        out_shape=[
            shape((16, 16, D), BF),
            shape((8, 3 * D), F32),
            shape((8, D), F32),
            shape((8, 3 * D), F32),
            shape((8, D), F32),
        ],
        in_specs=[
            pl.BlockSpec(memory_space=pl.ANY),
            pl.BlockSpec(memory_space=pl.ANY),
            pl.BlockSpec(memory_space=pltpu.VMEM),
        ]
        + [pl.BlockSpec(memory_space=pl.ANY)] * 4,
        out_specs=[pl.BlockSpec(memory_space=pl.ANY)] + [pl.BlockSpec(memory_space=pltpu.VMEM)] * 4,
        scratch_shapes=[
            pltpu.VMEM((D, 3 * D), BF),
            pltpu.VMEM((D, D), BF),
            pltpu.VMEM((D, 3 * D), BF),
            pltpu.VMEM((D, D), BF),
            pltpu.VMEM((2, 128, D), BF),
            pltpu.VMEM((2, 128, D), BF),
            pltpu.VMEM((16, 16, D), BF),
            pltpu.VMEM((256, D), BF),
            pltpu.VMEM((256, D), BF),
            pltpu.VMEM((256, D), BF),
            pltpu.VMEM((256, D), BF),
            pltpu.VMEM((256, 3 * D), BF),
            pltpu.VMEM((256, 3 * D), BF),
            pltpu.VMEM((256, D), BF),
            pltpu.VMEM((256, D), F32),
            pltpu.VMEM((2, 128, 128), F32),
            pltpu.VMEM((256, 256), F32),
            pltpu.VMEM((2, 512, D), BF),
            pltpu.VMEM((2, 512, 3 * D), BF),
            pltpu.VMEM((2, 512, D), BF),
            pltpu.VMEM((4, 128, D), BF),
            pltpu.VMEM((512, D), BF),
            pltpu.VMEM((3, 512, 512), BF),
            pltpu.VMEM((512, 512), BF),
        ]
        + [pltpu.VMEM((3, 128, 4096), BF)]
        + scatter_bufs()
        + scatter_bufs()
        + [
            pltpu.SemaphoreType.DMA((5,)),
            pltpu.SemaphoreType.DMA((7, 16)),
            pltpu.SemaphoreType.DMA((7, 16)),
            pltpu.SemaphoreType.DMA((2, 4)),
            pltpu.SemaphoreType.DMA((2, 4)),
            pltpu.SemaphoreType.DMA((2, 3, 3, 3)),
            pltpu.SemaphoreType.DMA((2, 3, 3, 3)),
        ],
        compiler_params=pltpu.CompilerParams(
            collective_id=0, has_side_effects=True, vmem_limit_bytes=61 * 1024 * 1024
        ),
    )(
        tokens.reshape(16, 16, D),
        cotangent.reshape(256, D),
        observed.reshape(256, STEPS),
        time_qkv,
        time_out,
        agent_qkv,
        agent_out,
    )
    return (grad_tokens.reshape(1, 16, 16, D), *grads)


def solution(mesh):
    in_specs = (P(None, "ag", "tm", None), P(None, "ag", "tm", None), P(), P(), P(), P(), P())
    out_specs = (
        P(None, "ag", "tm", None),
        P(("ag", "tm"), None),
        P(("ag", "tm"), None),
        P(("ag", "tm"), None),
        P(("ag", "tm"), None),
    )
    return jax.shard_map(local, mesh=mesh, in_specs=in_specs, out_specs=out_specs, check_vma=False)
```

```python
import functools

import jax
import jax.numpy as jnp
from jax import lax
from jax.experimental import pallas as pl
from jax.experimental.pallas import tpu as pltpu
from jax.sharding import PartitionSpec as P

D = 1024
H = 16
HD = 64
STEPS = 128
epsilon = 1e-06
masked_score = -1e30

MESH = pl.DeviceIdType.MESH
BF = jnp.bfloat16
F32 = jnp.float32
NT = (((1,), (1,)), ((), ()))
TN = (((0,), (0,)), ((), ()))

STREAMS = ((0, 1408, "xyz"), (1408, 2816, "yzx"), (2816, 4096, "zxy"))


def matmul(left, right, dims=(((1,), (0,)), ((), ()))):
    return lax.dot_general(left, right, dims, preferred_element_type=F32)


class Place:
    def __init__(self):
        self.ag = lax.axis_index("ag")
        self.tm = lax.axis_index("tm")
        self.y = self.ag // 4
        self.zlo = (self.ag // 2) % 2
        self.core = self.ag % 2
        self.zhi = self.tm // 4
        self.x = self.tm % 4
        self.z = self.zhi * 2 + self.zlo

    def at(self, axis):
        return {"x": self.x, "y": self.y, "z": self.z}[axis]

    def ring(self, axis, step):
        if axis == "x":
            return (self.ag, self.zhi * 4 + (self.x + step) % 4)
        if axis == "y":
            return (((self.y + step) % 4) * 4 + self.ag % 4, self.tm)
        z = (self.z + step) % 4
        return (self.y * 4 + (z % 2) * 2 + self.core, (z // 2) * 4 + self.x)

    def twin(self):
        return (self.ag + 1 - 2 * self.core, self.tm)


def remote(src, dst, send, recv, device):
    return pltpu.make_async_remote_copy(
        src_ref=src, dst_ref=dst, send_sem=send, recv_sem=recv, device_id=device, device_id_type=MESH
    )


def greet(devices):
    barrier = pltpu.get_barrier_semaphore()
    for device in devices:
        pl.semaphore_signal(barrier, inc=1, device_id=device, device_id_type=MESH)
    pl.semaphore_wait(barrier, len(devices))


def selector(core, x_first):
    at = lax.broadcasted_iota(jnp.int32, (128, 256), 0)
    row = lax.broadcasted_iota(jnp.int32, (128, 256), 1)
    high, low = at // 32, (at // 8) % 4
    x, z = (high, low) if x_first else (low, high)
    wanted = (z % 2) * 128 + core * 64 + (z // 2) * 32 + x * 8 + at % 8
    return jnp.where(row == wanted, 1.0, 0.0).astype(BF)


class Twin:
    def __init__(self, place, send, recv):
        self.place, self.send, self.recv = place, send, recv

    def copy(self, slot, ref, cols=None):
        cols = slice(None) if cols is None else cols
        return remote(
            ref.at[0:256, cols], ref.at[256:512, cols], self.send.at[slot], self.recv.at[slot], self.place.twin()
        )

    def copy_rows(self, slot, ref):
        return remote(ref.at[0:2], ref.at[2:4], self.send.at[slot], self.recv.at[slot], self.place.twin())


class Scatter:
    def __init__(self, place, block, second_block, bufs, send, recv):
        self.place, self.second_block = place, second_block
        self.block, (self.own, self.r1, self.r2, self.s3, self.r3) = block, bufs
        self.send, self.recv = send, recv

    def copy(self, stream, phase, step):
        lo, hi, axes = STREAMS[stream]
        cols = slice(lo, hi)
        axis = axes[phase]
        to = (self.place.at(axis) + step) % 4
        slot = step - 1
        if phase == 0:
            src, dst = self.block(stream, slot), self.r1.at[slot, :, cols]
        elif phase == 1:
            src = self.second_block(stream).at[pl.ds(pl.multiple_of(to * 32, 32), 32), :]
            dst = self.r2.at[slot, :, cols]
        else:
            src = self.s3.at[to, :, cols]
            dst = self.r3.at[slot, :, cols]
        return remote(
            src,
            dst,
            self.send.at[stream, phase, slot],
            self.recv.at[stream, phase, slot],
            self.place.ring(axis, step),
        )

    def product(self, stream, ut, ut_mixed, gm, g, block):
        lo, hi, _ = STREAMS[stream]
        rows = pl.ds(pl.multiple_of(block * 128, 128), 128)
        if stream < 2:
            return [(lo, hi, matmul(ut[stream][rows, :], gm[:, lo:hi]))]
        return [
            (lo, 3072, matmul(ut[2][rows, :], gm[:, lo:3072])),
            (3072, 4096, matmul(ut_mixed[rows, :], g[...].reshape(512, D))),
        ]

    def start(self, stream, ut, ut_mixed, gm, g):
        first, _, axes = STREAMS[stream]
        at = self.place.at(axes[0])

        def one(step, carry):
            for lo, hi, part in self.product(stream, ut, ut_mixed, gm, g, (at + step) % 4):
                self.block(stream, step - 1)[:, lo - first : hi - first] = part.astype(BF)
            self.copy(stream, 0, step).start()
            return carry

        lax.fori_loop(1, 4, one, 0)
        for lo, hi, part in self.product(stream, ut, ut_mixed, gm, g, at):
            self.own[:, lo:hi] = part

    def second(self, stream):
        lo, hi, _ = STREAMS[stream]
        for step in (1, 2, 3):
            self.copy(stream, 0, step).wait_recv()

        def one(q, carry):
            rows = pl.ds(pl.multiple_of(q * 32, 32), 32)
            total = self.own[rows, lo:hi]
            for slot in range(3):
                total = total + self.r1[slot, rows, lo:hi].astype(F32)
            self.own[rows, lo:hi] = total
            self.second_block(stream)[rows, :] = total.astype(BF)
            return carry

        lax.fori_loop(0, 4, one, 0)
        for step in (1, 2, 3):
            self.copy(stream, 1, step).start()

    def third(self, stream):
        lo, hi, axes = STREAMS[stream]
        for step in (1, 2, 3):
            self.copy(stream, 1, step).wait_recv()
        total = self.own[pl.ds(pl.multiple_of(self.place.at(axes[1]) * 32, 32), 32), lo:hi]
        for slot in range(3):
            total = total + self.r2[slot, :, lo:hi].astype(F32)
        self.own[0:32, lo:hi] = total
        for q in range(4):
            self.s3[q, :, lo:hi] = total[q * 8 : q * 8 + 8].astype(BF)
        for step in (1, 2, 3):
            self.copy(stream, 2, step).start()

    def last(self, stream, qkv_ref, out_ref):
        lo, hi, axes = STREAMS[stream]
        for step in (1, 2, 3):
            self.copy(stream, 2, step).wait_recv()
        total = self.own[pl.ds(pl.multiple_of(self.place.at(axes[2]) * 8, 8), 8), lo:hi]
        for slot in range(3):
            total = total + self.r3[slot, :, lo:hi].astype(F32)
        top = min(hi, 3072)
        qkv_ref[:, lo:top] = total[:, : top - lo]
        if hi > 3072:
            out_ref[...] = total[:, 3072 - lo :]

    def drain(self):
        for stream in range(3):
            for phase in range(3):
                for step in (1, 2, 3):
                    self.copy(stream, phase, step).wait_send()


def scatter_bufs():
    return [
        pltpu.VMEM((128, 4096), F32),
        pltpu.VMEM((3, 128, 4096), BF),
        pltpu.VMEM((3, 32, 4096), BF),
        pltpu.VMEM((4, 8, 4096), BF),
        pltpu.VMEM((3, 8, 4096), BF),
    ]


def transposed(place, unit, mixed, ut, ut_mixed, spare):
    sel_x = selector(place.core, True)
    sel_z = selector(place.core, False)

    def last_order(part, y):
        for z in range(4):
            for x in range(4):
                at = (z % 2) * 128 + x * 32 + y * 8
                spare[at : at + 8, (z // 2) * 512 : (z // 2) * 512 + 512] = part[z * 32 + x * 8 : z * 32 + x * 8 + 8]

    for y in range(4):
        cols = slice(y * 256, y * 256 + 256)
        part = matmul(sel_x, unit[:, cols], NT).astype(BF)
        for x in range(4):
            ut[0][x * 128 + y * 32 : x * 128 + y * 32 + 32, :] = part[x * 32 : x * 32 + 32]
        part = matmul(sel_z, unit[:, cols], NT)
        ut[1][y * 128 : y * 128 + 128, :] = part.astype(BF)
        last_order(part, y)
    ut[2][0:256, :] = spare[:, 0:512].astype(BF)
    ut[2][256:512, :] = spare[:, 512:1024].astype(BF)
    for y in range(4):
        last_order(matmul(sel_z, mixed[:, y * 256 : y * 256 + 256], NT), y)
    ut_mixed[0:256, :] = spare[:, 0:512].astype(BF)
    ut_mixed[256:512, :] = spare[:, 512:1024].astype(BF)


def normal(x_ref):
    x = x_ref[...].reshape(256, D).astype(F32)
    inverse = lax.rsqrt(jnp.mean(x * x, axis=-1, keepdims=True) + epsilon)
    return x * inverse, inverse


def span(start, size):
    return pl.ds(pl.multiple_of(start * size, size), size)


def project(x_ref, unit, w, merged):
    unit[0:256, :] = normal(x_ref)[0].astype(BF)

    def one(n, carry):
        cols = span(n, 512)
        merged[:, cols] = matmul(unit[0:256, :], w[:, cols]).astype(BF)
        return carry

    lax.fori_loop(0, 6, one, 0)


def halves():
    lane = lax.broadcasted_iota(jnp.int32, (1, 128), 1)
    low = jnp.where(lane < HD, 1.0, 0.0)
    return low.astype(BF), (1.0 - low).astype(BF)


def pair_parts(merged, rows, pair):
    q = merged[rows, span(pair, 128)] * BF(HD**-0.5)
    k = merged[rows, pl.ds(pl.multiple_of(D + pair * 128, 128), 128)]
    v = merged[rows, pl.ds(pl.multiple_of(2 * D + pair * 128, 128), 128)]
    return q, k, v


def attend(merged, mixed, seqs, biases, group):
    def one(turn, carry):
        low_high = halves()
        jobs = []
        for rows, bias in zip(seqs, biases):
            for i in range(group):
                pair = turn * group + i
                q, k, v = pair_parts(merged, rows, pair)
                for half in low_high:
                    jobs.append((rows, pair, bias, q * half, k, v * half))
        scores = [matmul(q, k, NT) + bias[...] for _, _, bias, q, k, _ in jobs]
        probs = probs_of(scores)
        parts = [matmul(p.astype(BF), job[5]) for p, job in zip(probs, jobs)]
        for i in range(0, len(jobs), 2):
            rows, pair = jobs[i][:2]
            mixed[rows, span(pair, 128)] = (parts[i] + parts[i + 1]).astype(BF)
        return carry

    lax.fori_loop(0, H // 2 // group, one, 0)


def probs_of(scores):
    tops = [jnp.max(s, axis=-1, keepdims=True) for s in scores]
    shifted = [jnp.exp(s - t) for s, t in zip(scores, tops)]
    sums = [jnp.sum(s, axis=-1, keepdims=True) for s in shifted]
    return [s * (1.0 / t) for s, t in zip(shifted, sums)]


def attend_back(merged, gmix, mixed, gm, seqs, biases, group):
    def one(turn, carry):
        low_high = halves()
        jobs = []
        for rows, bias in zip(seqs, biases):
            for i in range(group):
                pair = turn * group + i
                q, k, v = pair_parts(merged, rows, pair)
                go = gmix[rows, span(pair, 128)]
                for half in low_high:
                    jobs.append((rows, pair, bias, q * half, k, v, go * half, half))
        scores = [matmul(job[3], job[4], NT) + job[2][...] for job in jobs]
        gps = [matmul(job[6], job[5], NT) for job in jobs]
        probs = probs_of(scores)
        means = [jnp.sum(gp * p, axis=-1, keepdims=True) for gp, p in zip(gps, probs)]
        gss = [(p * (gp - m)).astype(BF) for p, gp, m in zip(probs, gps, means)]
        rounded = [p.astype(BF) for p in probs]
        gq = [matmul(gs, job[4] * job[7]) for gs, job in zip(gss, jobs)]
        gk = [matmul(gs, job[3], TN) for gs, job in zip(gss, jobs)]
        gv = [matmul(p, job[6], TN) for p, job in zip(rounded, jobs)]
        if mixed is not None:
            mx = [matmul(p, job[5] * job[7]) for p, job in zip(rounded, jobs)]
        for i in range(0, len(jobs), 2):
            rows, pair = jobs[i][:2]
            gm[rows, span(pair, 128)] = ((gq[i] + gq[i + 1]) * HD**-0.5).astype(BF)
            gm[rows, pl.ds(pl.multiple_of(D + pair * 128, 128), 128)] = (gk[i] + gk[i + 1]).astype(BF)
            gm[rows, pl.ds(pl.multiple_of(2 * D + pair * 128, 128), 128)] = (gv[i] + gv[i + 1]).astype(BF)
            if mixed is not None:
                mixed[rows, span(pair, 128)] = (mx[i] + mx[i + 1]).astype(BF)
        return carry

    lax.fori_loop(0, H // 2 // group, one, 0)


def add_residual(x_ref, mixed, w, out_ref, shape):
    for n in range(2):
        cols = slice(n * 512, n * 512 + 512)
        x = x_ref[..., cols].reshape(256, 512).astype(F32)
        out = x + matmul(mixed[0:256, :], w[:, cols])
        out_ref[..., cols] = out.astype(BF).reshape(shape + (512,))


def grad_of_mixed(g, w, gmix):
    def one(n, carry):
        rows = span(n, 256)
        gmix[:, rows] = matmul(g[...].reshape(256, D), w[rows, :], NT).astype(BF)
        return carry

    lax.fori_loop(0, 4, one, 0)


def grad_of_input(x_ref, g, gm, w, gu, out_ref, shape):
    def one(n, carry):
        rows = span(n, 256)
        gu[:, rows] = matmul(gm[0:256, :], w[rows, :], NT)
        return carry

    lax.fori_loop(0, 4, one, 0)
    normed, inverse = normal(x_ref)
    grad_unit = gu[...]
    rows = inverse * (grad_unit - normed * jnp.mean(grad_unit * normed, axis=-1, keepdims=True))
    out_ref[...] = (g[...].reshape(256, D).astype(F32) + rows).astype(BF).reshape(shape + (D,))


def swap_rows(src, dst):
    at = lax.broadcasted_iota(jnp.int32, (256, 256), 0)
    row = lax.broadcasted_iota(jnp.int32, (256, 256), 1)
    swap = jnp.where(row == (at % 16) * 16 + at // 16, 1.0, 0.0).astype(BF)
    for n in range(2):
        cols = slice(n * 512, n * 512 + 512)
        out = matmul(swap, src[..., cols].reshape(256, 512)).astype(BF)
        dst[..., cols] = out.reshape(dst.shape[:-1] + (512,))


class Swap:
    def __init__(self, place, axis, send, recv, source, target):
        self.place, self.axis, self.send, self.recv = place, axis, send, recv
        self.source, self.target = source, target
        self.size = 8 if axis == "tm" else 16
        self.me = place.tm if axis == "tm" else place.ag

    def copy(self, step):
        to = (self.me + step) % self.size
        device = (self.place.ag, to) if self.axis == "tm" else (to, self.place.tm)
        return remote(self.source(to), self.target(self.me), self.send.at[step], self.recv.at[step], device)

    def local(self):
        return pltpu.make_async_copy(self.source(self.me), self.target(self.me), self.recv.at[0])

    def start(self):
        def one(step, carry):
            self.copy(step).start()
            return carry

        lax.fori_loop(1, self.size, one, 0)
        self.local().start()

    def wait(self):
        def one(step, carry):
            self.copy(step).wait_recv()
            return carry

        lax.fori_loop(1, self.size, one, 0)
        self.local().wait()

    def drain(self):
        def one(step, carry):
            self.copy(step).wait_send()
            return carry

        lax.fori_loop(1, self.size, one, 0)


def block_kernel(
    tokens, cotangent, observed, time_qkv, time_out, agent_qkv, agent_out,
    grad_tokens, tq_ref, to_ref, aq_ref, ao_ref,
    w_tq, w_to, w_aq, w_ao,
    x_time, made, home, turned, x_agent, cot, back,
    merged_t, merged_a, gmix, gu, bias_t, bias_a,
    units, gms, mixeds, g_time, g_agent,
    *rest,
):
    grad_a = rest[0]
    bufs = (rest[1:6], rest[6:11])
    load, swap_send, swap_recv, twin_send, twin_recv, sc_send, sc_recv = rest[11:]
    place = Place()
    loads = [
        pltpu.make_async_copy(src, dst, load.at[i])
        for i, (src, dst) in enumerate(
            (
                (cotangent, cot),
                (time_qkv, w_tq),
                (time_out, w_to),
                (agent_out, w_ao),
                (agent_qkv, w_aq),
            )
        )
    ]
    for copy in loads:
        copy.start()
    far = [
        (place.y * 4 + (1 - place.zlo) * 2 + place.core, (1 - place.zhi) * 4 + place.x),
    ]
    greet(
        [((place.ag + step) % 16, place.tm) for step in range(1, 16)]
        + [(place.ag, (place.tm + step) % 8) for step in range(1, 8)]
        + far
    )

    def swap(slot, axis, source, target):
        return Swap(place, axis, swap_send.at[slot], swap_recv.at[slot], source, target)

    def two(ref):
        return lambda i: ref.at[pl.ds(i * 2, 2)]

    def sixteen(ref):
        return lambda i: ref.at[0:2, span(i, 16), :]

    def rows16(ref):
        return lambda i: ref.at[span(i, 16), :]

    tokens_in = swap(0, "tm", two(tokens), sixteen(x_time))
    cot_in = swap(1, "ag", rows16(turned), rows16(g_agent))
    first_home = swap(2, "tm", sixteen(made), two(home))
    first_agent = swap(3, "ag", rows16(turned), rows16(x_agent))
    back_home = swap(4, "ag", rows16(cot), rows16(back))
    back_time = swap(5, "tm", two(home), sixteen(g_time))
    tokens_out = swap(6, "tm", sixteen(made), two(grad_tokens))
    twins = [Twin(place, twin_send.at[s], twin_recv.at[s]) for s in range(2)]

    def block_a(stream, slot):
        lo, hi, _ = STREAMS[stream]
        return grad_a.at[slot, :, lo:hi]

    def block_t(stream, slot):
        lo, hi, _ = STREAMS[stream]
        if stream < 2:
            return w_aq.at[span(slot, 128), lo:hi]
        return w_aq.at[span(slot + 4, 128), 0 : hi - lo]

    def second_a(stream):
        lo, hi, _ = STREAMS[stream]
        return w_aq.at[512 + stream * 128 : 640 + stream * 128, 1408 : 1408 + hi - lo]

    def second_t(stream):
        lo, hi, _ = STREAMS[stream]
        if stream < 2:
            return w_aq.at[384:512, lo:hi]
        return w_aq.at[896:1024, 0 : hi - lo]

    blocks, seconds = (block_a, block_t), (second_a, second_t)
    scatters = [Scatter(place, blocks[s], seconds[s], bufs[s], sc_send.at[s], sc_recv.at[s]) for s in range(2)]
    unit_a, unit_t = units.at[0], units.at[1]
    gm_a, gm_t = gms.at[0], gms.at[1]
    mixed_a, mixed_t = mixeds.at[0], mixeds.at[1]
    ut = [w_ao.at[0:512, 0:512], w_ao.at[0:512, 512:1024], w_ao.at[512:1024, 0:512]]
    ut_mixed = w_ao.at[512:1024, 512:1024]
    seqs = [slice(0, 128), slice(128, 256)]
    biases_t = [bias_t.at[0], bias_t.at[1]]

    with jax.named_scope("tokens_to_agents"):
        tokens_in.start()
        loads[0].wait()
        swap_rows(cot, turned)
        cot_in.start()
        self_t = lax.broadcasted_iota(jnp.int32, (128, 128), 0) == lax.broadcasted_iota(jnp.int32, (128, 128), 1)
        for a in range(2):
            row = observed[pl.ds(place.ag * 16 + place.tm * 2 + a, 1), :]
            bias_t[a] = jnp.where((row > 0) | self_t, 0.0, masked_score)
        at_step = lax.broadcasted_iota(jnp.int32, (8, STEPS), 1) == place.tm * 16 + place.ag
        seen = matmul(jnp.where(at_step, 1.0, 0.0).astype(BF), observed[...].astype(F32).astype(BF), NT)
        self_a = lax.broadcasted_iota(jnp.int32, (256, 256), 0) == lax.broadcasted_iota(jnp.int32, (256, 256), 1)
        bias_a[...] = jnp.where((seen[0:1, :] > 0.5) | self_a, 0.0, masked_score)
        loads[1].wait()
        tokens_in.wait()
    with jax.named_scope("time_forward"):
        project(x_time, unit_t, w_tq, merged_t)
        twins[1].copy(0, unit_t).start()
        attend(merged_t, mixed_t, seqs, biases_t, 4)
        twins[1].copy(2, mixed_t).start()
        loads[2].wait()
        add_residual(x_time, mixed_t, w_to, made, (2, 128))
        first_home.start()
    with jax.named_scope("first_to_steps"):
        cot_in.wait()
        twins[0].copy(3, g_agent).start()
        loads[3].wait()
        grad_of_mixed(g_agent.at[0:256, :], w_ao, gmix)
        cot_in.drain()
        first_home.wait()
        swap_rows(home, turned)
        first_agent.start()
        loads[4].wait()
        first_agent.wait()
    with jax.named_scope("agent_backward"):
        project(x_agent, unit_a, w_aq, merged_a)
        twins[0].copy(0, unit_a).start()
        attend_back(merged_a, gmix, mixed_a, gm_a, [slice(0, 256)], [bias_a], 2)
        twins[0].copy(2, mixed_a).start()
        twins[0].copy(1, gm_a).start()
        grad_of_input(x_agent, g_agent.at[0:256, :], gm_a, w_aq, gu, cot, (256,))
        back_home.start()
    with jax.named_scope("agent_weights"):
        for slot, ref in enumerate((unit_a, gm_a, mixed_a, g_agent)):
            twins[0].copy(slot, ref).wait_recv()
        transposed(place, unit_a, mixed_a, ut, ut_mixed, gu)
        for stream in range(3):
            scatters[0].start(stream, ut, ut_mixed, gm_a, g_agent)
    with jax.named_scope("grad_first_to_agents"):
        back_home.wait()
        swap_rows(back, home)
        back_time.start()
        back_time.wait()
        twins[1].copy_rows(3, g_time).start()
    with jax.named_scope("time_backward"):
        g_own = g_time.at[0:2]
        grad_of_mixed(g_own, w_to, gmix)
        attend_back(merged_t, gmix, None, gm_t, seqs, biases_t, 4)
        twins[1].copy(1, gm_t).start()
        first_home.drain()
        grad_of_input(x_time, g_own, gm_t, w_tq, gu, made, (2, 128))
        tokens_out.start()
    with jax.named_scope("time_weights"):
        for slot, ref in enumerate((unit_t, gm_t, mixed_t)):
            twins[1].copy(slot, ref).wait_recv()
        twins[1].copy_rows(3, g_time).wait_recv()
        transposed(place, unit_t, mixed_t, ut, ut_mixed, gu)
        for stream in range(3):
            scatters[1].start(stream, ut, ut_mixed, gm_t, g_time)
    with jax.named_scope("rings"):
        outs = ((aq_ref, ao_ref), (tq_ref, to_ref))
        for stream in range(3):
            scatters[0].second(stream)
        for stream in range(3):
            scatters[0].third(stream)
        for stream in range(3):
            scatters[1].second(stream)
        for stream in range(3):
            scatters[0].last(stream, *outs[0])
        for stream in range(3):
            scatters[1].third(stream)
        for stream in range(3):
            scatters[1].last(stream, *outs[1])
        tokens_out.wait()
    with jax.named_scope("drain"):
        for s in range(2):
            scatters[s].drain()
        for slot, ref in enumerate((unit_a, gm_a, mixed_a, g_agent)):
            twins[0].copy(slot, ref).wait_send()
        for slot, ref in enumerate((unit_t, gm_t, mixed_t)):
            twins[1].copy(slot, ref).wait_send()
        twins[1].copy_rows(3, g_time).wait_send()
        for moved in (tokens_in, first_agent, back_home, back_time, tokens_out):
            moved.drain()


def hand_on(*refs):
    copies = [pltpu.make_async_copy(refs[i], refs[5 + i], refs[10].at[i]) for i in range(5)]
    for copy in copies:
        copy.start()
    for copy in copies:
        copy.wait()


def local(tokens, cotangent, observed, time_qkv, time_out, agent_qkv, agent_out):
    shape = jax.ShapeDtypeStruct
    grad_tokens, *grads = pl.pallas_call(
        block_kernel,
        out_shape=[
            shape((16, 16, D), BF),
            shape((8, 3 * D), F32),
            shape((8, D), F32),
            shape((8, 3 * D), F32),
            shape((8, D), F32),
        ],
        in_specs=[
            pl.BlockSpec(memory_space=pl.ANY),
            pl.BlockSpec(memory_space=pl.ANY),
            pl.BlockSpec(memory_space=pltpu.VMEM),
        ]
        + [pl.BlockSpec(memory_space=pl.ANY)] * 4,
        out_specs=[pl.BlockSpec(memory_space=pl.ANY)] + [pl.BlockSpec(memory_space=pltpu.VMEM)] * 4,
        scratch_shapes=[
            pltpu.VMEM((D, 3 * D), BF),
            pltpu.VMEM((D, D), BF),
            pltpu.VMEM((D, 3 * D), BF),
            pltpu.VMEM((D, D), BF),
            pltpu.VMEM((2, 128, D), BF),
            pltpu.VMEM((2, 128, D), BF),
            pltpu.VMEM((16, 16, D), BF),
            pltpu.VMEM((256, D), BF),
            pltpu.VMEM((256, D), BF),
            pltpu.VMEM((256, D), BF),
            pltpu.VMEM((256, D), BF),
            pltpu.VMEM((256, 3 * D), BF),
            pltpu.VMEM((256, 3 * D), BF),
            pltpu.VMEM((256, D), BF),
            pltpu.VMEM((256, D), F32),
            pltpu.VMEM((2, 128, 128), F32),
            pltpu.VMEM((256, 256), F32),
            pltpu.VMEM((2, 512, D), BF),
            pltpu.VMEM((2, 512, 3 * D), BF),
            pltpu.VMEM((2, 512, D), BF),
            pltpu.VMEM((4, 128, D), BF),
            pltpu.VMEM((512, D), BF),
        ]
        + [pltpu.VMEM((3, 128, 4096), BF)]
        + scatter_bufs()
        + scatter_bufs()
        + [
            pltpu.SemaphoreType.DMA((5,)),
            pltpu.SemaphoreType.DMA((7, 16)),
            pltpu.SemaphoreType.DMA((7, 16)),
            pltpu.SemaphoreType.DMA((2, 4)),
            pltpu.SemaphoreType.DMA((2, 4)),
            pltpu.SemaphoreType.DMA((2, 3, 3, 3)),
            pltpu.SemaphoreType.DMA((2, 3, 3, 3)),
        ],
        compiler_params=pltpu.CompilerParams(
            collective_id=0, has_side_effects=True, vmem_limit_bytes=61 * 1024 * 1024
        ),
    )(
        tokens.reshape(16, 16, D),
        cotangent.reshape(256, D),
        observed.reshape(256, STEPS),
        time_qkv,
        time_out,
        agent_qkv,
        agent_out,
    )
    made = [grad_tokens, *grads]
    grad_tokens, *grads = pl.pallas_call(
        hand_on,
        out_shape=[shape(x.shape, x.dtype) for x in made],
        in_specs=[pl.BlockSpec(memory_space=pl.ANY)] * 5,
        out_specs=[pl.BlockSpec(memory_space=pl.ANY)] * 5,
        scratch_shapes=[pltpu.SemaphoreType.DMA((5,))],
    )(*made)
    return (grad_tokens.reshape(1, 16, 16, D), *grads)


def solution(mesh):
    in_specs = (P(None, "ag", "tm", None), P(None, "ag", "tm", None), P(), P(), P(), P(), P())
    out_specs = (
        P(None, "ag", "tm", None),
        P(("ag", "tm"), None),
        P(("ag", "tm"), None),
        P(("ag", "tm"), None),
        P(("ag", "tm"), None),
    )
    return jax.shard_map(local, mesh=mesh, in_specs=in_specs, out_specs=out_specs, check_vma=False)
```

```python
import functools

import jax
import jax.numpy as jnp
from jax import lax
from jax.experimental import pallas as pl
from jax.experimental.pallas import tpu as pltpu
from jax.sharding import PartitionSpec as P

D = 1024
H = 16
HD = 64
STEPS = 128
epsilon = 1e-06
masked_score = -1e30

MESH = pl.DeviceIdType.MESH
BF = jnp.bfloat16
F32 = jnp.float32
NT = (((1,), (1,)), ((), ()))
TN = (((0,), (0,)), ((), ()))

STREAMS = ((0, 1408, "xyz"), (1408, 2816, "yzx"), (2816, 4096, "zxy"))


def matmul(left, right, dims=(((1,), (0,)), ((), ()))):
    return lax.dot_general(left, right, dims, preferred_element_type=F32)


class Place:
    def __init__(self):
        self.ag = lax.axis_index("ag")
        self.tm = lax.axis_index("tm")
        self.y = self.ag // 4
        self.zlo = (self.ag // 2) % 2
        self.core = self.ag % 2
        self.zhi = self.tm // 4
        self.x = self.tm % 4
        self.z = self.zhi * 2 + self.zlo

    def at(self, axis):
        return {"x": self.x, "y": self.y, "z": self.z}[axis]

    def ring(self, axis, step):
        if axis == "x":
            return (self.ag, self.zhi * 4 + (self.x + step) % 4)
        if axis == "y":
            return (((self.y + step) % 4) * 4 + self.ag % 4, self.tm)
        z = (self.z + step) % 4
        return (self.y * 4 + (z % 2) * 2 + self.core, (z // 2) * 4 + self.x)

    def twin(self):
        return (self.ag + 1 - 2 * self.core, self.tm)


def remote(src, dst, send, recv, device):
    return pltpu.make_async_remote_copy(
        src_ref=src, dst_ref=dst, send_sem=send, recv_sem=recv, device_id=device, device_id_type=MESH
    )


def greet(devices):
    barrier = pltpu.get_barrier_semaphore()
    for device in devices:
        pl.semaphore_signal(barrier, inc=1, device_id=device, device_id_type=MESH)
    pl.semaphore_wait(barrier, len(devices))


def selector(core, x_first):
    at = lax.broadcasted_iota(jnp.int32, (128, 256), 0)
    row = lax.broadcasted_iota(jnp.int32, (128, 256), 1)
    high, low = at // 32, (at // 8) % 4
    x, z = (high, low) if x_first else (low, high)
    wanted = (z % 2) * 128 + core * 64 + (z // 2) * 32 + x * 8 + at % 8
    return jnp.where(row == wanted, 1.0, 0.0).astype(BF)


class Twin:
    def __init__(self, place, send, recv):
        self.place, self.send, self.recv = place, send, recv

    def copy(self, slot, ref, cols=None):
        cols = slice(None) if cols is None else cols
        return remote(
            ref.at[0:256, cols], ref.at[256:512, cols], self.send.at[slot], self.recv.at[slot], self.place.twin()
        )

    def copy_rows(self, slot, ref):
        return remote(ref.at[0:2], ref.at[2:4], self.send.at[slot], self.recv.at[slot], self.place.twin())


class Scatter:
    def __init__(self, place, block, second_block, bufs, send, recv):
        self.place, self.second_block = place, second_block
        self.block, (self.own, self.r1, self.r2, self.s3, self.r3) = block, bufs
        self.send, self.recv = send, recv

    def copy(self, stream, phase, step):
        lo, hi, axes = STREAMS[stream]
        cols = slice(lo, hi)
        axis = axes[phase]
        to = (self.place.at(axis) + step) % 4
        slot = step - 1
        if phase == 0:
            src, dst = self.block(stream, slot), self.r1.at[slot, :, cols]
        elif phase == 1:
            src = self.second_block(stream).at[pl.ds(pl.multiple_of(to * 32, 32), 32), :]
            dst = self.r2.at[slot, :, cols]
        else:
            src = self.s3.at[to, :, cols]
            dst = self.r3.at[slot, :, cols]
        return remote(
            src,
            dst,
            self.send.at[stream, phase, slot],
            self.recv.at[stream, phase, slot],
            self.place.ring(axis, step),
        )

    def product(self, stream, ut, ut_mixed, gm, g, block):
        lo, hi, _ = STREAMS[stream]
        rows = pl.ds(pl.multiple_of(block * 128, 128), 128)
        if stream < 2:
            return [(lo, hi, matmul(ut[stream][rows, :], gm[:, lo:hi]))]
        return [
            (lo, 3072, matmul(ut[2][rows, :], gm[:, lo:3072])),
            (3072, 4096, matmul(ut_mixed[rows, :], g[...].reshape(512, D))),
        ]

    def start(self, stream, ut, ut_mixed, gm, g):
        first, _, axes = STREAMS[stream]
        at = self.place.at(axes[0])

        def one(step, carry):
            for lo, hi, part in self.product(stream, ut, ut_mixed, gm, g, (at + step) % 4):
                self.block(stream, step - 1)[:, lo - first : hi - first] = part.astype(BF)
            self.copy(stream, 0, step).start()
            return carry

        lax.fori_loop(1, 4, one, 0)
        for lo, hi, part in self.product(stream, ut, ut_mixed, gm, g, at):
            self.own[:, lo:hi] = part

    def second(self, stream):
        lo, hi, _ = STREAMS[stream]
        for step in (1, 2, 3):
            self.copy(stream, 0, step).wait_recv()

        def one(q, carry):
            rows = pl.ds(pl.multiple_of(q * 32, 32), 32)
            total = self.own[rows, lo:hi]
            for slot in range(3):
                total = total + self.r1[slot, rows, lo:hi].astype(F32)
            self.own[rows, lo:hi] = total
            self.second_block(stream)[rows, :] = total.astype(BF)
            return carry

        lax.fori_loop(0, 4, one, 0)
        for step in (1, 2, 3):
            self.copy(stream, 1, step).start()

    def third(self, stream):
        lo, hi, axes = STREAMS[stream]
        for step in (1, 2, 3):
            self.copy(stream, 1, step).wait_recv()
        total = self.own[pl.ds(pl.multiple_of(self.place.at(axes[1]) * 32, 32), 32), lo:hi]
        for slot in range(3):
            total = total + self.r2[slot, :, lo:hi].astype(F32)
        self.own[0:32, lo:hi] = total
        for q in range(4):
            self.s3[q, :, lo:hi] = total[q * 8 : q * 8 + 8].astype(BF)
        for step in (1, 2, 3):
            self.copy(stream, 2, step).start()

    def last(self, stream, qkv_ref, out_ref):
        lo, hi, axes = STREAMS[stream]
        for step in (1, 2, 3):
            self.copy(stream, 2, step).wait_recv()
        total = self.own[pl.ds(pl.multiple_of(self.place.at(axes[2]) * 8, 8), 8), lo:hi]
        for slot in range(3):
            total = total + self.r3[slot, :, lo:hi].astype(F32)
        top = min(hi, 3072)
        qkv_ref[:, lo:top] = total[:, : top - lo]
        if hi > 3072:
            out_ref[...] = total[:, 3072 - lo :]

    def drain(self):
        for stream in range(3):
            for phase in range(3):
                for step in (1, 2, 3):
                    self.copy(stream, phase, step).wait_send()


def scatter_bufs():
    return [
        pltpu.VMEM((128, 4096), F32),
        pltpu.VMEM((3, 128, 4096), BF),
        pltpu.VMEM((3, 32, 4096), BF),
        pltpu.VMEM((4, 8, 4096), BF),
        pltpu.VMEM((3, 8, 4096), BF),
    ]


def transposed(place, unit, mixed, ut, ut_mixed, spare):
    sel_x = selector(place.core, True)
    sel_z = selector(place.core, False)

    def last_order(part, y):
        for z in range(4):
            for x in range(4):
                at = (z % 2) * 128 + x * 32 + y * 8
                spare[at : at + 8, (z // 2) * 512 : (z // 2) * 512 + 512] = part[z * 32 + x * 8 : z * 32 + x * 8 + 8]

    for y in range(4):
        cols = slice(y * 256, y * 256 + 256)
        part = matmul(sel_x, unit[:, cols], NT).astype(BF)
        for x in range(4):
            ut[0][x * 128 + y * 32 : x * 128 + y * 32 + 32, :] = part[x * 32 : x * 32 + 32]
        part = matmul(sel_z, unit[:, cols], NT)
        ut[1][y * 128 : y * 128 + 128, :] = part.astype(BF)
        last_order(part, y)
    ut[2][0:256, :] = spare[:, 0:512].astype(BF)
    ut[2][256:512, :] = spare[:, 512:1024].astype(BF)
    for y in range(4):
        last_order(matmul(sel_z, mixed[:, y * 256 : y * 256 + 256], NT), y)
    ut_mixed[0:256, :] = spare[:, 0:512].astype(BF)
    ut_mixed[256:512, :] = spare[:, 512:1024].astype(BF)


def normal(x_ref):
    x = x_ref[...].reshape(256, D).astype(F32)
    inverse = lax.rsqrt(jnp.mean(x * x, axis=-1, keepdims=True) + epsilon)
    return x * inverse, inverse


def span(start, size):
    return pl.ds(pl.multiple_of(start * size, size), size)


def project(x_ref, unit, w, merged):
    unit[0:256, :] = normal(x_ref)[0].astype(BF)

    def one(n, carry):
        cols = span(n, 512)
        merged[:, cols] = matmul(unit[0:256, :], w[:, cols]).astype(BF)
        return carry

    lax.fori_loop(0, 6, one, 0)


def halves():
    lane = lax.broadcasted_iota(jnp.int32, (1, 128), 1)
    low = jnp.where(lane < HD, 1.0, 0.0)
    return low.astype(BF), (1.0 - low).astype(BF)


def pair_parts(merged, rows, pair):
    q = merged[rows, span(pair, 128)] * BF(HD**-0.5)
    k = merged[rows, pl.ds(pl.multiple_of(D + pair * 128, 128), 128)]
    v = merged[rows, pl.ds(pl.multiple_of(2 * D + pair * 128, 128), 128)]
    return q, k, v


def attend(merged, mixed, seqs, biases, group):
    def one(turn, carry):
        low_high = halves()
        jobs = []
        for rows, bias in zip(seqs, biases):
            for i in range(group):
                pair = turn * group + i
                q, k, v = pair_parts(merged, rows, pair)
                for half in low_high:
                    jobs.append((rows, pair, bias, q * half, k, v * half))
        scores = [matmul(q, k, NT) + bias[...] for _, _, bias, q, k, _ in jobs]
        probs = probs_of(scores)
        parts = [matmul(p.astype(BF), job[5]) for p, job in zip(probs, jobs)]
        for i in range(0, len(jobs), 2):
            rows, pair = jobs[i][:2]
            mixed[rows, span(pair, 128)] = (parts[i] + parts[i + 1]).astype(BF)
        return carry

    lax.fori_loop(0, H // 2 // group, one, 0)


def probs_of(scores):
    tops = [jnp.max(s, axis=-1, keepdims=True) for s in scores]
    shifted = [jnp.exp(s - t) for s, t in zip(scores, tops)]
    sums = [jnp.sum(s, axis=-1, keepdims=True) for s in shifted]
    return [s * (1.0 / t) for s, t in zip(shifted, sums)]


def attend_back(merged, gmix, mixed, gm, seqs, biases, group):
    def one(turn, carry):
        low_high = halves()
        jobs = []
        for rows, bias in zip(seqs, biases):
            for i in range(group):
                pair = turn * group + i
                q, k, v = pair_parts(merged, rows, pair)
                go = gmix[rows, span(pair, 128)]
                for half in low_high:
                    jobs.append((rows, pair, bias, q * half, k, v, go * half, half))
        scores = [matmul(job[3], job[4], NT) + job[2][...] for job in jobs]
        gps = [matmul(job[6], job[5], NT) for job in jobs]
        probs = probs_of(scores)
        means = [jnp.sum(gp * p, axis=-1, keepdims=True) for gp, p in zip(gps, probs)]
        gss = [(p * (gp - m)).astype(BF) for p, gp, m in zip(probs, gps, means)]
        rounded = [p.astype(BF) for p in probs]
        gq = [matmul(gs, job[4] * job[7]) for gs, job in zip(gss, jobs)]
        gk = [matmul(gs, job[3], TN) for gs, job in zip(gss, jobs)]
        gv = [matmul(p, job[6], TN) for p, job in zip(rounded, jobs)]
        if mixed is not None:
            mx = [matmul(p, job[5] * job[7]) for p, job in zip(rounded, jobs)]
        for i in range(0, len(jobs), 2):
            rows, pair = jobs[i][:2]
            gm[rows, span(pair, 128)] = ((gq[i] + gq[i + 1]) * HD**-0.5).astype(BF)
            gm[rows, pl.ds(pl.multiple_of(D + pair * 128, 128), 128)] = (gk[i] + gk[i + 1]).astype(BF)
            gm[rows, pl.ds(pl.multiple_of(2 * D + pair * 128, 128), 128)] = (gv[i] + gv[i + 1]).astype(BF)
            if mixed is not None:
                mixed[rows, span(pair, 128)] = (mx[i] + mx[i + 1]).astype(BF)
        return carry

    lax.fori_loop(0, H // 2 // group, one, 0)


def add_residual(x_ref, mixed, w, out_ref, shape):
    for n in range(2):
        cols = slice(n * 512, n * 512 + 512)
        x = x_ref[..., cols].reshape(256, 512).astype(F32)
        out = x + matmul(mixed[0:256, :], w[:, cols])
        out_ref[..., cols] = out.astype(BF).reshape(shape + (512,))


def grad_of_mixed(g, w, gmix):
    def one(n, carry):
        rows = span(n, 256)
        gmix[:, rows] = matmul(g[...].reshape(256, D), w[rows, :], NT).astype(BF)
        return carry

    lax.fori_loop(0, 4, one, 0)


def grad_of_input(x_ref, g, gm, w, gu, out_ref, shape):
    def one(n, carry):
        rows = span(n, 256)
        gu[:, rows] = matmul(gm[0:256, :], w[rows, :], NT)
        return carry

    lax.fori_loop(0, 4, one, 0)
    normed, inverse = normal(x_ref)
    grad_unit = gu[...]
    rows = inverse * (grad_unit - normed * jnp.mean(grad_unit * normed, axis=-1, keepdims=True))
    out_ref[...] = (g[...].reshape(256, D).astype(F32) + rows).astype(BF).reshape(shape + (D,))


def swap_rows(src, dst):
    at = lax.broadcasted_iota(jnp.int32, (256, 256), 0)
    row = lax.broadcasted_iota(jnp.int32, (256, 256), 1)
    swap = jnp.where(row == (at % 16) * 16 + at // 16, 1.0, 0.0).astype(BF)
    for n in range(2):
        cols = slice(n * 512, n * 512 + 512)
        out = matmul(swap, src[..., cols].reshape(256, 512)).astype(BF)
        dst[..., cols] = out.reshape(dst.shape[:-1] + (512,))


class Swap:
    def __init__(self, place, axis, send, recv, source, target):
        self.place, self.axis, self.send, self.recv = place, axis, send, recv
        self.source, self.target = source, target
        self.size = 8 if axis == "tm" else 16
        self.me = place.tm if axis == "tm" else place.ag

    def copy(self, step):
        to = (self.me + step) % self.size
        device = (self.place.ag, to) if self.axis == "tm" else (to, self.place.tm)
        return remote(self.source(to), self.target(self.me), self.send.at[step], self.recv.at[step], device)

    def local(self):
        return pltpu.make_async_copy(self.source(self.me), self.target(self.me), self.recv.at[0])

    def start(self):
        def one(step, carry):
            self.copy(step).start()
            return carry

        lax.fori_loop(1, self.size, one, 0)
        self.local().start()

    def wait(self):
        def one(step, carry):
            self.copy(step).wait_recv()
            return carry

        lax.fori_loop(1, self.size, one, 0)
        self.local().wait()

    def drain(self):
        def one(step, carry):
            self.copy(step).wait_send()
            return carry

        lax.fori_loop(1, self.size, one, 0)


def spread_index():
    at = lax.broadcasted_iota(jnp.int32, (256, 256), 0)
    row = lax.broadcasted_iota(jnp.int32, (256, 256), 1)
    return at, row


def one_hot(wanted, row):
    return jnp.where(row == wanted, 1.0, 0.0).astype(BF)


def pack_time(src, dst):
    at, row = spread_index()
    i, c, a = at // 16, (at // 2) % 8, at % 2
    turn = one_hot(c * 32 + a * 16 + i, row)

    def one(n, carry):
        rows = span(n, 16)
        parts = [src[a, rows, c * 128 : c * 128 + 128] for c in range(8) for a in range(2)]
        out = matmul(turn, jnp.concatenate(parts, axis=0)).astype(BF)
        dst[rows] = out.reshape(16, 16, 128)
        return carry

    lax.fori_loop(0, 8, one, 0)


def unpack_time(src, dst):
    at, row = spread_index()
    c, a, i = at // 32, (at // 16) % 2, at % 16
    turn = one_hot(i * 16 + c * 2 + a, row)

    def one(n, carry):
        rows = span(n, 16)
        out = matmul(turn, src[rows].reshape(256, 128)).astype(BF)
        for c in range(8):
            for a in range(2):
                part = out[c * 32 + a * 16 : c * 32 + a * 16 + 16]
                dst[a, rows, c * 128 : c * 128 + 128] = part
        return carry

    lax.fori_loop(0, 8, one, 0)


def pack_agent(src, dst):
    at, row = spread_index()
    i, c, a = at // 16, (at // 2) % 8, at % 2
    turn = one_hot(c * 32 + i * 2 + a, row)

    def one(n, carry):
        parts = [src[span(n, 32), c * 128 : c * 128 + 128] for c in range(8)]
        out = matmul(turn, jnp.concatenate(parts, axis=0)).astype(BF)
        dst[span(n, 16)] = out.reshape(16, 16, 128)
        return carry

    lax.fori_loop(0, 8, one, 0)


def unpack_agent(src, dst):
    at, row = spread_index()
    c, i, a = at // 32, (at // 2) % 16, at % 2
    turn = one_hot(i * 16 + c * 2 + a, row)

    def one(n, carry):
        out = matmul(turn, src[span(n, 16)].reshape(256, 128)).astype(BF)
        for c in range(8):
            dst[span(n, 32), c * 128 : c * 128 + 128] = out[c * 32 : c * 32 + 32]
        return carry

    lax.fori_loop(0, 8, one, 0)


class Spread:
    def __init__(self, place, send, recv, src, dst, to_steps):
        self.place, self.send, self.recv, self.src, self.dst, self.to_steps = place, send, recv, src, dst, to_steps

    def places(self, ag, tm):
        return ag * 8 + tm, tm * 16 + ag

    def start(self):
        place = self.place
        agents, steps = self.places(place.ag, place.tm)
        mine = agents if self.to_steps else steps

        def one(step, carry):
            ag, tm = (place.ag + step // 8) % 16, (place.tm + step % 8) % 8
            by_agents, by_steps = self.places(ag, tm)
            theirs = by_steps if self.to_steps else by_agents
            remote(self.src.at[theirs], self.dst.at[mine], self.send, self.recv, (ag, tm)).start()
            return carry

        lax.fori_loop(1, 128, one, 0)
        own = steps if self.to_steps else agents
        pltpu.make_async_copy(self.src.at[own], self.dst.at[mine], self.recv).start()

    def wait(self):
        pltpu.make_async_copy(self.src, self.dst, self.recv).wait()

    def drain(self):
        pltpu.make_async_copy(self.src.at[0:127], self.dst.at[0:127], self.send).wait()


def block_kernel(
    tokens, cotangent, observed, time_qkv, time_out, agent_qkv, agent_out,
    grad_tokens, tq_ref, to_ref, aq_ref, ao_ref,
    w_tq, w_to, w_aq, w_ao,
    x_time, made, turned, x_agent, cot, tiles_out, first_in, back_in,
    merged_t, merged_a, gmix, gu, bias_t, bias_a,
    units, gms, mixeds, g_time, g_agent,
    *rest,
):
    grad_a = rest[0]
    bufs = (rest[1:6], rest[6:11])
    load, spread_send, spread_recv, swap_send, swap_recv, twin_send, twin_recv, sc_send, sc_recv = rest[11:]
    place = Place()
    loads = [
        pltpu.make_async_copy(src, dst, load.at[i])
        for i, (src, dst) in enumerate(
            (
                (cotangent, cot),
                (time_qkv, w_tq),
                (time_out, w_to),
                (agent_out, w_ao),
                (agent_qkv, w_aq),
            )
        )
    ]
    for copy in loads:
        copy.start()
    far = [
        (place.y * 4 + (1 - place.zlo) * 2 + place.core, (1 - place.zhi) * 4 + place.x),
    ]
    greet(
        [((place.ag + step) % 16, place.tm) for step in range(1, 16)]
        + [(place.ag, (place.tm + step) % 8) for step in range(1, 8)]
        + far
    )

    def swap(slot, axis, source, target):
        return Swap(place, axis, swap_send.at[slot], swap_recv.at[slot], source, target)

    def two(ref):
        return lambda i: ref.at[pl.ds(i * 2, 2)]

    def sixteen(ref):
        return lambda i: ref.at[0:2, span(i, 16), :]

    def rows16(ref):
        return lambda i: ref.at[span(i, 16), :]

    tokens_in = swap(0, "tm", two(tokens), sixteen(x_time))
    cot_in = swap(1, "ag", rows16(turned), rows16(g_agent))
    first = Spread(place, spread_send.at[0], spread_recv.at[0], tiles_out, first_in, True)
    back = Spread(place, spread_send.at[1], spread_recv.at[1], tiles_out, back_in, False)
    tokens_out = swap(2, "tm", sixteen(made), two(grad_tokens))
    twins = [Twin(place, twin_send.at[s], twin_recv.at[s]) for s in range(2)]

    def block_a(stream, slot):
        lo, hi, _ = STREAMS[stream]
        return grad_a.at[slot, :, lo:hi]

    def block_t(stream, slot):
        lo, hi, _ = STREAMS[stream]
        if stream < 2:
            return w_aq.at[span(slot, 128), lo:hi]
        return w_aq.at[span(slot + 4, 128), 0 : hi - lo]

    def second_a(stream):
        lo, hi, _ = STREAMS[stream]
        return w_aq.at[512 + stream * 128 : 640 + stream * 128, 1408 : 1408 + hi - lo]

    def second_t(stream):
        lo, hi, _ = STREAMS[stream]
        if stream < 2:
            return w_aq.at[384:512, lo:hi]
        return w_aq.at[896:1024, 0 : hi - lo]

    blocks, seconds = (block_a, block_t), (second_a, second_t)
    scatters = [Scatter(place, blocks[s], seconds[s], bufs[s], sc_send.at[s], sc_recv.at[s]) for s in range(2)]
    unit_a, unit_t = units.at[0], units.at[1]
    gm_a, gm_t = gms.at[0], gms.at[1]
    mixed_a, mixed_t = mixeds.at[0], mixeds.at[1]
    ut = [w_ao.at[0:512, 0:512], w_ao.at[0:512, 512:1024], w_ao.at[512:1024, 0:512]]
    ut_mixed = w_ao.at[512:1024, 512:1024]
    seqs = [slice(0, 128), slice(128, 256)]
    biases_t = [bias_t.at[0], bias_t.at[1]]

    with jax.named_scope("tokens_to_agents"):
        tokens_in.start()
        loads[0].wait()
        swap_rows(cot, turned)
        cot_in.start()
        self_t = lax.broadcasted_iota(jnp.int32, (128, 128), 0) == lax.broadcasted_iota(jnp.int32, (128, 128), 1)
        for a in range(2):
            row = observed[pl.ds(place.ag * 16 + place.tm * 2 + a, 1), :]
            bias_t[a] = jnp.where((row > 0) | self_t, 0.0, masked_score)
        at_step = lax.broadcasted_iota(jnp.int32, (8, STEPS), 1) == place.tm * 16 + place.ag
        seen = matmul(jnp.where(at_step, 1.0, 0.0).astype(BF), observed[...].astype(F32).astype(BF), NT)
        self_a = lax.broadcasted_iota(jnp.int32, (256, 256), 0) == lax.broadcasted_iota(jnp.int32, (256, 256), 1)
        bias_a[...] = jnp.where((seen[0:1, :] > 0.5) | self_a, 0.0, masked_score)
        loads[1].wait()
        tokens_in.wait()
    with jax.named_scope("time_forward"):
        project(x_time, unit_t, w_tq, merged_t)
        twins[1].copy(0, unit_t).start()
        attend(merged_t, mixed_t, seqs, biases_t, 4)
        twins[1].copy(2, mixed_t).start()
        loads[2].wait()
        add_residual(x_time, mixed_t, w_to, made, (2, 128))
        pack_time(made, tiles_out)
        first.start()
    with jax.named_scope("first_to_steps"):
        cot_in.wait()
        twins[0].copy(3, g_agent).start()
        loads[3].wait()
        grad_of_mixed(g_agent.at[0:256, :], w_ao, gmix)
        cot_in.drain()
        loads[4].wait()
        first.wait()
        unpack_agent(first_in, x_agent)
    with jax.named_scope("agent_backward"):
        project(x_agent, unit_a, w_aq, merged_a)
        twins[0].copy(0, unit_a).start()
        attend_back(merged_a, gmix, mixed_a, gm_a, [slice(0, 256)], [bias_a], 2)
        twins[0].copy(2, mixed_a).start()
        twins[0].copy(1, gm_a).start()
        grad_of_input(x_agent, g_agent.at[0:256, :], gm_a, w_aq, gu, cot, (256,))
        first.drain()
        pack_agent(cot, tiles_out)
        back.start()
    with jax.named_scope("agent_weights"):
        for slot, ref in enumerate((unit_a, gm_a, mixed_a, g_agent)):
            twins[0].copy(slot, ref).wait_recv()
        transposed(place, unit_a, mixed_a, ut, ut_mixed, gu)
        for stream in range(3):
            scatters[0].start(stream, ut, ut_mixed, gm_a, g_agent)
    with jax.named_scope("grad_first_to_agents"):
        back.wait()
        unpack_time(back_in, g_time)
        twins[1].copy_rows(3, g_time).start()
    with jax.named_scope("time_backward"):
        g_own = g_time.at[0:2]
        grad_of_mixed(g_own, w_to, gmix)
        attend_back(merged_t, gmix, None, gm_t, seqs, biases_t, 4)
        twins[1].copy(1, gm_t).start()
        grad_of_input(x_time, g_own, gm_t, w_tq, gu, made, (2, 128))
        tokens_out.start()
    with jax.named_scope("time_weights"):
        for slot, ref in enumerate((unit_t, gm_t, mixed_t)):
            twins[1].copy(slot, ref).wait_recv()
        twins[1].copy_rows(3, g_time).wait_recv()
        transposed(place, unit_t, mixed_t, ut, ut_mixed, gu)
        for stream in range(3):
            scatters[1].start(stream, ut, ut_mixed, gm_t, g_time)
    with jax.named_scope("rings"):
        outs = ((aq_ref, ao_ref), (tq_ref, to_ref))
        for stream in range(3):
            scatters[0].second(stream)
        for stream in range(3):
            scatters[0].third(stream)
        for stream in range(3):
            scatters[1].second(stream)
        for stream in range(3):
            scatters[0].last(stream, *outs[0])
        for stream in range(3):
            scatters[1].third(stream)
        for stream in range(3):
            scatters[1].last(stream, *outs[1])
        tokens_out.wait()
    with jax.named_scope("drain"):
        for s in range(2):
            scatters[s].drain()
        for slot, ref in enumerate((unit_a, gm_a, mixed_a, g_agent)):
            twins[0].copy(slot, ref).wait_send()
        for slot, ref in enumerate((unit_t, gm_t, mixed_t)):
            twins[1].copy(slot, ref).wait_send()
        twins[1].copy_rows(3, g_time).wait_send()
        for moved in (tokens_in, back, tokens_out):
            moved.drain()


def hand_on(*refs):
    for source, target in zip(refs[:5], refs[5:]):
        target[...] = source[...]


def local(tokens, cotangent, observed, time_qkv, time_out, agent_qkv, agent_out):
    shape = jax.ShapeDtypeStruct
    grad_tokens, *grads = pl.pallas_call(
        block_kernel,
        out_shape=[
            shape((16, 16, D), BF),
            shape((8, 3 * D), F32),
            shape((8, D), F32),
            shape((8, 3 * D), F32),
            shape((8, D), F32),
        ],
        in_specs=[
            pl.BlockSpec(memory_space=pl.ANY),
            pl.BlockSpec(memory_space=pl.ANY),
            pl.BlockSpec(memory_space=pltpu.VMEM),
        ]
        + [pl.BlockSpec(memory_space=pl.ANY)] * 4,
        out_specs=[pl.BlockSpec(memory_space=pl.ANY)] + [pl.BlockSpec(memory_space=pltpu.VMEM)] * 4,
        scratch_shapes=[
            pltpu.VMEM((D, 3 * D), BF),
            pltpu.VMEM((D, D), BF),
            pltpu.VMEM((D, 3 * D), BF),
            pltpu.VMEM((D, D), BF),
            pltpu.VMEM((2, 128, D), BF),
            pltpu.VMEM((2, 128, D), BF),
            pltpu.VMEM((256, D), BF),
            pltpu.VMEM((256, D), BF),
            pltpu.VMEM((256, D), BF),
            pltpu.VMEM((128, 16, 128), BF),
            pltpu.VMEM((128, 16, 128), BF),
            pltpu.VMEM((128, 16, 128), BF),
            pltpu.VMEM((256, 3 * D), BF),
            pltpu.VMEM((256, 3 * D), BF),
            pltpu.VMEM((256, D), BF),
            pltpu.VMEM((256, D), F32),
            pltpu.VMEM((2, 128, 128), F32),
            pltpu.VMEM((256, 256), F32),
            pltpu.VMEM((2, 512, D), BF),
            pltpu.VMEM((2, 512, 3 * D), BF),
            pltpu.VMEM((2, 512, D), BF),
            pltpu.VMEM((4, 128, D), BF),
            pltpu.VMEM((512, D), BF),
        ]
        + [pltpu.VMEM((3, 128, 4096), BF)]
        + scatter_bufs()
        + scatter_bufs()
        + [
            pltpu.SemaphoreType.DMA((5,)),
            pltpu.SemaphoreType.DMA((2,)),
            pltpu.SemaphoreType.DMA((2,)),
            pltpu.SemaphoreType.DMA((3, 16)),
            pltpu.SemaphoreType.DMA((3, 16)),
            pltpu.SemaphoreType.DMA((2, 4)),
            pltpu.SemaphoreType.DMA((2, 4)),
            pltpu.SemaphoreType.DMA((2, 3, 3, 3)),
            pltpu.SemaphoreType.DMA((2, 3, 3, 3)),
        ],
        compiler_params=pltpu.CompilerParams(
            collective_id=0, has_side_effects=True, vmem_limit_bytes=61 * 1024 * 1024
        ),
    )(
        tokens.reshape(16, 16, D),
        cotangent.reshape(256, D),
        observed.reshape(256, STEPS),
        time_qkv,
        time_out,
        agent_qkv,
        agent_out,
    )
    made = [grad_tokens, *grads]
    grad_tokens, *grads = pl.pallas_call(
        hand_on,
        out_shape=[shape(x.shape, x.dtype) for x in made],
        in_specs=[pl.BlockSpec(memory_space=pltpu.VMEM)] * 5,
        out_specs=[pl.BlockSpec(memory_space=pltpu.VMEM)] * 5,
    )(*made)
    return (grad_tokens.reshape(1, 16, 16, D), *grads)


def solution(mesh):
    in_specs = (P(None, "ag", "tm", None), P(None, "ag", "tm", None), P(), P(), P(), P(), P())
    out_specs = (
        P(None, "ag", "tm", None),
        P(("ag", "tm"), None),
        P(("ag", "tm"), None),
        P(("ag", "tm"), None),
        P(("ag", "tm"), None),
    )
    return jax.shard_map(local, mesh=mesh, in_specs=in_specs, out_specs=out_specs, check_vma=False)
```

```python
import functools

import jax
import jax.numpy as jnp
from jax import lax
from jax.experimental import pallas as pl
from jax.experimental.pallas import tpu as pltpu
from jax.sharding import PartitionSpec as P

D = 1024
H = 16
HD = 64
STEPS = 128
epsilon = 1e-06
masked_score = -1e30

MESH = pl.DeviceIdType.MESH
BF = jnp.bfloat16
F32 = jnp.float32
NT = (((1,), (1,)), ((), ()))
TN = (((0,), (0,)), ((), ()))

STREAMS = ((0, 1408, "xyz"), (1408, 2816, "yzx"), (2816, 4096, "zxy"))


def matmul(left, right, dims=(((1,), (0,)), ((), ()))):
    return lax.dot_general(left, right, dims, preferred_element_type=F32)


class Place:
    def __init__(self):
        self.ag = lax.axis_index("ag")
        self.tm = lax.axis_index("tm")
        self.y = self.ag // 4
        self.zlo = (self.ag // 2) % 2
        self.core = self.ag % 2
        self.zhi = self.tm // 4
        self.x = self.tm % 4
        self.z = self.zhi * 2 + self.zlo

    def at(self, axis):
        return {"x": self.x, "y": self.y, "z": self.z}[axis]

    def ring(self, axis, step):
        if axis == "x":
            return (self.ag, self.zhi * 4 + (self.x + step) % 4)
        if axis == "y":
            return (((self.y + step) % 4) * 4 + self.ag % 4, self.tm)
        z = (self.z + step) % 4
        return (self.y * 4 + (z % 2) * 2 + self.core, (z // 2) * 4 + self.x)

    def twin(self):
        return (self.ag + 1 - 2 * self.core, self.tm)


def remote(src, dst, send, recv, device):
    return pltpu.make_async_remote_copy(
        src_ref=src, dst_ref=dst, send_sem=send, recv_sem=recv, device_id=device, device_id_type=MESH
    )


def greet(devices):
    barrier = pltpu.get_barrier_semaphore()
    for device in devices:
        pl.semaphore_signal(barrier, inc=1, device_id=device, device_id_type=MESH)
    pl.semaphore_wait(barrier, len(devices))


def selector(core, x_first):
    at = lax.broadcasted_iota(jnp.int32, (128, 256), 0)
    row = lax.broadcasted_iota(jnp.int32, (128, 256), 1)
    high, low = at // 32, (at // 8) % 4
    x, z = (high, low) if x_first else (low, high)
    wanted = (z % 2) * 128 + core * 64 + (z // 2) * 32 + x * 8 + at % 8
    return jnp.where(row == wanted, 1.0, 0.0).astype(BF)


class Twin:
    def __init__(self, place, send, recv):
        self.place, self.send, self.recv = place, send, recv

    def copy(self, slot, ref, cols=None):
        cols = slice(None) if cols is None else cols
        return remote(
            ref.at[0:256, cols], ref.at[256:512, cols], self.send.at[slot], self.recv.at[slot], self.place.twin()
        )

    def copy_rows(self, slot, ref):
        return remote(ref.at[0:2], ref.at[2:4], self.send.at[slot], self.recv.at[slot], self.place.twin())


class Scatter:
    def __init__(self, place, block, second_block, bufs, send, recv):
        self.place, self.second_block = place, second_block
        self.block, (self.own, self.r1, self.relay, self.r2, self.s3, self.r3) = block, bufs
        self.send, self.recv = send, recv

    def first(self, stream, part):
        lo, hi, axes = STREAMS[stream]
        mid = (hi - lo) // 256 * 128
        half_a, half_b = slice(0, mid), slice(mid, hi - lo)
        all_a, all_b = slice(lo, lo + mid), slice(lo + mid, hi)
        slot, near, far = (
            (1, half_a, self.relay.at[:, all_a]),
            (1, half_b, self.relay.at[:, all_b]),
            (0, half_b, self.r1.at[0, :, all_b]),
            (2, half_a, self.r1.at[1, :, all_a]),
            (0, half_a, self.r1.at[0, :, all_a]),
            (2, half_b, self.r1.at[1, :, all_b]),
        )[part]
        return remote(
            self.block(stream, slot).at[:, near], far, self.send.at[stream, part], self.recv.at[stream, part],
            self.place.ring(axes[0], 3 if part % 2 else 1),
        )

    def copy(self, stream, phase, step):
        lo, hi, axes = STREAMS[stream]
        cols = slice(lo, hi)
        axis = axes[phase]
        to = (self.place.at(axis) + step) % 4
        slot = step - 1
        if phase == 1:
            src = self.second_block(stream).at[pl.ds(pl.multiple_of(to * 32, 32), 32), :]
            dst = self.r2.at[slot, :, cols]
        else:
            src, dst = self.s3.at[to, :, cols], self.r3.at[slot, :, cols]
        sem = 3 + 3 * phase + slot
        return remote(
            src, dst, self.send.at[stream, sem], self.recv.at[stream, sem], self.place.ring(axis, step)
        )

    def product(self, stream, ut, ut_mixed, gm, g, block):
        lo, hi, _ = STREAMS[stream]
        rows = pl.ds(pl.multiple_of(block * 128, 128), 128)
        if stream < 2:
            return [(lo, hi, matmul(ut[stream][rows, :], gm[:, lo:hi]))]
        return [
            (lo, 3072, matmul(ut[2][rows, :], gm[:, lo:3072])),
            (3072, 4096, matmul(ut_mixed[rows, :], g[...].reshape(512, D))),
        ]

    def start(self, stream, ut, ut_mixed, gm, g):
        first, _, axes = STREAMS[stream]
        at = self.place.at(axes[0])
        for step, parts in ((2, (0, 1)), (1, (2,)), (3, (3,))):
            for lo, hi, made in self.product(stream, ut, ut_mixed, gm, g, (at + step) % 4):
                self.block(stream, step - 1)[:, lo - first : hi - first] = made.astype(BF)
            for part in parts:
                self.first(stream, part).start()
        for lo, hi, made in self.product(stream, ut, ut_mixed, gm, g, at):
            self.own[:, lo:hi] = made

    def pass_on(self, stream):
        lo, hi, _ = STREAMS[stream]
        mid = (hi - lo) // 256 * 128
        for part, slot, left, right in ((0, 0, 0, mid), (1, 2, mid, hi - lo)):
            self.first(stream, part).wait_recv()
            block = self.block(stream, slot)
            came = self.relay[:, lo + left : lo + right].astype(F32)
            block[:, left:right] = (block[:, left:right].astype(F32) + came).astype(BF)
            self.first(stream, part + 4).start()

    def second(self, stream):
        lo, hi, _ = STREAMS[stream]
        for part in (2, 3, 4, 5):
            self.first(stream, part).wait_recv()

        def one(q, carry):
            rows = pl.ds(pl.multiple_of(q * 32, 32), 32)
            total = self.own[rows, lo:hi]
            for slot in range(2):
                total = total + self.r1[slot, rows, lo:hi].astype(F32)
            self.own[rows, lo:hi] = total
            self.second_block(stream)[rows, :] = total.astype(BF)
            return carry

        lax.fori_loop(0, 4, one, 0)
        for step in (1, 2, 3):
            self.copy(stream, 1, step).start()

    def third(self, stream):
        lo, hi, axes = STREAMS[stream]
        for step in (1, 2, 3):
            self.copy(stream, 1, step).wait_recv()
        total = self.own[pl.ds(pl.multiple_of(self.place.at(axes[1]) * 32, 32), 32), lo:hi]
        for slot in range(3):
            total = total + self.r2[slot, :, lo:hi].astype(F32)
        self.own[0:32, lo:hi] = total
        for q in range(4):
            self.s3[q, :, lo:hi] = total[q * 8 : q * 8 + 8].astype(BF)
        for step in (1, 2, 3):
            self.copy(stream, 2, step).start()

    def last(self, stream, qkv_ref, out_ref):
        lo, hi, axes = STREAMS[stream]
        for step in (1, 2, 3):
            self.copy(stream, 2, step).wait_recv()
        total = self.own[pl.ds(pl.multiple_of(self.place.at(axes[2]) * 8, 8), 8), lo:hi]
        for slot in range(3):
            total = total + self.r3[slot, :, lo:hi].astype(F32)
        top = min(hi, 3072)
        qkv_ref[:, lo:top] = total[:, : top - lo]
        if hi > 3072:
            out_ref[...] = total[:, 3072 - lo :]

    def drain(self):
        for stream in range(3):
            for part in range(6):
                self.first(stream, part).wait_send()
            for phase in (1, 2):
                for step in (1, 2, 3):
                    self.copy(stream, phase, step).wait_send()


def scatter_bufs():
    return [
        pltpu.VMEM((128, 4096), F32),
        pltpu.VMEM((2, 128, 4096), BF),
        pltpu.VMEM((128, 4096), BF),
        pltpu.VMEM((3, 32, 4096), BF),
        pltpu.VMEM((4, 8, 4096), BF),
        pltpu.VMEM((3, 8, 4096), BF),
    ]


def transposed(place, unit, mixed, ut, ut_mixed, spare):
    sel_x = selector(place.core, True)
    sel_z = selector(place.core, False)

    def last_order(part, y):
        for z in range(4):
            for x in range(4):
                at = (z % 2) * 128 + x * 32 + y * 8
                spare[at : at + 8, (z // 2) * 512 : (z // 2) * 512 + 512] = part[z * 32 + x * 8 : z * 32 + x * 8 + 8]

    for y in range(4):
        cols = slice(y * 256, y * 256 + 256)
        part = matmul(sel_x, unit[:, cols], NT).astype(BF)
        for x in range(4):
            ut[0][x * 128 + y * 32 : x * 128 + y * 32 + 32, :] = part[x * 32 : x * 32 + 32]
        part = matmul(sel_z, unit[:, cols], NT)
        ut[1][y * 128 : y * 128 + 128, :] = part.astype(BF)
        last_order(part, y)
    ut[2][0:256, :] = spare[:, 0:512].astype(BF)
    ut[2][256:512, :] = spare[:, 512:1024].astype(BF)
    for y in range(4):
        last_order(matmul(sel_z, mixed[:, y * 256 : y * 256 + 256], NT), y)
    ut_mixed[0:256, :] = spare[:, 0:512].astype(BF)
    ut_mixed[256:512, :] = spare[:, 512:1024].astype(BF)


def normal(x_ref):
    x = x_ref[...].reshape(256, D).astype(F32)
    inverse = lax.rsqrt(jnp.mean(x * x, axis=-1, keepdims=True) + epsilon)
    return x * inverse, inverse


def span(start, size):
    return pl.ds(pl.multiple_of(start * size, size), size)


def project(x_ref, unit, w, merged):
    unit[0:256, :] = normal(x_ref)[0].astype(BF)

    def one(n, carry):
        cols = span(n, 512)
        merged[:, cols] = matmul(unit[0:256, :], w[:, cols]).astype(BF)
        return carry

    lax.fori_loop(0, 6, one, 0)


def halves():
    lane = lax.broadcasted_iota(jnp.int32, (1, 128), 1)
    low = jnp.where(lane < HD, 1.0, 0.0)
    return low.astype(BF), (1.0 - low).astype(BF)


def pair_parts(merged, rows, pair):
    q = merged[rows, span(pair, 128)] * BF(HD**-0.5)
    k = merged[rows, pl.ds(pl.multiple_of(D + pair * 128, 128), 128)]
    v = merged[rows, pl.ds(pl.multiple_of(2 * D + pair * 128, 128), 128)]
    return q, k, v


def attend(merged, mixed, seqs, biases, group):
    def one(turn, carry):
        low_high = halves()
        jobs = []
        for rows, bias in zip(seqs, biases):
            for i in range(group):
                pair = turn * group + i
                q, k, v = pair_parts(merged, rows, pair)
                for half in low_high:
                    jobs.append((rows, pair, bias, q * half, k, v * half))
        scores = [matmul(q, k, NT) + bias[...] for _, _, bias, q, k, _ in jobs]
        probs = probs_of(scores)
        parts = [matmul(p.astype(BF), job[5]) for p, job in zip(probs, jobs)]
        for i in range(0, len(jobs), 2):
            rows, pair = jobs[i][:2]
            mixed[rows, span(pair, 128)] = (parts[i] + parts[i + 1]).astype(BF)
        return carry

    lax.fori_loop(0, H // 2 // group, one, 0)


def probs_of(scores):
    tops = [jnp.max(s, axis=-1, keepdims=True) for s in scores]
    shifted = [jnp.exp(s - t) for s, t in zip(scores, tops)]
    sums = [jnp.sum(s, axis=-1, keepdims=True) for s in shifted]
    return [s * (1.0 / t) for s, t in zip(shifted, sums)]


def attend_back(merged, gmix, mixed, gm, seqs, biases, group):
    def one(turn, carry):
        low_high = halves()
        jobs = []
        for rows, bias in zip(seqs, biases):
            for i in range(group):
                pair = turn * group + i
                q, k, v = pair_parts(merged, rows, pair)
                go = gmix[rows, span(pair, 128)]
                for half in low_high:
                    jobs.append((rows, pair, bias, q * half, k, v, go * half, half))
        scores = [matmul(job[3], job[4], NT) + job[2][...] for job in jobs]
        gps = [matmul(job[6], job[5], NT) for job in jobs]
        probs = probs_of(scores)
        means = [jnp.sum(gp * p, axis=-1, keepdims=True) for gp, p in zip(gps, probs)]
        gss = [(p * (gp - m)).astype(BF) for p, gp, m in zip(probs, gps, means)]
        rounded = [p.astype(BF) for p in probs]
        gq = [matmul(gs, job[4] * job[7]) for gs, job in zip(gss, jobs)]
        gk = [matmul(gs, job[3], TN) for gs, job in zip(gss, jobs)]
        gv = [matmul(p, job[6], TN) for p, job in zip(rounded, jobs)]
        if mixed is not None:
            mx = [matmul(p, job[5] * job[7]) for p, job in zip(rounded, jobs)]
        for i in range(0, len(jobs), 2):
            rows, pair = jobs[i][:2]
            gm[rows, span(pair, 128)] = ((gq[i] + gq[i + 1]) * HD**-0.5).astype(BF)
            gm[rows, pl.ds(pl.multiple_of(D + pair * 128, 128), 128)] = (gk[i] + gk[i + 1]).astype(BF)
            gm[rows, pl.ds(pl.multiple_of(2 * D + pair * 128, 128), 128)] = (gv[i] + gv[i + 1]).astype(BF)
            if mixed is not None:
                mixed[rows, span(pair, 128)] = (mx[i] + mx[i + 1]).astype(BF)
        return carry

    lax.fori_loop(0, H // 2 // group, one, 0)


def add_residual(x_ref, mixed, w, out_ref, shape):
    for n in range(2):
        cols = slice(n * 512, n * 512 + 512)
        x = x_ref[..., cols].reshape(256, 512).astype(F32)
        out = x + matmul(mixed[0:256, :], w[:, cols])
        out_ref[..., cols] = out.astype(BF).reshape(shape + (512,))


def grad_of_mixed(g, w, gmix):
    def one(n, carry):
        rows = span(n, 256)
        gmix[:, rows] = matmul(g[...].reshape(256, D), w[rows, :], NT).astype(BF)
        return carry

    lax.fori_loop(0, 4, one, 0)


def grad_of_input(x_ref, g, gm, w, gu, out_ref, shape):
    def one(n, carry):
        rows = span(n, 256)
        gu[:, rows] = matmul(gm[0:256, :], w[rows, :], NT)
        return carry

    lax.fori_loop(0, 4, one, 0)
    normed, inverse = normal(x_ref)
    grad_unit = gu[...]
    rows = inverse * (grad_unit - normed * jnp.mean(grad_unit * normed, axis=-1, keepdims=True))
    out_ref[...] = (g[...].reshape(256, D).astype(F32) + rows).astype(BF).reshape(shape + (D,))


def swap_rows(src, dst):
    at = lax.broadcasted_iota(jnp.int32, (256, 256), 0)
    row = lax.broadcasted_iota(jnp.int32, (256, 256), 1)
    swap = jnp.where(row == (at % 16) * 16 + at // 16, 1.0, 0.0).astype(BF)
    for n in range(2):
        cols = slice(n * 512, n * 512 + 512)
        out = matmul(swap, src[..., cols].reshape(256, 512)).astype(BF)
        dst[..., cols] = out.reshape(dst.shape[:-1] + (512,))


class Swap:
    def __init__(self, place, axis, send, recv, source, target):
        self.place, self.axis, self.send, self.recv = place, axis, send, recv
        self.source, self.target = source, target
        self.size = 8 if axis == "tm" else 16
        self.me = place.tm if axis == "tm" else place.ag

    def copy(self, step):
        to = (self.me + step) % self.size
        device = (self.place.ag, to) if self.axis == "tm" else (to, self.place.tm)
        return remote(self.source(to), self.target(self.me), self.send.at[step], self.recv.at[step], device)

    def local(self):
        return pltpu.make_async_copy(self.source(self.me), self.target(self.me), self.recv.at[0])

    def start(self):
        def one(step, carry):
            self.copy(step).start()
            return carry

        lax.fori_loop(1, self.size, one, 0)
        self.local().start()

    def wait(self):
        def one(step, carry):
            self.copy(step).wait_recv()
            return carry

        lax.fori_loop(1, self.size, one, 0)
        self.local().wait()

    def drain(self):
        def one(step, carry):
            self.copy(step).wait_send()
            return carry

        lax.fori_loop(1, self.size, one, 0)


def spread_index():
    at = lax.broadcasted_iota(jnp.int32, (256, 256), 0)
    row = lax.broadcasted_iota(jnp.int32, (256, 256), 1)
    return at, row


def one_hot(wanted, row):
    return jnp.where(row == wanted, 1.0, 0.0).astype(BF)


def pack_time(src, dst):
    at, row = spread_index()
    i, c, a = at // 16, (at // 2) % 8, at % 2
    turn = one_hot(c * 32 + a * 16 + i, row)

    def one(n, carry):
        rows = span(n, 16)
        parts = [src[a, rows, c * 128 : c * 128 + 128] for c in range(8) for a in range(2)]
        out = matmul(turn, jnp.concatenate(parts, axis=0)).astype(BF)
        dst[rows] = out.reshape(16, 16, 128)
        return carry

    lax.fori_loop(0, 8, one, 0)


def unpack_time(src, dst):
    at, row = spread_index()
    c, a, i = at // 32, (at // 16) % 2, at % 16
    turn = one_hot(i * 16 + c * 2 + a, row)

    def one(n, carry):
        rows = span(n, 16)
        out = matmul(turn, src[rows].reshape(256, 128)).astype(BF)
        for c in range(8):
            for a in range(2):
                part = out[c * 32 + a * 16 : c * 32 + a * 16 + 16]
                dst[a, rows, c * 128 : c * 128 + 128] = part
        return carry

    lax.fori_loop(0, 8, one, 0)


def pack_agent(src, dst):
    at, row = spread_index()
    i, c, a = at // 16, (at // 2) % 8, at % 2
    turn = one_hot(c * 32 + i * 2 + a, row)

    def one(n, carry):
        parts = [src[span(n, 32), c * 128 : c * 128 + 128] for c in range(8)]
        out = matmul(turn, jnp.concatenate(parts, axis=0)).astype(BF)
        dst[span(n, 16)] = out.reshape(16, 16, 128)
        return carry

    lax.fori_loop(0, 8, one, 0)


def unpack_agent(src, dst):
    at, row = spread_index()
    c, i, a = at // 32, (at // 2) % 16, at % 2
    turn = one_hot(i * 16 + c * 2 + a, row)

    def one(n, carry):
        out = matmul(turn, src[span(n, 16)].reshape(256, 128)).astype(BF)
        for c in range(8):
            dst[span(n, 32), c * 128 : c * 128 + 128] = out[c * 32 : c * 32 + 32]
        return carry

    lax.fori_loop(0, 8, one, 0)


class Spread:
    def __init__(self, place, send, recv, src, dst, to_steps):
        self.place, self.send, self.recv, self.src, self.dst, self.to_steps = place, send, recv, src, dst, to_steps

    def places(self, ag, tm):
        return ag * 8 + tm, tm * 16 + ag

    def start(self):
        place = self.place
        agents, steps = self.places(place.ag, place.tm)
        mine = agents if self.to_steps else steps

        def one(step, carry):
            ag, tm = (place.ag + step // 8) % 16, (place.tm + step % 8) % 8
            by_agents, by_steps = self.places(ag, tm)
            theirs = by_steps if self.to_steps else by_agents
            remote(self.src.at[theirs], self.dst.at[mine], self.send, self.recv, (ag, tm)).start()
            return carry

        lax.fori_loop(1, 128, one, 0)
        own = steps if self.to_steps else agents
        pltpu.make_async_copy(self.src.at[own], self.dst.at[mine], self.recv).start()

    def wait(self):
        pltpu.make_async_copy(self.src, self.dst, self.recv).wait()

    def drain(self):
        pltpu.make_async_copy(self.src.at[0:127], self.dst.at[0:127], self.send).wait()


def block_kernel(
    tokens, cotangent, observed, time_qkv, time_out, agent_qkv, agent_out,
    grad_tokens, tq_ref, to_ref, aq_ref, ao_ref,
    w_tq, w_to, w_aq, w_ao,
    x_time, made, turned, x_agent, cot, tiles_out, first_in, back_in,
    merged_t, merged_a, gmix, gu, bias_t, bias_a,
    units, gms, mixeds, g_time, g_agent,
    *rest,
):
    grad_a = rest[0]
    bufs = (rest[1:7], rest[7:13])
    load, spread_send, spread_recv, swap_send, swap_recv, twin_send, twin_recv, sc_send, sc_recv = rest[13:]
    place = Place()
    loads = [
        pltpu.make_async_copy(src, dst, load.at[i])
        for i, (src, dst) in enumerate(
            (
                (cotangent, cot),
                (time_qkv, w_tq),
                (time_out, w_to),
                (agent_out, w_ao),
                (agent_qkv, w_aq),
            )
        )
    ]
    for copy in loads:
        copy.start()
    far = [
        (place.y * 4 + (1 - place.zlo) * 2 + place.core, (1 - place.zhi) * 4 + place.x),
    ]
    greet(
        [((place.ag + step) % 16, place.tm) for step in range(1, 16)]
        + [(place.ag, (place.tm + step) % 8) for step in range(1, 8)]
        + far
    )

    def swap(slot, axis, source, target):
        return Swap(place, axis, swap_send.at[slot], swap_recv.at[slot], source, target)

    def two(ref):
        return lambda i: ref.at[pl.ds(i * 2, 2)]

    def sixteen(ref):
        return lambda i: ref.at[0:2, span(i, 16), :]

    def rows16(ref):
        return lambda i: ref.at[span(i, 16), :]

    tokens_in = swap(0, "tm", two(tokens), sixteen(x_time))
    cot_in = swap(1, "ag", rows16(turned), rows16(g_agent))
    first = Spread(place, spread_send.at[0], spread_recv.at[0], tiles_out, first_in, True)
    back = Spread(place, spread_send.at[1], spread_recv.at[1], tiles_out, back_in, False)
    tokens_out = swap(2, "tm", sixteen(made), two(grad_tokens))
    twins = [Twin(place, twin_send.at[s], twin_recv.at[s]) for s in range(2)]

    def block_a(stream, slot):
        lo, hi, _ = STREAMS[stream]
        return grad_a.at[slot, :, lo:hi]

    def block_t(stream, slot):
        lo, hi, _ = STREAMS[stream]
        if stream < 2:
            return w_aq.at[span(slot, 128), lo:hi]
        return w_aq.at[span(slot + 4, 128), 0 : hi - lo]

    def second_a(stream):
        lo, hi, _ = STREAMS[stream]
        return w_aq.at[512 + stream * 128 : 640 + stream * 128, 1408 : 1408 + hi - lo]

    def second_t(stream):
        lo, hi, _ = STREAMS[stream]
        if stream < 2:
            return w_aq.at[384:512, lo:hi]
        return w_aq.at[896:1024, 0 : hi - lo]

    blocks, seconds = (block_a, block_t), (second_a, second_t)
    scatters = [Scatter(place, blocks[s], seconds[s], bufs[s], sc_send.at[s], sc_recv.at[s]) for s in range(2)]
    unit_a, unit_t = units.at[0], units.at[1]
    gm_a, gm_t = gms.at[0], gms.at[1]
    mixed_a, mixed_t = mixeds.at[0], mixeds.at[1]
    ut = [w_ao.at[0:512, 0:512], w_ao.at[0:512, 512:1024], w_ao.at[512:1024, 0:512]]
    ut_mixed = w_ao.at[512:1024, 512:1024]
    seqs = [slice(0, 128), slice(128, 256)]
    biases_t = [bias_t.at[0], bias_t.at[1]]

    with jax.named_scope("tokens_to_agents"):
        tokens_in.start()
        loads[0].wait()
        swap_rows(cot, turned)
        self_t = lax.broadcasted_iota(jnp.int32, (128, 128), 0) == lax.broadcasted_iota(jnp.int32, (128, 128), 1)
        for a in range(2):
            row = observed[pl.ds(place.ag * 16 + place.tm * 2 + a, 1), :]
            bias_t[a] = jnp.where((row > 0) | self_t, 0.0, masked_score)
        at_step = lax.broadcasted_iota(jnp.int32, (8, STEPS), 1) == place.tm * 16 + place.ag
        seen = matmul(jnp.where(at_step, 1.0, 0.0).astype(BF), observed[...].astype(F32).astype(BF), NT)
        self_a = lax.broadcasted_iota(jnp.int32, (256, 256), 0) == lax.broadcasted_iota(jnp.int32, (256, 256), 1)
        bias_a[...] = jnp.where((seen[0:1, :] > 0.5) | self_a, 0.0, masked_score)
        loads[1].wait()
        tokens_in.wait()
        cot_in.start()
    with jax.named_scope("time_forward"):
        project(x_time, unit_t, w_tq, merged_t)
        twins[1].copy(0, unit_t).start()
        attend(merged_t, mixed_t, seqs, biases_t, 4)
        twins[1].copy(2, mixed_t).start()
        loads[2].wait()
        add_residual(x_time, mixed_t, w_to, made, (2, 128))
        pack_time(made, tiles_out)
        first.start()
    with jax.named_scope("first_to_steps"):
        cot_in.wait()
        twins[0].copy(3, g_agent).start()
        loads[3].wait()
        grad_of_mixed(g_agent.at[0:256, :], w_ao, gmix)
        cot_in.drain()
        loads[4].wait()
        first.wait()
        unpack_agent(first_in, x_agent)
    with jax.named_scope("agent_backward"):
        project(x_agent, unit_a, w_aq, merged_a)
        twins[0].copy(0, unit_a).start()
        attend_back(merged_a, gmix, mixed_a, gm_a, [slice(0, 256)], [bias_a], 2)
        twins[0].copy(2, mixed_a).start()
        twins[0].copy(1, gm_a).start()
        grad_of_input(x_agent, g_agent.at[0:256, :], gm_a, w_aq, gu, cot, (256,))
        first.drain()
        pack_agent(cot, tiles_out)
        back.start()
    with jax.named_scope("agent_weights"):
        for slot, ref in enumerate((unit_a, gm_a, mixed_a, g_agent)):
            twins[0].copy(slot, ref).wait_recv()
        transposed(place, unit_a, mixed_a, ut, ut_mixed, gu)
        for stream in range(3):
            scatters[0].start(stream, ut, ut_mixed, gm_a, g_agent)
    with jax.named_scope("grad_first_to_agents"):
        back.wait()
        unpack_time(back_in, g_time)
        twins[1].copy_rows(3, g_time).start()
    with jax.named_scope("time_backward"):
        g_own = g_time.at[0:2]
        grad_of_mixed(g_own, w_to, gmix)
        attend_back(merged_t, gmix, None, gm_t, seqs, biases_t, 4)
        twins[1].copy(1, gm_t).start()
        for stream in range(3):
            scatters[0].pass_on(stream)
        grad_of_input(x_time, g_own, gm_t, w_tq, gu, made, (2, 128))
        tokens_out.start()
        for stream in range(3):
            scatters[0].second(stream)
    with jax.named_scope("time_weights"):
        for slot, ref in enumerate((unit_t, gm_t, mixed_t)):
            twins[1].copy(slot, ref).wait_recv()
        twins[1].copy_rows(3, g_time).wait_recv()
        transposed(place, unit_t, mixed_t, ut, ut_mixed, gu)
        for stream in range(3):
            scatters[1].start(stream, ut, ut_mixed, gm_t, g_time)
    with jax.named_scope("rings"):
        outs = ((aq_ref, ao_ref), (tq_ref, to_ref))
        for stream in range(3):
            scatters[0].third(stream)
        for stream in range(3):
            scatters[1].pass_on(stream)
        for stream in range(3):
            scatters[1].second(stream)
        for stream in range(3):
            scatters[0].last(stream, *outs[0])
        for stream in range(3):
            scatters[1].third(stream)
        for stream in range(3):
            scatters[1].last(stream, *outs[1])
        tokens_out.wait()
    with jax.named_scope("drain"):
        for s in range(2):
            scatters[s].drain()
        for slot, ref in enumerate((unit_a, gm_a, mixed_a, g_agent)):
            twins[0].copy(slot, ref).wait_send()
        for slot, ref in enumerate((unit_t, gm_t, mixed_t)):
            twins[1].copy(slot, ref).wait_send()
        twins[1].copy_rows(3, g_time).wait_send()
        for moved in (tokens_in, back, tokens_out):
            moved.drain()


def hand_on(*refs):
    for source, target in zip(refs[:5], refs[5:]):
        target[...] = source[...]


def local(tokens, cotangent, observed, time_qkv, time_out, agent_qkv, agent_out):
    shape = jax.ShapeDtypeStruct
    grad_tokens, *grads = pl.pallas_call(
        block_kernel,
        out_shape=[
            shape((16, 16, D), BF),
            shape((8, 3 * D), F32),
            shape((8, D), F32),
            shape((8, 3 * D), F32),
            shape((8, D), F32),
        ],
        in_specs=[
            pl.BlockSpec(memory_space=pl.ANY),
            pl.BlockSpec(memory_space=pl.ANY),
            pl.BlockSpec(memory_space=pltpu.VMEM),
        ]
        + [pl.BlockSpec(memory_space=pl.ANY)] * 4,
        out_specs=[pl.BlockSpec(memory_space=pl.ANY)] + [pl.BlockSpec(memory_space=pltpu.VMEM)] * 4,
        scratch_shapes=[
            pltpu.VMEM((D, 3 * D), BF),
            pltpu.VMEM((D, D), BF),
            pltpu.VMEM((D, 3 * D), BF),
            pltpu.VMEM((D, D), BF),
            pltpu.VMEM((2, 128, D), BF),
            pltpu.VMEM((2, 128, D), BF),
            pltpu.VMEM((256, D), BF),
            pltpu.VMEM((256, D), BF),
            pltpu.VMEM((256, D), BF),
            pltpu.VMEM((128, 16, 128), BF),
            pltpu.VMEM((128, 16, 128), BF),
            pltpu.VMEM((128, 16, 128), BF),
            pltpu.VMEM((256, 3 * D), BF),
            pltpu.VMEM((256, 3 * D), BF),
            pltpu.VMEM((256, D), BF),
            pltpu.VMEM((256, D), F32),
            pltpu.VMEM((2, 128, 128), F32),
            pltpu.VMEM((256, 256), F32),
            pltpu.VMEM((2, 512, D), BF),
            pltpu.VMEM((2, 512, 3 * D), BF),
            pltpu.VMEM((2, 512, D), BF),
            pltpu.VMEM((4, 128, D), BF),
            pltpu.VMEM((512, D), BF),
        ]
        + [pltpu.VMEM((3, 128, 4096), BF)]
        + scatter_bufs()
        + scatter_bufs()
        + [
            pltpu.SemaphoreType.DMA((5,)),
            pltpu.SemaphoreType.DMA((2,)),
            pltpu.SemaphoreType.DMA((2,)),
            pltpu.SemaphoreType.DMA((3, 16)),
            pltpu.SemaphoreType.DMA((3, 16)),
            pltpu.SemaphoreType.DMA((2, 4)),
            pltpu.SemaphoreType.DMA((2, 4)),
            pltpu.SemaphoreType.DMA((2, 3, 12)),
            pltpu.SemaphoreType.DMA((2, 3, 12)),
        ],
        compiler_params=pltpu.CompilerParams(
            collective_id=0, has_side_effects=True, vmem_limit_bytes=61 * 1024 * 1024
        ),
    )(
        tokens.reshape(16, 16, D),
        cotangent.reshape(256, D),
        observed.reshape(256, STEPS),
        time_qkv,
        time_out,
        agent_qkv,
        agent_out,
    )
    made = [grad_tokens, *grads]
    grad_tokens, *grads = pl.pallas_call(
        hand_on,
        out_shape=[shape(x.shape, x.dtype) for x in made],
        in_specs=[pl.BlockSpec(memory_space=pltpu.VMEM)] * 5,
        out_specs=[pl.BlockSpec(memory_space=pltpu.VMEM)] * 5,
    )(*made)
    return (grad_tokens.reshape(1, 16, 16, D), *grads)


def solution(mesh):
    in_specs = (P(None, "ag", "tm", None), P(None, "ag", "tm", None), P(), P(), P(), P(), P())
    out_specs = (
        P(None, "ag", "tm", None),
        P(("ag", "tm"), None),
        P(("ag", "tm"), None),
        P(("ag", "tm"), None),
        P(("ag", "tm"), None),
    )
    return jax.shard_map(local, mesh=mesh, in_specs=in_specs, out_specs=out_specs, check_vma=False)
```

```python
import functools

import jax
import jax.numpy as jnp
from jax import lax
from jax.experimental import pallas as pl
from jax.experimental.pallas import tpu as pltpu
from jax.sharding import PartitionSpec as P

D = 1024
H = 16
HD = 64
STEPS = 128
epsilon = 1e-06
masked_score = -1e30

MESH = pl.DeviceIdType.MESH
BF = jnp.bfloat16
F32 = jnp.float32
NT = (((1,), (1,)), ((), ()))
TN = (((0,), (0,)), ((), ()))

STREAMS = ((0, 1408, "xyz"), (1408, 2816, "yzx"), (2816, 4096, "zxy"))


def matmul(left, right, dims=(((1,), (0,)), ((), ()))):
    return lax.dot_general(left, right, dims, preferred_element_type=F32)


class Place:
    def __init__(self):
        self.ag = lax.axis_index("ag")
        self.tm = lax.axis_index("tm")
        self.y = self.ag // 4
        self.zlo = (self.ag // 2) % 2
        self.core = self.ag % 2
        self.zhi = self.tm // 4
        self.x = self.tm % 4
        self.z = self.zhi * 2 + self.zlo

    def at(self, axis):
        return {"x": self.x, "y": self.y, "z": self.z}[axis]

    def ring(self, axis, step):
        if axis == "x":
            return (self.ag, self.zhi * 4 + (self.x + step) % 4)
        if axis == "y":
            return (((self.y + step) % 4) * 4 + self.ag % 4, self.tm)
        z = (self.z + step) % 4
        return (self.y * 4 + (z % 2) * 2 + self.core, (z // 2) * 4 + self.x)

    def twin(self):
        return (self.ag + 1 - 2 * self.core, self.tm)


def remote(src, dst, send, recv, device):
    return pltpu.make_async_remote_copy(
        src_ref=src, dst_ref=dst, send_sem=send, recv_sem=recv, device_id=device, device_id_type=MESH
    )


def greet(devices):
    barrier = pltpu.get_barrier_semaphore()
    for device in devices:
        pl.semaphore_signal(barrier, inc=1, device_id=device, device_id_type=MESH)
    pl.semaphore_wait(barrier, len(devices))


def selector(core, x_first):
    at = lax.broadcasted_iota(jnp.int32, (128, 256), 0)
    row = lax.broadcasted_iota(jnp.int32, (128, 256), 1)
    high, low = at // 32, (at // 8) % 4
    x, z = (high, low) if x_first else (low, high)
    wanted = (z % 2) * 128 + core * 64 + (z // 2) * 32 + x * 8 + at % 8
    return jnp.where(row == wanted, 1.0, 0.0).astype(BF)


class Twin:
    def __init__(self, place, send, recv):
        self.place, self.send, self.recv = place, send, recv

    def copy(self, slot, ref, cols=None):
        cols = slice(None) if cols is None else cols
        return remote(
            ref.at[0:256, cols], ref.at[256:512, cols], self.send.at[slot], self.recv.at[slot], self.place.twin()
        )

    def copy_rows(self, slot, ref):
        return remote(ref.at[0:2], ref.at[2:4], self.send.at[slot], self.recv.at[slot], self.place.twin())


class Scatter:
    def __init__(self, place, block, second_block, bufs, send, recv):
        self.place, self.second_block = place, second_block
        self.block, (self.own, self.r1, self.relay, self.r2, self.s3, self.r3) = block, bufs
        self.send, self.recv = send, recv

    def first(self, stream, part):
        lo, hi, axes = STREAMS[stream]
        mid = (hi - lo) // 256 * 128
        half_a, half_b = slice(0, mid), slice(mid, hi - lo)
        all_a, all_b = slice(lo, lo + mid), slice(lo + mid, hi)
        slot, near, far = (
            (1, half_a, self.relay.at[:, all_a]),
            (1, half_b, self.relay.at[:, all_b]),
            (0, half_b, self.r1.at[0, :, all_b]),
            (2, half_a, self.r1.at[1, :, all_a]),
            (0, half_a, self.r1.at[0, :, all_a]),
            (2, half_b, self.r1.at[1, :, all_b]),
        )[part]
        return remote(
            self.block(stream, slot).at[:, near], far, self.send.at[stream, part], self.recv.at[stream, part],
            self.place.ring(axes[0], 3 if part % 2 else 1),
        )

    def copy(self, stream, phase, step):
        lo, hi, axes = STREAMS[stream]
        cols = slice(lo, hi)
        axis = axes[phase]
        to = (self.place.at(axis) + step) % 4
        slot = step - 1
        if phase == 1:
            src = self.second_block(stream).at[pl.ds(pl.multiple_of(to * 32, 32), 32), :]
            dst = self.r2.at[slot, :, cols]
        else:
            src, dst = self.s3.at[to, :, cols], self.r3.at[slot, :, cols]
        sem = 3 + 3 * phase + slot
        return remote(
            src, dst, self.send.at[stream, sem], self.recv.at[stream, sem], self.place.ring(axis, step)
        )

    def product(self, stream, ut, ut_mixed, gm, g, block):
        lo, hi, _ = STREAMS[stream]
        rows = pl.ds(pl.multiple_of(block * 128, 128), 128)
        if stream < 2:
            return [(lo, hi, matmul(ut[stream][rows, :], gm[:, lo:hi]))]
        return [
            (lo, 3072, matmul(ut[2][rows, :], gm[:, lo:3072])),
            (3072, 4096, matmul(ut_mixed[rows, :], g[...].reshape(512, D))),
        ]

    def start(self, stream, ut, ut_mixed, gm, g):
        first, _, axes = STREAMS[stream]
        at = self.place.at(axes[0])
        for step, parts in ((2, (0, 1)), (1, (2,)), (3, (3,))):
            for lo, hi, made in self.product(stream, ut, ut_mixed, gm, g, (at + step) % 4):
                self.block(stream, step - 1)[:, lo - first : hi - first] = made.astype(BF)
            for part in parts:
                self.first(stream, part).start()
        for lo, hi, made in self.product(stream, ut, ut_mixed, gm, g, at):
            self.own[:, lo:hi] = made

    def pass_on(self, stream):
        lo, hi, _ = STREAMS[stream]
        mid = (hi - lo) // 256 * 128
        for part, slot, left, right in ((0, 0, 0, mid), (1, 2, mid, hi - lo)):
            self.first(stream, part).wait_recv()
            block = self.block(stream, slot)
            came = self.relay[:, lo + left : lo + right].astype(F32)
            block[:, left:right] = (block[:, left:right].astype(F32) + came).astype(BF)
            self.first(stream, part + 4).start()

    def second(self, stream):
        lo, hi, _ = STREAMS[stream]
        for part in (2, 3, 4, 5):
            self.first(stream, part).wait_recv()

        def one(q, carry):
            rows = pl.ds(pl.multiple_of(q * 32, 32), 32)
            total = self.own[rows, lo:hi]
            for slot in range(2):
                total = total + self.r1[slot, rows, lo:hi].astype(F32)
            self.own[rows, lo:hi] = total
            self.second_block(stream)[rows, :] = total.astype(BF)
            return carry

        lax.fori_loop(0, 4, one, 0)
        for step in (1, 2, 3):
            self.copy(stream, 1, step).start()

    def third(self, stream):
        lo, hi, axes = STREAMS[stream]
        for step in (1, 2, 3):
            self.copy(stream, 1, step).wait_recv()
        total = self.own[pl.ds(pl.multiple_of(self.place.at(axes[1]) * 32, 32), 32), lo:hi]
        for slot in range(3):
            total = total + self.r2[slot, :, lo:hi].astype(F32)
        self.own[0:32, lo:hi] = total
        for q in range(4):
            self.s3[q, :, lo:hi] = total[q * 8 : q * 8 + 8].astype(BF)
        for step in (1, 2, 3):
            self.copy(stream, 2, step).start()

    def last(self, stream, qkv_ref, out_ref):
        lo, hi, axes = STREAMS[stream]
        for step in (1, 2, 3):
            self.copy(stream, 2, step).wait_recv()
        total = self.own[pl.ds(pl.multiple_of(self.place.at(axes[2]) * 8, 8), 8), lo:hi]
        for slot in range(3):
            total = total + self.r3[slot, :, lo:hi].astype(F32)
        top = min(hi, 3072)
        qkv_ref[:, lo:top] = total[:, : top - lo]
        if hi > 3072:
            out_ref[...] = total[:, 3072 - lo :]

    def drain(self):
        for stream in range(3):
            for part in range(6):
                self.first(stream, part).wait_send()
            for phase in (1, 2):
                for step in (1, 2, 3):
                    self.copy(stream, phase, step).wait_send()


def scatter_bufs():
    return [
        pltpu.VMEM((128, 4096), F32),
        pltpu.VMEM((2, 128, 4096), BF),
        pltpu.VMEM((128, 4096), BF),
        pltpu.VMEM((3, 32, 4096), BF),
        pltpu.VMEM((4, 8, 4096), BF),
        pltpu.VMEM((3, 8, 4096), BF),
    ]


def transposed(place, unit, mixed, ut, ut_mixed, spare):
    sel_x = selector(place.core, True)
    sel_z = selector(place.core, False)

    def last_order(part, y):
        for z in range(4):
            for x in range(4):
                at = (z % 2) * 128 + x * 32 + y * 8
                spare[at : at + 8, (z // 2) * 512 : (z // 2) * 512 + 512] = part[z * 32 + x * 8 : z * 32 + x * 8 + 8]

    for y in range(4):
        cols = slice(y * 256, y * 256 + 256)
        part = matmul(sel_x, unit[:, cols], NT).astype(BF)
        for x in range(4):
            ut[0][x * 128 + y * 32 : x * 128 + y * 32 + 32, :] = part[x * 32 : x * 32 + 32]
        part = matmul(sel_z, unit[:, cols], NT)
        ut[1][y * 128 : y * 128 + 128, :] = part.astype(BF)
        last_order(part, y)
    ut[2][0:256, :] = spare[:, 0:512].astype(BF)
    ut[2][256:512, :] = spare[:, 512:1024].astype(BF)
    for y in range(4):
        last_order(matmul(sel_z, mixed[:, y * 256 : y * 256 + 256], NT), y)
    ut_mixed[0:256, :] = spare[:, 0:512].astype(BF)
    ut_mixed[256:512, :] = spare[:, 512:1024].astype(BF)


def normal(x_ref):
    x = x_ref[...].reshape(256, D).astype(F32)
    inverse = lax.rsqrt(jnp.mean(x * x, axis=-1, keepdims=True) + epsilon)
    return x * inverse, inverse


def span(start, size):
    return pl.ds(pl.multiple_of(start * size, size), size)


def project(x_ref, unit, w, merged):
    unit[0:256, :] = normal(x_ref)[0].astype(BF)

    def one(n, carry):
        cols = span(n, 512)
        merged[:, cols] = matmul(unit[0:256, :], w[:, cols]).astype(BF)
        return carry

    lax.fori_loop(0, 6, one, 0, unroll=6)


def halves():
    lane = lax.broadcasted_iota(jnp.int32, (1, 128), 1)
    low = jnp.where(lane < HD, 1.0, 0.0)
    return low.astype(BF), (1.0 - low).astype(BF)


def pair_parts(merged, rows, pair):
    q = merged[rows, span(pair, 128)] * BF(HD**-0.5)
    k = merged[rows, pl.ds(pl.multiple_of(D + pair * 128, 128), 128)]
    v = merged[rows, pl.ds(pl.multiple_of(2 * D + pair * 128, 128), 128)]
    return q, k, v


def attend(merged, mixed, seqs, biases, group):
    def one(turn, carry):
        low_high = halves()
        jobs = []
        for rows, bias in zip(seqs, biases):
            for i in range(group):
                pair = turn * group + i
                q, k, v = pair_parts(merged, rows, pair)
                for half in low_high:
                    jobs.append((rows, pair, bias, q * half, k, v * half))
        scores = [matmul(q, k, NT) + bias[...] for _, _, bias, q, k, _ in jobs]
        probs = probs_of(scores)
        parts = [matmul(p.astype(BF), job[5]) for p, job in zip(probs, jobs)]
        for i in range(0, len(jobs), 2):
            rows, pair = jobs[i][:2]
            mixed[rows, span(pair, 128)] = (parts[i] + parts[i + 1]).astype(BF)
        return carry

    lax.fori_loop(0, H // 2 // group, one, 0)


def probs_of(scores):
    tops = [jnp.max(s, axis=-1, keepdims=True) for s in scores]
    shifted = [jnp.exp(s - t) for s, t in zip(scores, tops)]
    sums = [jnp.sum(s, axis=-1, keepdims=True) for s in shifted]
    return [s * (1.0 / t) for s, t in zip(shifted, sums)]


def attend_back(merged, gmix, mixed, gm, seqs, biases, group):
    def one(turn, carry):
        low_high = halves()
        jobs = []
        for rows, bias in zip(seqs, biases):
            for i in range(group):
                pair = turn * group + i
                q, k, v = pair_parts(merged, rows, pair)
                go = gmix[rows, span(pair, 128)]
                for half in low_high:
                    jobs.append((rows, pair, bias, q * half, k, v, go * half, half))
        scores = [matmul(job[3], job[4], NT) + job[2][...] for job in jobs]
        gps = [matmul(job[6], job[5], NT) for job in jobs]
        probs = probs_of(scores)
        means = [jnp.sum(gp * p, axis=-1, keepdims=True) for gp, p in zip(gps, probs)]
        gss = [(p * (gp - m)).astype(BF) for p, gp, m in zip(probs, gps, means)]
        rounded = [p.astype(BF) for p in probs]
        gq = [matmul(gs, job[4] * job[7]) for gs, job in zip(gss, jobs)]
        gk = [matmul(gs, job[3], TN) for gs, job in zip(gss, jobs)]
        gv = [matmul(p, job[6], TN) for p, job in zip(rounded, jobs)]
        if mixed is not None:
            mx = [matmul(p, job[5] * job[7]) for p, job in zip(rounded, jobs)]
        for i in range(0, len(jobs), 2):
            rows, pair = jobs[i][:2]
            gm[rows, span(pair, 128)] = ((gq[i] + gq[i + 1]) * HD**-0.5).astype(BF)
            gm[rows, pl.ds(pl.multiple_of(D + pair * 128, 128), 128)] = (gk[i] + gk[i + 1]).astype(BF)
            gm[rows, pl.ds(pl.multiple_of(2 * D + pair * 128, 128), 128)] = (gv[i] + gv[i + 1]).astype(BF)
            if mixed is not None:
                mixed[rows, span(pair, 128)] = (mx[i] + mx[i + 1]).astype(BF)
        return carry

    lax.fori_loop(0, H // 2 // group, one, 0)


def add_residual(x_ref, mixed, w, out_ref, shape):
    for n in range(2):
        cols = slice(n * 512, n * 512 + 512)
        x = x_ref[..., cols].reshape(256, 512).astype(F32)
        out = x + matmul(mixed[0:256, :], w[:, cols])
        out_ref[..., cols] = out.astype(BF).reshape(shape + (512,))


def grad_of_mixed(g, w, gmix):
    def one(n, carry):
        rows = span(n, 256)
        gmix[:, rows] = matmul(g[...].reshape(256, D), w[rows, :], NT).astype(BF)
        return carry

    lax.fori_loop(0, 4, one, 0, unroll=4)


def grad_of_input(x_ref, g, gm, w, gu, out_ref, shape):
    def one(n, carry):
        rows = span(n, 512)
        gu[:, rows] = matmul(gm[0:256, :], w[rows, :], NT)
        return carry

    lax.fori_loop(0, 2, one, 0, unroll=2)
    normed, inverse = normal(x_ref)
    grad_unit = gu[...]
    rows = inverse * (grad_unit - normed * jnp.mean(grad_unit * normed, axis=-1, keepdims=True))
    out_ref[...] = (g[...].reshape(256, D).astype(F32) + rows).astype(BF).reshape(shape + (D,))


def swap_rows(src, dst):
    at = lax.broadcasted_iota(jnp.int32, (256, 256), 0)
    row = lax.broadcasted_iota(jnp.int32, (256, 256), 1)
    swap = jnp.where(row == (at % 16) * 16 + at // 16, 1.0, 0.0).astype(BF)
    for n in range(2):
        cols = slice(n * 512, n * 512 + 512)
        out = matmul(swap, src[..., cols].reshape(256, 512)).astype(BF)
        dst[..., cols] = out.reshape(dst.shape[:-1] + (512,))


class Swap:
    def __init__(self, place, axis, send, recv, source, target):
        self.place, self.axis, self.send, self.recv = place, axis, send, recv
        self.source, self.target = source, target
        self.size = 8 if axis == "tm" else 16
        self.me = place.tm if axis == "tm" else place.ag

    def copy(self, step):
        to = (self.me + step) % self.size
        device = (self.place.ag, to) if self.axis == "tm" else (to, self.place.tm)
        return remote(self.source(to), self.target(self.me), self.send.at[step], self.recv.at[step], device)

    def local(self):
        return pltpu.make_async_copy(self.source(self.me), self.target(self.me), self.recv.at[0])

    def start(self):
        def one(step, carry):
            self.copy(step).start()
            return carry

        lax.fori_loop(1, self.size, one, 0)
        self.local().start()

    def wait(self):
        def one(step, carry):
            self.copy(step).wait_recv()
            return carry

        lax.fori_loop(1, self.size, one, 0)
        self.local().wait()

    def drain(self):
        def one(step, carry):
            self.copy(step).wait_send()
            return carry

        lax.fori_loop(1, self.size, one, 0)


def spread_index():
    at = lax.broadcasted_iota(jnp.int32, (256, 256), 0)
    row = lax.broadcasted_iota(jnp.int32, (256, 256), 1)
    return at, row


def one_hot(wanted, row):
    return jnp.where(row == wanted, 1.0, 0.0).astype(BF)


def pack_time(src, dst):
    at, row = spread_index()
    i, c, a = at // 16, (at // 2) % 8, at % 2
    turn = one_hot(c * 32 + a * 16 + i, row)

    def one(n, carry):
        rows = span(n, 16)
        parts = [src[a, rows, c * 128 : c * 128 + 128] for c in range(8) for a in range(2)]
        out = matmul(turn, jnp.concatenate(parts, axis=0)).astype(BF)
        dst[rows] = out.reshape(16, 16, 128)
        return carry

    lax.fori_loop(0, 8, one, 0, unroll=8)


def unpack_time(src, dst):
    at, row = spread_index()
    c, a, i = at // 32, (at // 16) % 2, at % 16
    turn = one_hot(i * 16 + c * 2 + a, row)

    def one(n, carry):
        rows = span(n, 16)
        out = matmul(turn, src[rows].reshape(256, 128)).astype(BF)
        for c in range(8):
            for a in range(2):
                part = out[c * 32 + a * 16 : c * 32 + a * 16 + 16]
                dst[a, rows, c * 128 : c * 128 + 128] = part
        return carry

    lax.fori_loop(0, 8, one, 0, unroll=8)


def pack_agent(src, dst):
    at, row = spread_index()
    i, c, a = at // 16, (at // 2) % 8, at % 2
    turn = one_hot(c * 32 + i * 2 + a, row)

    def one(n, carry):
        parts = [src[span(n, 32), c * 128 : c * 128 + 128] for c in range(8)]
        out = matmul(turn, jnp.concatenate(parts, axis=0)).astype(BF)
        dst[span(n, 16)] = out.reshape(16, 16, 128)
        return carry

    lax.fori_loop(0, 8, one, 0, unroll=8)


def unpack_agent(src, dst):
    at, row = spread_index()
    c, i, a = at // 32, (at // 2) % 16, at % 2
    turn = one_hot(i * 16 + c * 2 + a, row)

    def one(n, carry):
        out = matmul(turn, src[span(n, 16)].reshape(256, 128)).astype(BF)
        for c in range(8):
            dst[span(n, 32), c * 128 : c * 128 + 128] = out[c * 32 : c * 32 + 32]
        return carry

    lax.fori_loop(0, 8, one, 0, unroll=8)


class Spread:
    def __init__(self, place, send, recv, src, dst, to_steps):
        self.place, self.send, self.recv, self.src, self.dst, self.to_steps = place, send, recv, src, dst, to_steps

    def places(self, ag, tm):
        return ag * 8 + tm, tm * 16 + ag

    def start(self):
        place = self.place
        agents, steps = self.places(place.ag, place.tm)
        mine = agents if self.to_steps else steps

        def one(step, carry):
            ag, tm = (place.ag + step // 8) % 16, (place.tm + step % 8) % 8
            by_agents, by_steps = self.places(ag, tm)
            theirs = by_steps if self.to_steps else by_agents
            remote(self.src.at[theirs], self.dst.at[mine], self.send, self.recv, (ag, tm)).start()
            return carry

        lax.fori_loop(1, 128, one, 0)
        own = steps if self.to_steps else agents
        pltpu.make_async_copy(self.src.at[own], self.dst.at[mine], self.recv).start()

    def wait(self):
        pltpu.make_async_copy(self.src, self.dst, self.recv).wait()

    def drain(self):
        pltpu.make_async_copy(self.src.at[0:127], self.dst.at[0:127], self.send).wait()


def block_kernel(
    tokens, cotangent, observed_in, time_qkv, time_out, agent_qkv, agent_out,
    grad_tokens, tq_ref, to_ref, aq_ref, ao_ref,
    w_tq, w_to, w_aq, w_ao,
    x_time, made, turned, x_agent, cot, tiles_out, first_in, back_in,
    merged_t, merged_a, gmix, gu, bias_t, bias_a, observed,
    units, gms, mixeds, g_time, g_agent,
    *rest,
):
    grad_a = rest[0]
    bufs = (rest[1:7], rest[7:13])
    load, spread_send, spread_recv, swap_send, swap_recv, twin_send, twin_recv, sc_send, sc_recv = rest[13:]
    place = Place()
    loads = [
        pltpu.make_async_copy(src, dst, load.at[i])
        for i, (src, dst) in enumerate(
            (
                (cotangent, cot),
                (observed_in, observed),
                (time_qkv, w_tq),
                (time_out, w_to),
                (agent_out, w_ao),
                (agent_qkv, w_aq),
            )
        )
    ]
    for copy in loads:
        copy.start()
    far = [
        (place.y * 4 + (1 - place.zlo) * 2 + place.core, (1 - place.zhi) * 4 + place.x),
    ]
    greet(
        [((place.ag + step) % 16, place.tm) for step in range(1, 16)]
        + [(place.ag, (place.tm + step) % 8) for step in range(1, 8)]
        + far
    )

    def swap(slot, axis, source, target):
        return Swap(place, axis, swap_send.at[slot], swap_recv.at[slot], source, target)

    def two(ref):
        return lambda i: ref.at[pl.ds(i * 2, 2)]

    def sixteen(ref):
        return lambda i: ref.at[0:2, span(i, 16), :]

    def rows16(ref):
        return lambda i: ref.at[span(i, 16), :]

    tokens_in = swap(0, "tm", two(tokens), sixteen(x_time))
    cot_in = swap(1, "ag", rows16(turned), rows16(g_agent))
    first = Spread(place, spread_send.at[0], spread_recv.at[0], tiles_out, first_in, True)
    back = Spread(place, spread_send.at[1], spread_recv.at[1], tiles_out, back_in, False)
    tokens_out = swap(2, "tm", sixteen(made), two(grad_tokens))
    twins = [Twin(place, twin_send.at[s], twin_recv.at[s]) for s in range(2)]

    def block_a(stream, slot):
        lo, hi, _ = STREAMS[stream]
        return grad_a.at[slot, :, lo:hi]

    def block_t(stream, slot):
        lo, hi, _ = STREAMS[stream]
        if stream < 2:
            return w_aq.at[span(slot, 128), lo:hi]
        return w_aq.at[span(slot + 4, 128), 0 : hi - lo]

    def second_a(stream):
        lo, hi, _ = STREAMS[stream]
        return w_aq.at[512 + stream * 128 : 640 + stream * 128, 1408 : 1408 + hi - lo]

    def second_t(stream):
        lo, hi, _ = STREAMS[stream]
        if stream < 2:
            return w_aq.at[384:512, lo:hi]
        return w_aq.at[896:1024, 0 : hi - lo]

    blocks, seconds = (block_a, block_t), (second_a, second_t)
    scatters = [Scatter(place, blocks[s], seconds[s], bufs[s], sc_send.at[s], sc_recv.at[s]) for s in range(2)]
    unit_a, unit_t = units.at[0], units.at[1]
    gm_a, gm_t = gms.at[0], gms.at[1]
    mixed_a, mixed_t = mixeds.at[0], mixeds.at[1]
    ut = [w_ao.at[0:512, 0:512], w_ao.at[0:512, 512:1024], w_ao.at[512:1024, 0:512]]
    ut_mixed = w_ao.at[512:1024, 512:1024]
    seqs = [slice(0, 128), slice(128, 256)]
    biases_t = [bias_t.at[0], bias_t.at[1]]

    with jax.named_scope("tokens_to_agents"):
        tokens_in.start()
        loads[0].wait()
        swap_rows(cot, turned)
        loads[1].wait()
        self_t = lax.broadcasted_iota(jnp.int32, (128, 128), 0) == lax.broadcasted_iota(jnp.int32, (128, 128), 1)
        for a in range(2):
            row = observed[pl.ds(place.ag * 16 + place.tm * 2 + a, 1), :]
            bias_t[a] = jnp.where((row > 0) | self_t, 0.0, masked_score)
        at_step = lax.broadcasted_iota(jnp.int32, (8, STEPS), 1) == place.tm * 16 + place.ag
        seen = matmul(jnp.where(at_step, 1.0, 0.0).astype(BF), observed[...].astype(F32).astype(BF), NT)
        self_a = lax.broadcasted_iota(jnp.int32, (256, 256), 0) == lax.broadcasted_iota(jnp.int32, (256, 256), 1)
        bias_a[...] = jnp.where((seen[0:1, :] > 0.5) | self_a, 0.0, masked_score)
        loads[2].wait()
        tokens_in.wait()
        cot_in.start()
    with jax.named_scope("time_forward"):
        project(x_time, unit_t, w_tq, merged_t)
        twins[1].copy(0, unit_t).start()
        attend(merged_t, mixed_t, seqs, biases_t, 4)
        twins[1].copy(2, mixed_t).start()
        loads[3].wait()
        add_residual(x_time, mixed_t, w_to, made, (2, 128))
        pack_time(made, tiles_out)
        first.start()
    with jax.named_scope("first_to_steps"):
        cot_in.wait()
        twins[0].copy(3, g_agent).start()
        loads[4].wait()
        grad_of_mixed(g_agent.at[0:256, :], w_ao, gmix)
        cot_in.drain()
        loads[5].wait()
        first.wait()
        unpack_agent(first_in, x_agent)
    with jax.named_scope("agent_backward"):
        project(x_agent, unit_a, w_aq, merged_a)
        twins[0].copy(0, unit_a).start()
        attend_back(merged_a, gmix, mixed_a, gm_a, [slice(0, 256)], [bias_a], 2)
        twins[0].copy(2, mixed_a).start()
        twins[0].copy(1, gm_a).start()
        grad_of_input(x_agent, g_agent.at[0:256, :], gm_a, w_aq, gu, cot, (256,))
        first.drain()
        pack_agent(cot, tiles_out)
        back.start()
    with jax.named_scope("agent_weights"):
        for slot, ref in enumerate((unit_a, gm_a, mixed_a, g_agent)):
            twins[0].copy(slot, ref).wait_recv()
        transposed(place, unit_a, mixed_a, ut, ut_mixed, gu)
        for stream in range(3):
            scatters[0].start(stream, ut, ut_mixed, gm_a, g_agent)
    with jax.named_scope("grad_first_to_agents"):
        back.wait()
        unpack_time(back_in, g_time)
        twins[1].copy_rows(3, g_time).start()
    with jax.named_scope("time_backward"):
        g_own = g_time.at[0:2]
        grad_of_mixed(g_own, w_to, gmix)
        attend_back(merged_t, gmix, None, gm_t, seqs, biases_t, 4)
        twins[1].copy(1, gm_t).start()
        for stream in range(3):
            scatters[0].pass_on(stream)
        grad_of_input(x_time, g_own, gm_t, w_tq, gu, made, (2, 128))
        tokens_out.start()
        for stream in range(3):
            scatters[0].second(stream)
    with jax.named_scope("time_weights"):
        for slot, ref in enumerate((unit_t, gm_t, mixed_t)):
            twins[1].copy(slot, ref).wait_recv()
        twins[1].copy_rows(3, g_time).wait_recv()
        transposed(place, unit_t, mixed_t, ut, ut_mixed, gu)
        for stream in range(3):
            scatters[1].start(stream, ut, ut_mixed, gm_t, g_time)
    with jax.named_scope("rings"):
        outs = ((aq_ref, ao_ref), (tq_ref, to_ref))
        for stream in range(3):
            scatters[0].third(stream)
        for stream in range(3):
            scatters[1].pass_on(stream)
        for stream in range(3):
            scatters[1].second(stream)
        for stream in range(3):
            scatters[0].last(stream, *outs[0])
        for stream in range(3):
            scatters[1].third(stream)
        for stream in range(3):
            scatters[1].last(stream, *outs[1])
        tokens_out.wait()
    with jax.named_scope("drain"):
        for s in range(2):
            scatters[s].drain()
        for slot, ref in enumerate((unit_a, gm_a, mixed_a, g_agent)):
            twins[0].copy(slot, ref).wait_send()
        for slot, ref in enumerate((unit_t, gm_t, mixed_t)):
            twins[1].copy(slot, ref).wait_send()
        twins[1].copy_rows(3, g_time).wait_send()
        for moved in (tokens_in, back, tokens_out):
            moved.drain()


def hand_on(*refs):
    for source, target in zip(refs[:5], refs[5:]):
        target[...] = source[...]


def local(tokens, cotangent, observed, time_qkv, time_out, agent_qkv, agent_out):
    shape = jax.ShapeDtypeStruct
    grad_tokens, *grads = pl.pallas_call(
        block_kernel,
        out_shape=[
            shape((16, 16, D), BF),
            shape((8, 3 * D), F32),
            shape((8, D), F32),
            shape((8, 3 * D), F32),
            shape((8, D), F32),
        ],
        in_specs=[
            pl.BlockSpec(memory_space=pl.ANY)
        ]
        * 7,
        out_specs=[pl.BlockSpec(memory_space=pl.ANY)] + [pl.BlockSpec(memory_space=pltpu.VMEM)] * 4,
        scratch_shapes=[
            pltpu.VMEM((D, 3 * D), BF),
            pltpu.VMEM((D, D), BF),
            pltpu.VMEM((D, 3 * D), BF),
            pltpu.VMEM((D, D), BF),
            pltpu.VMEM((2, 128, D), BF),
            pltpu.VMEM((2, 128, D), BF),
            pltpu.VMEM((256, D), BF),
            pltpu.VMEM((256, D), BF),
            pltpu.VMEM((256, D), BF),
            pltpu.VMEM((128, 16, 128), BF),
            pltpu.VMEM((128, 16, 128), BF),
            pltpu.VMEM((128, 16, 128), BF),
            pltpu.VMEM((256, 3 * D), BF),
            pltpu.VMEM((256, 3 * D), BF),
            pltpu.VMEM((256, D), BF),
            pltpu.VMEM((256, D), F32),
            pltpu.VMEM((2, 128, 128), F32),
            pltpu.VMEM((256, 256), F32),
            pltpu.VMEM((256, STEPS), jnp.int32),
            pltpu.VMEM((2, 512, D), BF),
            pltpu.VMEM((2, 512, 3 * D), BF),
            pltpu.VMEM((2, 512, D), BF),
            pltpu.VMEM((4, 128, D), BF),
            pltpu.VMEM((512, D), BF),
        ]
        + [pltpu.VMEM((3, 128, 4096), BF)]
        + scatter_bufs()
        + scatter_bufs()
        + [
            pltpu.SemaphoreType.DMA((6,)),
            pltpu.SemaphoreType.DMA((2,)),
            pltpu.SemaphoreType.DMA((2,)),
            pltpu.SemaphoreType.DMA((3, 16)),
            pltpu.SemaphoreType.DMA((3, 16)),
            pltpu.SemaphoreType.DMA((2, 4)),
            pltpu.SemaphoreType.DMA((2, 4)),
            pltpu.SemaphoreType.DMA((2, 3, 12)),
            pltpu.SemaphoreType.DMA((2, 3, 12)),
        ],
        compiler_params=pltpu.CompilerParams(
            collective_id=0, has_side_effects=True, vmem_limit_bytes=61 * 1024 * 1024
        ),
    )(
        tokens.reshape(16, 16, D),
        cotangent.reshape(256, D),
        observed.reshape(256, STEPS),
        time_qkv,
        time_out,
        agent_qkv,
        agent_out,
    )
    made = [grad_tokens, *grads]
    grad_tokens, *grads = pl.pallas_call(
        hand_on,
        out_shape=[shape(x.shape, x.dtype) for x in made],
        in_specs=[pl.BlockSpec(memory_space=pltpu.VMEM)] * 5,
        out_specs=[pl.BlockSpec(memory_space=pltpu.VMEM)] * 5,
    )(*made)
    return (grad_tokens.reshape(1, 16, 16, D), *grads)


def solution(mesh):
    in_specs = (P(None, "ag", "tm", None), P(None, "ag", "tm", None), P(), P(), P(), P(), P())
    out_specs = (
        P(None, "ag", "tm", None),
        P(("ag", "tm"), None),
        P(("ag", "tm"), None),
        P(("ag", "tm"), None),
        P(("ag", "tm"), None),
    )
    return jax.shard_map(local, mesh=mesh, in_specs=in_specs, out_specs=out_specs, check_vma=False)
```

```python
import functools

import jax
import jax.numpy as jnp
from jax import lax
from jax.experimental import pallas as pl
from jax.experimental.pallas import tpu as pltpu
from jax.sharding import PartitionSpec as P

D = 1024
H = 16
HD = 64
STEPS = 128
epsilon = 1e-06
masked_score = -1e30

MESH = pl.DeviceIdType.MESH
BF = jnp.bfloat16
F32 = jnp.float32
NT = (((1,), (1,)), ((), ()))
TN = (((0,), (0,)), ((), ()))

STREAMS = ((0, 1280, "xyz"), (1280, 2816, "yzx"), (2816, 4096, "zxy"))


def matmul(left, right, dims=(((1,), (0,)), ((), ()))):
    return lax.dot_general(left, right, dims, preferred_element_type=F32)


class Place:
    def __init__(self):
        self.ag = lax.axis_index("ag")
        self.tm = lax.axis_index("tm")
        self.y = self.ag // 4
        self.zlo = (self.ag // 2) % 2
        self.core = self.ag % 2
        self.zhi = self.tm // 4
        self.x = self.tm % 4
        self.z = self.zhi * 2 + self.zlo

    def at(self, axis):
        return {"x": self.x, "y": self.y, "z": self.z}[axis]

    def ring(self, axis, step):
        if axis == "x":
            return (self.ag, self.zhi * 4 + (self.x + step) % 4)
        if axis == "y":
            return (((self.y + step) % 4) * 4 + self.ag % 4, self.tm)
        z = (self.z + step) % 4
        return (self.y * 4 + (z % 2) * 2 + self.core, (z // 2) * 4 + self.x)

    def twin(self):
        return (self.ag + 1 - 2 * self.core, self.tm)


def remote(src, dst, send, recv, device):
    return pltpu.make_async_remote_copy(
        src_ref=src, dst_ref=dst, send_sem=send, recv_sem=recv, device_id=device, device_id_type=MESH
    )


def greet(devices):
    barrier = pltpu.get_barrier_semaphore()
    for device in devices:
        pl.semaphore_signal(barrier, inc=1, device_id=device, device_id_type=MESH)
    pl.semaphore_wait(barrier, len(devices))


def selector(core, x_first):
    at = lax.broadcasted_iota(jnp.int32, (128, 256), 0)
    row = lax.broadcasted_iota(jnp.int32, (128, 256), 1)
    high, low = at // 32, (at // 8) % 4
    x, z = (high, low) if x_first else (low, high)
    wanted = (z % 2) * 128 + core * 64 + (z // 2) * 32 + x * 8 + at % 8
    return jnp.where(row == wanted, 1.0, 0.0).astype(BF)


class Twin:
    def __init__(self, place, send, recv):
        self.place, self.send, self.recv = place, send, recv

    def copy(self, slot, ref, cols=None):
        cols = slice(None) if cols is None else cols
        return remote(
            ref.at[0:256, cols], ref.at[256:512, cols], self.send.at[slot], self.recv.at[slot], self.place.twin()
        )

    def copy_rows(self, slot, ref):
        return remote(ref.at[0:2], ref.at[2:4], self.send.at[slot], self.recv.at[slot], self.place.twin())


class Scatter:
    def __init__(self, place, block, second_block, bufs, send, recv):
        self.place, self.second_block = place, second_block
        self.block, (self.own, self.r1, self.relay, self.r2, self.s3, self.r3) = block, bufs
        self.send, self.recv = send, recv

    def first(self, stream, part):
        lo, hi, axes = STREAMS[stream]
        mid = (hi - lo) // 256 * 128
        half_a, half_b = slice(0, mid), slice(mid, hi - lo)
        all_a, all_b = slice(lo, lo + mid), slice(lo + mid, hi)
        slot, near, far = (
            (1, half_a, self.relay.at[:, all_a]),
            (1, half_b, self.relay.at[:, all_b]),
            (0, half_b, self.r1.at[0, :, all_b]),
            (2, half_a, self.r1.at[1, :, all_a]),
            (0, half_a, self.r1.at[0, :, all_a]),
            (2, half_b, self.r1.at[1, :, all_b]),
        )[part]
        return remote(
            self.block(stream, slot).at[:, near], far, self.send.at[stream, part], self.recv.at[stream, part],
            self.place.ring(axes[0], 3 if part % 2 else 1),
        )

    def copy(self, stream, phase, step):
        lo, hi, axes = STREAMS[stream]
        cols = slice(lo, hi)
        axis = axes[phase]
        to = (self.place.at(axis) + step) % 4
        slot = step - 1
        if phase == 1:
            src = self.second_block(stream).at[pl.ds(pl.multiple_of(to * 32, 32), 32), :]
            dst = self.r2.at[slot, :, cols]
        else:
            src, dst = self.s3.at[to, :, cols], self.r3.at[slot, :, cols]
        sem = 3 + 3 * phase + slot
        return remote(
            src, dst, self.send.at[stream, sem], self.recv.at[stream, sem], self.place.ring(axis, step)
        )

    def product(self, stream, ut, ut_mixed, gm, g, block):
        lo, hi, _ = STREAMS[stream]
        rows = pl.ds(pl.multiple_of(block * 128, 128), 128)
        if stream < 2:
            return [(lo, hi, matmul(ut[stream][rows, :], gm[:, lo:hi]))]
        return [
            (lo, 3072, matmul(ut[2][rows, :], gm[:, lo:3072])),
            (3072, 4096, matmul(ut_mixed[rows, :], g[...].reshape(512, D))),
        ]

    def start(self, stream, ut, ut_mixed, gm, g):
        first, _, axes = STREAMS[stream]
        at = self.place.at(axes[0])
        for step, parts in ((2, (0, 1)), (1, (2,)), (3, (3,))):
            for lo, hi, made in self.product(stream, ut, ut_mixed, gm, g, (at + step) % 4):
                self.block(stream, step - 1)[:, lo - first : hi - first] = made.astype(BF)
            for part in parts:
                self.first(stream, part).start()
        for lo, hi, made in self.product(stream, ut, ut_mixed, gm, g, at):
            self.own[:, lo:hi] = made

    def pass_on(self, stream):
        lo, hi, _ = STREAMS[stream]
        mid = (hi - lo) // 256 * 128
        for part, slot, left, right in ((0, 0, 0, mid), (1, 2, mid, hi - lo)):
            self.first(stream, part).wait_recv()
            block = self.block(stream, slot)
            came = self.relay[:, lo + left : lo + right].astype(F32)
            block[:, left:right] = (block[:, left:right].astype(F32) + came).astype(BF)
            self.first(stream, part + 4).start()

    def second(self, stream):
        lo, hi, _ = STREAMS[stream]
        for part in (2, 3, 4, 5):
            self.first(stream, part).wait_recv()

        def one(q, carry):
            rows = pl.ds(pl.multiple_of(q * 32, 32), 32)
            total = self.own[rows, lo:hi]
            for slot in range(2):
                total = total + self.r1[slot, rows, lo:hi].astype(F32)
            self.own[rows, lo:hi] = total
            self.second_block(stream)[rows, :] = total.astype(BF)
            return carry

        lax.fori_loop(0, 4, one, 0)
        for step in (1, 2, 3):
            self.copy(stream, 1, step).start()

    def third(self, stream):
        lo, hi, axes = STREAMS[stream]
        for step in (1, 2, 3):
            self.copy(stream, 1, step).wait_recv()
        total = self.own[pl.ds(pl.multiple_of(self.place.at(axes[1]) * 32, 32), 32), lo:hi]
        for slot in range(3):
            total = total + self.r2[slot, :, lo:hi].astype(F32)
        self.own[0:32, lo:hi] = total
        for q in range(4):
            self.s3[q, :, lo:hi] = total[q * 8 : q * 8 + 8].astype(BF)
        for step in (1, 2, 3):
            self.copy(stream, 2, step).start()

    def last(self, stream, qkv_ref, out_ref):
        lo, hi, axes = STREAMS[stream]
        for step in (1, 2, 3):
            self.copy(stream, 2, step).wait_recv()
        total = self.own[pl.ds(pl.multiple_of(self.place.at(axes[2]) * 8, 8), 8), lo:hi]
        for slot in range(3):
            total = total + self.r3[slot, :, lo:hi].astype(F32)
        top = min(hi, 3072)
        qkv_ref[:, lo:top] = total[:, : top - lo]
        if hi > 3072:
            out_ref[...] = total[:, 3072 - lo :]

    def drain(self):
        for stream in range(3):
            for part in range(6):
                self.first(stream, part).wait_send()
            for phase in (1, 2):
                for step in (1, 2, 3):
                    self.copy(stream, phase, step).wait_send()


def scatter_bufs():
    return [
        pltpu.VMEM((128, 4096), F32),
        pltpu.VMEM((2, 128, 4096), BF),
        pltpu.VMEM((128, 4096), BF),
        pltpu.VMEM((3, 32, 4096), BF),
        pltpu.VMEM((4, 8, 4096), BF),
        pltpu.VMEM((3, 8, 4096), BF),
    ]


def transposed(place, unit, mixed, ut, ut_mixed, spare):
    sel_x = selector(place.core, True)
    sel_z = selector(place.core, False)

    def last_order(part, y):
        for z in range(4):
            for x in range(4):
                at = (z % 2) * 128 + x * 32 + y * 8
                spare[at : at + 8, (z // 2) * 512 : (z // 2) * 512 + 512] = part[z * 32 + x * 8 : z * 32 + x * 8 + 8]

    for y in range(4):
        cols = slice(y * 256, y * 256 + 256)
        part = matmul(sel_x, unit[:, cols], NT).astype(BF)
        for x in range(4):
            ut[0][x * 128 + y * 32 : x * 128 + y * 32 + 32, :] = part[x * 32 : x * 32 + 32]
        part = matmul(sel_z, unit[:, cols], NT)
        ut[1][y * 128 : y * 128 + 128, :] = part.astype(BF)
        last_order(part, y)
    ut[2][0:256, :] = spare[:, 0:512].astype(BF)
    ut[2][256:512, :] = spare[:, 512:1024].astype(BF)
    for y in range(4):
        last_order(matmul(sel_z, mixed[:, y * 256 : y * 256 + 256], NT), y)
    ut_mixed[0:256, :] = spare[:, 0:512].astype(BF)
    ut_mixed[256:512, :] = spare[:, 512:1024].astype(BF)


def normal(x_ref):
    x = x_ref[...].reshape(256, D).astype(F32)
    inverse = lax.rsqrt(jnp.mean(x * x, axis=-1, keepdims=True) + epsilon)
    return x * inverse, inverse


def span(start, size):
    return pl.ds(pl.multiple_of(start * size, size), size)


def project(x_ref, unit, w, merged):
    unit[0:256, :] = normal(x_ref)[0].astype(BF)

    def one(n, carry):
        cols = span(n, 512)
        merged[:, cols] = matmul(unit[0:256, :], w[:, cols]).astype(BF)
        return carry

    lax.fori_loop(0, 6, one, 0, unroll=6)


def halves():
    lane = lax.broadcasted_iota(jnp.int32, (1, 128), 1)
    low = jnp.where(lane < HD, 1.0, 0.0)
    return low.astype(BF), (1.0 - low).astype(BF)


def pair_parts(merged, rows, pair):
    q = merged[rows, span(pair, 128)] * BF(HD**-0.5)
    k = merged[rows, pl.ds(pl.multiple_of(D + pair * 128, 128), 128)]
    v = merged[rows, pl.ds(pl.multiple_of(2 * D + pair * 128, 128), 128)]
    return q, k, v


def attend(merged, mixed, seqs, biases, group):
    def one(turn, carry):
        low_high = halves()
        jobs = []
        for rows, bias in zip(seqs, biases):
            for i in range(group):
                pair = turn * group + i
                q, k, v = pair_parts(merged, rows, pair)
                for half in low_high:
                    jobs.append((rows, pair, bias, q * half, k, v * half))
        scores = [matmul(q, k, NT) + bias[...] for _, _, bias, q, k, _ in jobs]
        probs = probs_of(scores)
        parts = [matmul(p.astype(BF), job[5]) for p, job in zip(probs, jobs)]
        for i in range(0, len(jobs), 2):
            rows, pair = jobs[i][:2]
            mixed[rows, span(pair, 128)] = (parts[i] + parts[i + 1]).astype(BF)
        return carry

    lax.fori_loop(0, H // 2 // group, one, 0)


def probs_of(scores):
    tops = [jnp.max(s, axis=-1, keepdims=True) for s in scores]
    shifted = [jnp.exp(s - t) for s, t in zip(scores, tops)]
    sums = [jnp.sum(s, axis=-1, keepdims=True) for s in shifted]
    return [s * (1.0 / t) for s, t in zip(shifted, sums)]


def attend_back(merged, gmix, mixed, gm, seqs, biases, group):
    def one(turn, carry):
        low_high = halves()
        jobs = []
        for rows, bias in zip(seqs, biases):
            for i in range(group):
                pair = turn * group + i
                q, k, v = pair_parts(merged, rows, pair)
                go = gmix[rows, span(pair, 128)]
                for half in low_high:
                    jobs.append((rows, pair, bias, q * half, k, v, go * half, half))
        scores = [matmul(job[3], job[4], NT) + job[2][...] for job in jobs]
        gps = [matmul(job[6], job[5], NT) for job in jobs]
        probs = probs_of(scores)
        means = [jnp.sum(gp * p, axis=-1, keepdims=True) for gp, p in zip(gps, probs)]
        gss = [(p * (gp - m)).astype(BF) for p, gp, m in zip(probs, gps, means)]
        rounded = [p.astype(BF) for p in probs]
        gq = [matmul(gs, job[4] * job[7]) for gs, job in zip(gss, jobs)]
        gk = [matmul(gs, job[3], TN) for gs, job in zip(gss, jobs)]
        gv = [matmul(p, job[6], TN) for p, job in zip(rounded, jobs)]
        if mixed is not None:
            mx = [matmul(p, job[5] * job[7]) for p, job in zip(rounded, jobs)]
        for i in range(0, len(jobs), 2):
            rows, pair = jobs[i][:2]
            gm[rows, span(pair, 128)] = ((gq[i] + gq[i + 1]) * HD**-0.5).astype(BF)
            gm[rows, pl.ds(pl.multiple_of(D + pair * 128, 128), 128)] = (gk[i] + gk[i + 1]).astype(BF)
            gm[rows, pl.ds(pl.multiple_of(2 * D + pair * 128, 128), 128)] = (gv[i] + gv[i + 1]).astype(BF)
            if mixed is not None:
                mixed[rows, span(pair, 128)] = (mx[i] + mx[i + 1]).astype(BF)
        return carry

    lax.fori_loop(0, H // 2 // group, one, 0)


def add_residual(x_ref, mixed, w, out_ref, shape):
    for n in range(2):
        cols = slice(n * 512, n * 512 + 512)
        x = x_ref[..., cols].reshape(256, 512).astype(F32)
        out = x + matmul(mixed[0:256, :], w[:, cols])
        out_ref[..., cols] = out.astype(BF).reshape(shape + (512,))


def grad_of_mixed(g, w, gmix):
    def one(n, carry):
        rows = span(n, 256)
        gmix[:, rows] = matmul(g[...].reshape(256, D), w[rows, :], NT).astype(BF)
        return carry

    lax.fori_loop(0, 4, one, 0, unroll=4)


def grad_of_input(x_ref, g, gm, w, gu, out_ref, shape):
    def one(n, carry):
        rows = span(n, 512)
        gu[:, rows] = matmul(gm[0:256, :], w[rows, :], NT)
        return carry

    lax.fori_loop(0, 2, one, 0, unroll=2)
    normed, inverse = normal(x_ref)
    grad_unit = gu[...]
    rows = inverse * (grad_unit - normed * jnp.mean(grad_unit * normed, axis=-1, keepdims=True))
    out_ref[...] = (g[...].reshape(256, D).astype(F32) + rows).astype(BF).reshape(shape + (D,))


def swap_rows(src, dst):
    at = lax.broadcasted_iota(jnp.int32, (256, 256), 0)
    row = lax.broadcasted_iota(jnp.int32, (256, 256), 1)
    swap = jnp.where(row == (at % 16) * 16 + at // 16, 1.0, 0.0).astype(BF)
    for n in range(2):
        cols = slice(n * 512, n * 512 + 512)
        out = matmul(swap, src[..., cols].reshape(256, 512)).astype(BF)
        dst[..., cols] = out.reshape(dst.shape[:-1] + (512,))


class Swap:
    def __init__(self, place, axis, send, recv, source, target):
        self.place, self.axis, self.send, self.recv = place, axis, send, recv
        self.source, self.target = source, target
        self.size = 8 if axis == "tm" else 16
        self.me = place.tm if axis == "tm" else place.ag

    def copy(self, step):
        to = (self.me + step) % self.size
        device = (self.place.ag, to) if self.axis == "tm" else (to, self.place.tm)
        return remote(self.source(to), self.target(self.me), self.send.at[step], self.recv.at[step], device)

    def local(self):
        return pltpu.make_async_copy(self.source(self.me), self.target(self.me), self.recv.at[0])

    def start(self):
        def one(step, carry):
            self.copy(step).start()
            return carry

        lax.fori_loop(1, self.size, one, 0)
        self.local().start()

    def wait(self):
        def one(step, carry):
            self.copy(step).wait_recv()
            return carry

        lax.fori_loop(1, self.size, one, 0)
        self.local().wait()

    def drain(self):
        def one(step, carry):
            self.copy(step).wait_send()
            return carry

        lax.fori_loop(1, self.size, one, 0)


def spread_index():
    at = lax.broadcasted_iota(jnp.int32, (256, 256), 0)
    row = lax.broadcasted_iota(jnp.int32, (256, 256), 1)
    return at, row


def one_hot(wanted, row):
    return jnp.where(row == wanted, 1.0, 0.0).astype(BF)


def pack_time(src, dst):
    at, row = spread_index()
    i, c, a = at // 16, (at // 2) % 8, at % 2
    turn = one_hot(c * 32 + a * 16 + i, row)

    def one(n, carry):
        rows = span(n, 16)
        parts = [src[a, rows, c * 128 : c * 128 + 128] for c in range(8) for a in range(2)]
        out = matmul(turn, jnp.concatenate(parts, axis=0)).astype(BF)
        dst[rows] = out.reshape(16, 16, 128)
        return carry

    lax.fori_loop(0, 8, one, 0, unroll=8)


def unpack_time(src, dst):
    at, row = spread_index()
    c, a, i = at // 32, (at // 16) % 2, at % 16
    turn = one_hot(i * 16 + c * 2 + a, row)

    def one(n, carry):
        rows = span(n, 16)
        out = matmul(turn, src[rows].reshape(256, 128)).astype(BF)
        for c in range(8):
            for a in range(2):
                part = out[c * 32 + a * 16 : c * 32 + a * 16 + 16]
                dst[a, rows, c * 128 : c * 128 + 128] = part
        return carry

    lax.fori_loop(0, 8, one, 0, unroll=8)


def pack_agent(src, dst):
    at, row = spread_index()
    i, c, a = at // 16, (at // 2) % 8, at % 2
    turn = one_hot(c * 32 + i * 2 + a, row)

    def one(n, carry):
        parts = [src[span(n, 32), c * 128 : c * 128 + 128] for c in range(8)]
        out = matmul(turn, jnp.concatenate(parts, axis=0)).astype(BF)
        dst[span(n, 16)] = out.reshape(16, 16, 128)
        return carry

    lax.fori_loop(0, 8, one, 0, unroll=8)


def unpack_agent(src, dst):
    at, row = spread_index()
    c, i, a = at // 32, (at // 2) % 16, at % 2
    turn = one_hot(i * 16 + c * 2 + a, row)

    def one(n, carry):
        out = matmul(turn, src[span(n, 16)].reshape(256, 128)).astype(BF)
        for c in range(8):
            dst[span(n, 32), c * 128 : c * 128 + 128] = out[c * 32 : c * 32 + 32]
        return carry

    lax.fori_loop(0, 8, one, 0, unroll=8)


class Spread:
    def __init__(self, place, send, recv, src, dst, to_steps):
        self.place, self.send, self.recv, self.src, self.dst, self.to_steps = place, send, recv, src, dst, to_steps

    def places(self, ag, tm):
        return ag * 8 + tm, tm * 16 + ag

    def start(self):
        place = self.place
        agents, steps = self.places(place.ag, place.tm)
        mine = agents if self.to_steps else steps

        def one(step, carry):
            ag, tm = (place.ag + step // 8) % 16, (place.tm + step % 8) % 8
            by_agents, by_steps = self.places(ag, tm)
            theirs = by_steps if self.to_steps else by_agents
            remote(self.src.at[theirs], self.dst.at[mine], self.send, self.recv, (ag, tm)).start()
            return carry

        lax.fori_loop(1, 128, one, 0)
        own = steps if self.to_steps else agents
        pltpu.make_async_copy(self.src.at[own], self.dst.at[mine], self.recv).start()

    def wait(self):
        pltpu.make_async_copy(self.src, self.dst, self.recv).wait()

    def drain(self):
        pltpu.make_async_copy(self.src.at[0:127], self.dst.at[0:127], self.send).wait()


def block_kernel(
    tokens, cotangent, observed_in, time_qkv, time_out, agent_qkv, agent_out,
    grad_tokens, tq_ref, to_ref, aq_ref, ao_ref,
    w_tq, w_to, w_aq, w_ao,
    x_time, made, turned, x_agent, cot, tiles_out, first_in, back_in,
    merged_t, merged_a, gmix, gu, bias_t, bias_a, observed,
    units, gms, mixeds, g_time, g_agent,
    *rest,
):
    grad_a = rest[0]
    bufs = (rest[1:7], rest[7:13])
    load, spread_send, spread_recv, swap_send, swap_recv, twin_send, twin_recv, sc_send, sc_recv = rest[13:]
    place = Place()
    loads = [
        pltpu.make_async_copy(src, dst, load.at[i])
        for i, (src, dst) in enumerate(
            (
                (cotangent, cot),
                (observed_in, observed),
                (time_qkv, w_tq),
                (time_out, w_to),
                (agent_out, w_ao),
                (agent_qkv, w_aq),
            )
        )
    ]
    for copy in loads:
        copy.start()
    far = [
        (place.y * 4 + (1 - place.zlo) * 2 + place.core, (1 - place.zhi) * 4 + place.x),
    ]
    greet(
        [((place.ag + step) % 16, place.tm) for step in range(1, 16)]
        + [(place.ag, (place.tm + step) % 8) for step in range(1, 8)]
        + far
    )

    def swap(slot, axis, source, target):
        return Swap(place, axis, swap_send.at[slot], swap_recv.at[slot], source, target)

    def two(ref):
        return lambda i: ref.at[pl.ds(i * 2, 2)]

    def sixteen(ref):
        return lambda i: ref.at[0:2, span(i, 16), :]

    def rows16(ref):
        return lambda i: ref.at[span(i, 16), :]

    tokens_in = swap(0, "tm", two(tokens), sixteen(x_time))
    cot_in = swap(1, "ag", rows16(turned), rows16(g_agent))
    first = Spread(place, spread_send.at[0], spread_recv.at[0], tiles_out, first_in, True)
    back = Spread(place, spread_send.at[1], spread_recv.at[1], tiles_out, back_in, False)
    tokens_out = swap(2, "tm", sixteen(made), two(grad_tokens))
    twins = [Twin(place, twin_send.at[s], twin_recv.at[s]) for s in range(2)]

    def block_a(stream, slot):
        lo, hi, _ = STREAMS[stream]
        return grad_a.at[slot, :, lo:hi]

    def block_t(stream, slot):
        lo, hi, _ = STREAMS[stream]
        if stream < 2:
            return w_aq.at[span(slot, 128), lo:hi]
        return w_aq.at[span(slot + 4, 128), 0 : hi - lo]

    def second_a(stream):
        lo, hi, _ = STREAMS[stream]
        return w_aq.at[512 + stream * 128 : 640 + stream * 128, 1408 : 1408 + hi - lo]

    def second_t(stream):
        lo, hi, _ = STREAMS[stream]
        if stream < 2:
            return w_aq.at[384:512, lo:hi]
        return w_aq.at[896:1024, 0 : hi - lo]

    blocks, seconds = (block_a, block_t), (second_a, second_t)
    scatters = [Scatter(place, blocks[s], seconds[s], bufs[s], sc_send.at[s], sc_recv.at[s]) for s in range(2)]
    unit_a, unit_t = units.at[0], units.at[1]
    gm_a, gm_t = gms.at[0], gms.at[1]
    mixed_a, mixed_t = mixeds.at[0], mixeds.at[1]
    ut = [w_ao.at[0:512, 0:512], w_ao.at[0:512, 512:1024], w_ao.at[512:1024, 0:512]]
    ut_mixed = w_ao.at[512:1024, 512:1024]
    seqs = [slice(0, 128), slice(128, 256)]
    biases_t = [bias_t.at[0], bias_t.at[1]]

    with jax.named_scope("tokens_to_agents"):
        tokens_in.start()
        loads[0].wait()
        swap_rows(cot, turned)
        loads[1].wait()
        self_t = lax.broadcasted_iota(jnp.int32, (128, 128), 0) == lax.broadcasted_iota(jnp.int32, (128, 128), 1)
        for a in range(2):
            row = observed[pl.ds(place.ag * 16 + place.tm * 2 + a, 1), :]
            bias_t[a] = jnp.where((row > 0) | self_t, 0.0, masked_score)
        at_step = lax.broadcasted_iota(jnp.int32, (8, STEPS), 1) == place.tm * 16 + place.ag
        seen = matmul(jnp.where(at_step, 1.0, 0.0).astype(BF), observed[...].astype(F32).astype(BF), NT)
        self_a = lax.broadcasted_iota(jnp.int32, (256, 256), 0) == lax.broadcasted_iota(jnp.int32, (256, 256), 1)
        bias_a[...] = jnp.where((seen[0:1, :] > 0.5) | self_a, 0.0, masked_score)
        loads[2].wait()
        tokens_in.wait()
        cot_in.start()
    with jax.named_scope("time_forward"):
        project(x_time, unit_t, w_tq, merged_t)
        twins[1].copy(0, unit_t).start()
        attend(merged_t, mixed_t, seqs, biases_t, 4)
        twins[1].copy(2, mixed_t).start()
        loads[3].wait()
        add_residual(x_time, mixed_t, w_to, made, (2, 128))
        pack_time(made, tiles_out)
        first.start()
    with jax.named_scope("first_to_steps"):
        cot_in.wait()
        twins[0].copy(3, g_agent).start()
        loads[4].wait()
        grad_of_mixed(g_agent.at[0:256, :], w_ao, gmix)
        cot_in.drain()
        loads[5].wait()
        first.wait()
        unpack_agent(first_in, x_agent)
    with jax.named_scope("agent_backward"):
        project(x_agent, unit_a, w_aq, merged_a)
        twins[0].copy(0, unit_a).start()
        attend_back(merged_a, gmix, mixed_a, gm_a, [slice(0, 256)], [bias_a], 2)
        twins[0].copy(2, mixed_a).start()
        twins[0].copy(1, gm_a).start()
        grad_of_input(x_agent, g_agent.at[0:256, :], gm_a, w_aq, gu, cot, (256,))
        first.drain()
        pack_agent(cot, tiles_out)
        back.start()
    with jax.named_scope("agent_weights"):
        for slot, ref in enumerate((unit_a, gm_a, mixed_a, g_agent)):
            twins[0].copy(slot, ref).wait_recv()
        transposed(place, unit_a, mixed_a, ut, ut_mixed, gu)
        for stream in range(3):
            scatters[0].start(stream, ut, ut_mixed, gm_a, g_agent)
    with jax.named_scope("grad_first_to_agents"):
        for slot, ref in ((0, unit_t), (2, mixed_t)):
            twins[1].copy(slot, ref).wait_recv()
        transposed(place, unit_t, mixed_t, ut, ut_mixed, gu)
        back.wait()
        unpack_time(back_in, g_time)
        twins[1].copy_rows(3, g_time).start()
    with jax.named_scope("time_backward"):
        g_own = g_time.at[0:2]
        grad_of_mixed(g_own, w_to, gmix)
        attend_back(merged_t, gmix, None, gm_t, seqs, biases_t, 4)
        twins[1].copy(1, gm_t).start()
        for stream in range(3):
            scatters[0].pass_on(stream)
        grad_of_input(x_time, g_own, gm_t, w_tq, gu, made, (2, 128))
    with jax.named_scope("time_weights"):
        twins[1].copy(1, gm_t).wait_recv()
        twins[1].copy_rows(3, g_time).wait_recv()
        for stream in range(3):
            scatters[1].start(stream, ut, ut_mixed, gm_t, g_time)
        tokens_out.start()
    with jax.named_scope("rings"):
        outs = ((aq_ref, ao_ref), (tq_ref, to_ref))
        for stream in range(3):
            scatters[0].second(stream)
        for stream in range(3):
            scatters[1].pass_on(stream)
        for stream in range(3):
            scatters[0].third(stream)
        for stream in range(3):
            scatters[1].second(stream)
        for stream in range(3):
            scatters[0].last(stream, *outs[0])
        for stream in range(3):
            scatters[1].third(stream)
        for stream in range(3):
            scatters[1].last(stream, *outs[1])
        tokens_out.wait()
    with jax.named_scope("drain"):
        for s in range(2):
            scatters[s].drain()
        for slot, ref in enumerate((unit_a, gm_a, mixed_a, g_agent)):
            twins[0].copy(slot, ref).wait_send()
        for slot, ref in enumerate((unit_t, gm_t, mixed_t)):
            twins[1].copy(slot, ref).wait_send()
        twins[1].copy_rows(3, g_time).wait_send()
        for moved in (tokens_in, back, tokens_out):
            moved.drain()


def hand_on(*refs):
    for source, target in zip(refs[:5], refs[5:]):
        target[...] = source[...]


def local(tokens, cotangent, observed, time_qkv, time_out, agent_qkv, agent_out):
    shape = jax.ShapeDtypeStruct
    grad_tokens, *grads = pl.pallas_call(
        block_kernel,
        out_shape=[
            shape((16, 16, D), BF),
            shape((8, 3 * D), F32),
            shape((8, D), F32),
            shape((8, 3 * D), F32),
            shape((8, D), F32),
        ],
        in_specs=[
            pl.BlockSpec(memory_space=pl.ANY)
        ]
        * 7,
        out_specs=[pl.BlockSpec(memory_space=pl.ANY)] + [pl.BlockSpec(memory_space=pltpu.VMEM)] * 4,
        scratch_shapes=[
            pltpu.VMEM((D, 3 * D), BF),
            pltpu.VMEM((D, D), BF),
            pltpu.VMEM((D, 3 * D), BF),
            pltpu.VMEM((D, D), BF),
            pltpu.VMEM((2, 128, D), BF),
            pltpu.VMEM((2, 128, D), BF),
            pltpu.VMEM((256, D), BF),
            pltpu.VMEM((256, D), BF),
            pltpu.VMEM((256, D), BF),
            pltpu.VMEM((128, 16, 128), BF),
            pltpu.VMEM((128, 16, 128), BF),
            pltpu.VMEM((128, 16, 128), BF),
            pltpu.VMEM((256, 3 * D), BF),
            pltpu.VMEM((256, 3 * D), BF),
            pltpu.VMEM((256, D), BF),
            pltpu.VMEM((256, D), F32),
            pltpu.VMEM((2, 128, 128), F32),
            pltpu.VMEM((256, 256), F32),
            pltpu.VMEM((256, STEPS), jnp.int32),
            pltpu.VMEM((2, 512, D), BF),
            pltpu.VMEM((2, 512, 3 * D), BF),
            pltpu.VMEM((2, 512, D), BF),
            pltpu.VMEM((4, 128, D), BF),
            pltpu.VMEM((512, D), BF),
        ]
        + [pltpu.VMEM((3, 128, 4096), BF)]
        + scatter_bufs()
        + scatter_bufs()
        + [
            pltpu.SemaphoreType.DMA((6,)),
            pltpu.SemaphoreType.DMA((2,)),
            pltpu.SemaphoreType.DMA((2,)),
            pltpu.SemaphoreType.DMA((3, 16)),
            pltpu.SemaphoreType.DMA((3, 16)),
            pltpu.SemaphoreType.DMA((2, 4)),
            pltpu.SemaphoreType.DMA((2, 4)),
            pltpu.SemaphoreType.DMA((2, 3, 12)),
            pltpu.SemaphoreType.DMA((2, 3, 12)),
        ],
        compiler_params=pltpu.CompilerParams(
            collective_id=0, has_side_effects=True, vmem_limit_bytes=61 * 1024 * 1024
        ),
    )(
        tokens.reshape(16, 16, D),
        cotangent.reshape(256, D),
        observed.reshape(256, STEPS),
        time_qkv,
        time_out,
        agent_qkv,
        agent_out,
    )
    made = [grad_tokens, *grads]
    grad_tokens, *grads = pl.pallas_call(
        hand_on,
        out_shape=[shape(x.shape, x.dtype) for x in made],
        in_specs=[pl.BlockSpec(memory_space=pltpu.VMEM)] * 5,
        out_specs=[pl.BlockSpec(memory_space=pltpu.VMEM)] * 5,
    )(*made)
    return (grad_tokens.reshape(1, 16, 16, D), *grads)


def solution(mesh):
    in_specs = (P(None, "ag", "tm", None), P(None, "ag", "tm", None), P(), P(), P(), P(), P())
    out_specs = (
        P(None, "ag", "tm", None),
        P(("ag", "tm"), None),
        P(("ag", "tm"), None),
        P(("ag", "tm"), None),
        P(("ag", "tm"), None),
    )
    return jax.shard_map(local, mesh=mesh, in_specs=in_specs, out_specs=out_specs, check_vma=False)
```

```python
import functools

import jax
import jax.numpy as jnp
from jax import lax
from jax.experimental import pallas as pl
from jax.experimental.pallas import tpu as pltpu
from jax.sharding import PartitionSpec as P

D = 1024
H = 16
HD = 64
STEPS = 128
epsilon = 1e-06
masked_score = -1e30

MESH = pl.DeviceIdType.MESH
BF = jnp.bfloat16
F32 = jnp.float32
NT = (((1,), (1,)), ((), ()))
TN = (((0,), (0,)), ((), ()))

STREAMS = ((0, 1280, "xyz"), (1280, 2816, "yzx"), (2816, 4096, "zxy"))


def matmul(left, right, dims=(((1,), (0,)), ((), ()))):
    return lax.dot_general(left, right, dims, preferred_element_type=F32)


class Place:
    def __init__(self):
        self.ag = lax.axis_index("ag")
        self.tm = lax.axis_index("tm")
        self.y = self.ag // 4
        self.zlo = (self.ag // 2) % 2
        self.core = self.ag % 2
        self.zhi = self.tm // 4
        self.x = self.tm % 4
        self.z = self.zhi * 2 + self.zlo

    def at(self, axis):
        return {"x": self.x, "y": self.y, "z": self.z}[axis]

    def ring(self, axis, step):
        if axis == "x":
            return (self.ag, self.zhi * 4 + (self.x + step) % 4)
        if axis == "y":
            return (((self.y + step) % 4) * 4 + self.ag % 4, self.tm)
        z = (self.z + step) % 4
        return (self.y * 4 + (z % 2) * 2 + self.core, (z // 2) * 4 + self.x)

    def twin(self):
        return (self.ag + 1 - 2 * self.core, self.tm)


def remote(src, dst, send, recv, device):
    return pltpu.make_async_remote_copy(
        src_ref=src, dst_ref=dst, send_sem=send, recv_sem=recv, device_id=device, device_id_type=MESH
    )


def greet(devices):
    barrier = pltpu.get_barrier_semaphore()
    for device in devices:
        pl.semaphore_signal(barrier, inc=1, device_id=device, device_id_type=MESH)
    pl.semaphore_wait(barrier, len(devices))


def selector(core, x_first):
    at = lax.broadcasted_iota(jnp.int32, (128, 256), 0)
    row = lax.broadcasted_iota(jnp.int32, (128, 256), 1)
    high, low = at // 32, (at // 8) % 4
    x, z = (high, low) if x_first else (low, high)
    wanted = (z % 2) * 128 + core * 64 + (z // 2) * 32 + x * 8 + at % 8
    return jnp.where(row == wanted, 1.0, 0.0).astype(BF)


class Twin:
    def __init__(self, place, send, recv):
        self.place, self.send, self.recv = place, send, recv

    def copy(self, slot, ref, cols=None):
        cols = slice(None) if cols is None else cols
        return remote(
            ref.at[0:256, cols], ref.at[256:512, cols], self.send.at[slot], self.recv.at[slot], self.place.twin()
        )

    def copy_rows(self, slot, ref):
        return remote(ref.at[0:2], ref.at[2:4], self.send.at[slot], self.recv.at[slot], self.place.twin())


class Scatter:
    def __init__(self, place, block, second_block, bufs, send, recv):
        self.place, self.second_block = place, second_block
        self.block, (self.own, self.r1, self.relay, self.r2, self.s3, self.r3) = block, bufs
        self.send, self.recv = send, recv

    def first(self, stream, part):
        lo, hi, axes = STREAMS[stream]
        mid = (hi - lo) // 256 * 128
        half_a, half_b = slice(0, mid), slice(mid, hi - lo)
        all_a, all_b = slice(lo, lo + mid), slice(lo + mid, hi)
        slot, near, far = (
            (1, half_a, self.relay.at[:, all_a]),
            (1, half_b, self.relay.at[:, all_b]),
            (0, half_b, self.r1.at[0, :, all_b]),
            (2, half_a, self.r1.at[1, :, all_a]),
            (0, half_a, self.r1.at[0, :, all_a]),
            (2, half_b, self.r1.at[1, :, all_b]),
        )[part]
        return remote(
            self.block(stream, slot).at[:, near], far, self.send.at[stream, part], self.recv.at[stream, part],
            self.place.ring(axes[0], 3 if part % 2 else 1),
        )

    def copy(self, stream, phase, step):
        lo, hi, axes = STREAMS[stream]
        cols = slice(lo, hi)
        axis = axes[phase]
        to = (self.place.at(axis) + step) % 4
        slot = step - 1
        if phase == 1:
            src = self.second_block(stream).at[pl.ds(pl.multiple_of(to * 32, 32), 32), :]
            dst = self.r2.at[slot, :, cols]
        else:
            src, dst = self.s3.at[to, :, cols], self.r3.at[slot, :, cols]
        sem = 3 + 3 * phase + slot
        return remote(
            src, dst, self.send.at[stream, sem], self.recv.at[stream, sem], self.place.ring(axis, step)
        )

    def product(self, stream, ut, ut_mixed, gm, g, block):
        lo, hi, _ = STREAMS[stream]
        rows = pl.ds(pl.multiple_of(block * 128, 128), 128)
        if stream < 2:
            return [(lo, hi, matmul(ut[stream][rows, :], gm[:, lo:hi]))]
        return [
            (lo, 3072, matmul(ut[2][rows, :], gm[:, lo:3072])),
            (3072, 4096, matmul(ut_mixed[rows, :], g[...].reshape(512, D))),
        ]

    def start(self, stream, ut, ut_mixed, gm, g):
        first, _, axes = STREAMS[stream]
        at = self.place.at(axes[0])
        for step, parts in ((2, (0, 1)), (1, (2,)), (3, (3,))):
            for lo, hi, made in self.product(stream, ut, ut_mixed, gm, g, (at + step) % 4):
                self.block(stream, step - 1)[:, lo - first : hi - first] = made.astype(BF)
            for part in parts:
                self.first(stream, part).start()
        for lo, hi, made in self.product(stream, ut, ut_mixed, gm, g, at):
            self.own[:, lo:hi] = made

    def pass_on(self, stream):
        lo, hi, _ = STREAMS[stream]
        mid = (hi - lo) // 256 * 128
        for part, slot, left, right in ((0, 0, 0, mid), (1, 2, mid, hi - lo)):
            self.first(stream, part).wait_recv()
            block = self.block(stream, slot)
            came = self.relay[:, lo + left : lo + right].astype(F32)
            block[:, left:right] = (block[:, left:right].astype(F32) + came).astype(BF)
            self.first(stream, part + 4).start()

    def second(self, stream):
        lo, hi, _ = STREAMS[stream]
        for part in (2, 3, 4, 5):
            self.first(stream, part).wait_recv()

        def one(q, carry):
            rows = pl.ds(pl.multiple_of(q * 32, 32), 32)
            total = self.own[rows, lo:hi]
            for slot in range(2):
                total = total + self.r1[slot, rows, lo:hi].astype(F32)
            self.own[rows, lo:hi] = total
            self.second_block(stream)[rows, :] = total.astype(BF)
            return carry

        lax.fori_loop(0, 4, one, 0)
        for step in (1, 2, 3):
            self.copy(stream, 1, step).start()

    def third(self, stream):
        lo, hi, axes = STREAMS[stream]
        for step in (1, 2, 3):
            self.copy(stream, 1, step).wait_recv()
        total = self.own[pl.ds(pl.multiple_of(self.place.at(axes[1]) * 32, 32), 32), lo:hi]
        for slot in range(3):
            total = total + self.r2[slot, :, lo:hi].astype(F32)
        self.own[0:32, lo:hi] = total
        for q in range(4):
            self.s3[q, :, lo:hi] = total[q * 8 : q * 8 + 8].astype(BF)
        for step in (1, 2, 3):
            self.copy(stream, 2, step).start()

    def last(self, stream, qkv_ref, out_ref):
        lo, hi, axes = STREAMS[stream]
        for step in (1, 2, 3):
            self.copy(stream, 2, step).wait_recv()
        total = self.own[pl.ds(pl.multiple_of(self.place.at(axes[2]) * 8, 8), 8), lo:hi]
        for slot in range(3):
            total = total + self.r3[slot, :, lo:hi].astype(F32)
        top = min(hi, 3072)
        qkv_ref[:, lo:top] = total[:, : top - lo]
        if hi > 3072:
            out_ref[...] = total[:, 3072 - lo :]

    def drain(self):
        for stream in range(3):
            for part in range(6):
                self.first(stream, part).wait_send()
            for phase in (1, 2):
                for step in (1, 2, 3):
                    self.copy(stream, phase, step).wait_send()


def scatter_bufs():
    return [
        pltpu.VMEM((128, 4096), F32),
        pltpu.VMEM((2, 128, 4096), BF),
        pltpu.VMEM((128, 4096), BF),
        pltpu.VMEM((3, 32, 4096), BF),
        pltpu.VMEM((4, 8, 4096), BF),
        pltpu.VMEM((3, 8, 4096), BF),
    ]


def transposed(place, unit, mixed, ut, ut_mixed, spare):
    sel_x = selector(place.core, True)
    sel_z = selector(place.core, False)

    def last_order(part, y):
        for z in range(4):
            for x in range(4):
                at = (z % 2) * 128 + x * 32 + y * 8
                spare[at : at + 8, (z // 2) * 512 : (z // 2) * 512 + 512] = part[z * 32 + x * 8 : z * 32 + x * 8 + 8]

    for y in range(4):
        cols = slice(y * 256, y * 256 + 256)
        part = matmul(sel_x, unit[:, cols], NT).astype(BF)
        for x in range(4):
            ut[0][x * 128 + y * 32 : x * 128 + y * 32 + 32, :] = part[x * 32 : x * 32 + 32]
        part = matmul(sel_z, unit[:, cols], NT)
        ut[1][y * 128 : y * 128 + 128, :] = part.astype(BF)
        last_order(part, y)
    ut[2][0:256, :] = spare[:, 0:512].astype(BF)
    ut[2][256:512, :] = spare[:, 512:1024].astype(BF)
    for y in range(4):
        last_order(matmul(sel_z, mixed[:, y * 256 : y * 256 + 256], NT), y)
    ut_mixed[0:256, :] = spare[:, 0:512].astype(BF)
    ut_mixed[256:512, :] = spare[:, 512:1024].astype(BF)


def normal(x_ref):
    x = x_ref[...].reshape(256, D).astype(F32)
    inverse = lax.rsqrt(jnp.mean(x * x, axis=-1, keepdims=True) + epsilon)
    return x * inverse, inverse


def span(start, size):
    return pl.ds(pl.multiple_of(start * size, size), size)


def project(x_ref, unit, w, merged):
    unit[0:256, :] = normal(x_ref)[0].astype(BF)

    def one(n, carry):
        cols = span(n, 512)
        merged[:, cols] = matmul(unit[0:256, :], w[:, cols]).astype(BF)
        return carry

    lax.fori_loop(0, 6, one, 0, unroll=6)


def halves():
    lane = lax.broadcasted_iota(jnp.int32, (1, 128), 1)
    low = jnp.where(lane < HD, 1.0, 0.0)
    return low.astype(BF), (1.0 - low).astype(BF)


def pair_parts(merged, rows, pair):
    q = merged[rows, span(pair, 128)] * BF(HD**-0.5)
    k = merged[rows, pl.ds(pl.multiple_of(D + pair * 128, 128), 128)]
    v = merged[rows, pl.ds(pl.multiple_of(2 * D + pair * 128, 128), 128)]
    return q, k, v


def attend(merged, mixed, seqs, biases, group):
    def one(turn, carry):
        low_high = halves()
        jobs = []
        for rows, bias in zip(seqs, biases):
            for i in range(group):
                pair = turn * group + i
                q, k, v = pair_parts(merged, rows, pair)
                for half in low_high:
                    jobs.append((rows, pair, bias, q * half, k, v * half))
        scores = [matmul(q, k, NT) + bias[...] for _, _, bias, q, k, _ in jobs]
        probs = probs_of(scores)
        parts = [matmul(p.astype(BF), job[5]) for p, job in zip(probs, jobs)]
        for i in range(0, len(jobs), 2):
            rows, pair = jobs[i][:2]
            mixed[rows, span(pair, 128)] = (parts[i] + parts[i + 1]).astype(BF)
        return carry

    lax.fori_loop(0, H // 2 // group, one, 0)


def probs_of(scores):
    tops = [jnp.max(s, axis=-1, keepdims=True) for s in scores]
    shifted = [jnp.exp(s - t) for s, t in zip(scores, tops)]
    sums = [jnp.sum(s, axis=-1, keepdims=True) for s in shifted]
    return [s * (1.0 / t) for s, t in zip(shifted, sums)]


def attend_back(merged, gmix, mixed, gm, seqs, biases, group):
    def one(turn, carry):
        low_high = halves()
        jobs = []
        for rows, bias in zip(seqs, biases):
            for i in range(group):
                pair = turn * group + i
                q, k, v = pair_parts(merged, rows, pair)
                go = gmix[rows, span(pair, 128)]
                for half in low_high:
                    jobs.append((rows, pair, bias, q * half, k, v, go * half, half))
        scores = [matmul(job[3], job[4], NT) + job[2][...] for job in jobs]
        gps = [matmul(job[6], job[5], NT) for job in jobs]
        probs = probs_of(scores)
        means = [jnp.sum(gp * p, axis=-1, keepdims=True) for gp, p in zip(gps, probs)]
        gss = [(p * (gp - m)).astype(BF) for p, gp, m in zip(probs, gps, means)]
        rounded = [p.astype(BF) for p in probs]
        gq = [matmul(gs, job[4] * job[7]) for gs, job in zip(gss, jobs)]
        gk = [matmul(gs, job[3], TN) for gs, job in zip(gss, jobs)]
        gv = [matmul(p, job[6], TN) for p, job in zip(rounded, jobs)]
        if mixed is not None:
            mx = [matmul(p, job[5] * job[7]) for p, job in zip(rounded, jobs)]
        for i in range(0, len(jobs), 2):
            rows, pair = jobs[i][:2]
            gm[rows, span(pair, 128)] = ((gq[i] + gq[i + 1]) * HD**-0.5).astype(BF)
            gm[rows, pl.ds(pl.multiple_of(D + pair * 128, 128), 128)] = (gk[i] + gk[i + 1]).astype(BF)
            gm[rows, pl.ds(pl.multiple_of(2 * D + pair * 128, 128), 128)] = (gv[i] + gv[i + 1]).astype(BF)
            if mixed is not None:
                mixed[rows, span(pair, 128)] = (mx[i] + mx[i + 1]).astype(BF)
        return carry

    lax.fori_loop(0, H // 2 // group, one, 0)


def add_residual(x_ref, mixed, w, out_ref, shape):
    for n in range(2):
        cols = slice(n * 512, n * 512 + 512)
        x = x_ref[..., cols].reshape(256, 512).astype(F32)
        out = x + matmul(mixed[0:256, :], w[:, cols])
        out_ref[..., cols] = out.astype(BF).reshape(shape + (512,))


def grad_of_mixed(g, w, gmix):
    def one(n, carry):
        rows = span(n, 256)
        gmix[:, rows] = matmul(g[...].reshape(256, D), w[rows, :], NT).astype(BF)
        return carry

    lax.fori_loop(0, 4, one, 0, unroll=4)


def grad_of_input(x_ref, g, gm, w, gu, out_ref, shape):
    def one(n, carry):
        rows = span(n, 512)
        gu[:, rows] = matmul(gm[0:256, :], w[rows, :], NT)
        return carry

    lax.fori_loop(0, 2, one, 0, unroll=2)
    normed, inverse = normal(x_ref)
    grad_unit = gu[...]
    rows = inverse * (grad_unit - normed * jnp.mean(grad_unit * normed, axis=-1, keepdims=True))
    out_ref[...] = (g[...].reshape(256, D).astype(F32) + rows).astype(BF).reshape(shape + (D,))


def swap_rows(src, dst):
    at = lax.broadcasted_iota(jnp.int32, (256, 256), 0)
    row = lax.broadcasted_iota(jnp.int32, (256, 256), 1)
    swap = jnp.where(row == (at % 16) * 16 + at // 16, 1.0, 0.0).astype(BF)
    for n in range(2):
        cols = slice(n * 512, n * 512 + 512)
        out = matmul(swap, src[..., cols].reshape(256, 512)).astype(BF)
        dst[..., cols] = out.reshape(dst.shape[:-1] + (512,))


class Swap:
    def __init__(self, place, axis, send, recv, source, target):
        self.place, self.axis, self.send, self.recv = place, axis, send, recv
        self.source, self.target = source, target
        self.size = 8 if axis == "tm" else 16
        self.me = place.tm if axis == "tm" else place.ag

    def copy(self, step):
        to = (self.me + step) % self.size
        device = (self.place.ag, to) if self.axis == "tm" else (to, self.place.tm)
        return remote(self.source(to), self.target(self.me), self.send.at[step], self.recv.at[step], device)

    def local(self):
        return pltpu.make_async_copy(self.source(self.me), self.target(self.me), self.recv.at[0])

    def start(self):
        def one(step, carry):
            self.copy(step).start()
            return carry

        lax.fori_loop(1, self.size, one, 0)
        self.local().start()

    def wait(self):
        def one(step, carry):
            self.copy(step).wait_recv()
            return carry

        lax.fori_loop(1, self.size, one, 0)
        self.local().wait()

    def drain(self):
        def one(step, carry):
            self.copy(step).wait_send()
            return carry

        lax.fori_loop(1, self.size, one, 0)


def spread_index():
    at = lax.broadcasted_iota(jnp.int32, (256, 256), 0)
    row = lax.broadcasted_iota(jnp.int32, (256, 256), 1)
    return at, row


def one_hot(wanted, row):
    return jnp.where(row == wanted, 1.0, 0.0).astype(BF)


def pack_time(src, dst):
    at, row = spread_index()
    i, c, a = at // 16, (at // 2) % 8, at % 2
    turn = one_hot(c * 32 + a * 16 + i, row)

    def one(n, carry):
        rows = span(n, 16)
        parts = [src[a, rows, c * 128 : c * 128 + 128] for c in range(8) for a in range(2)]
        out = matmul(turn, jnp.concatenate(parts, axis=0)).astype(BF)
        dst[rows] = out.reshape(16, 16, 128)
        return carry

    lax.fori_loop(0, 8, one, 0, unroll=8)


def unpack_time(src, dst):
    at, row = spread_index()
    c, a, i = at // 32, (at // 16) % 2, at % 16
    turn = one_hot(i * 16 + c * 2 + a, row)

    def one(n, carry):
        rows = span(n, 16)
        out = matmul(turn, src[rows].reshape(256, 128)).astype(BF)
        for c in range(8):
            for a in range(2):
                part = out[c * 32 + a * 16 : c * 32 + a * 16 + 16]
                dst[a, rows, c * 128 : c * 128 + 128] = part
        return carry

    lax.fori_loop(0, 8, one, 0, unroll=8)


def pack_agent(src, dst):
    at, row = spread_index()
    i, c, a = at // 16, (at // 2) % 8, at % 2
    turn = one_hot(c * 32 + i * 2 + a, row)

    def one(n, carry):
        parts = [src[span(n, 32), c * 128 : c * 128 + 128] for c in range(8)]
        out = matmul(turn, jnp.concatenate(parts, axis=0)).astype(BF)
        dst[span(n, 16)] = out.reshape(16, 16, 128)
        return carry

    lax.fori_loop(0, 8, one, 0, unroll=8)


def unpack_agent(src, dst):
    at, row = spread_index()
    c, i, a = at // 32, (at // 2) % 16, at % 2
    turn = one_hot(i * 16 + c * 2 + a, row)

    def one(n, carry):
        out = matmul(turn, src[span(n, 16)].reshape(256, 128)).astype(BF)
        for c in range(8):
            dst[span(n, 32), c * 128 : c * 128 + 128] = out[c * 32 : c * 32 + 32]
        return carry

    lax.fori_loop(0, 8, one, 0, unroll=8)


class Spread:
    def __init__(self, place, send, recv, src, dst, to_steps):
        self.place, self.send, self.recv, self.src, self.dst, self.to_steps = place, send, recv, src, dst, to_steps

    def places(self, ag, tm):
        return ag * 8 + tm, tm * 16 + ag

    def start(self):
        place = self.place
        agents, steps = self.places(place.ag, place.tm)
        mine = agents if self.to_steps else steps

        def one(step, carry):
            ag, tm = (place.ag + step // 8) % 16, (place.tm + step % 8) % 8
            by_agents, by_steps = self.places(ag, tm)
            theirs = by_steps if self.to_steps else by_agents
            remote(self.src.at[theirs], self.dst.at[mine], self.send, self.recv, (ag, tm)).start()
            return carry

        lax.fori_loop(1, 128, one, 0)
        own = steps if self.to_steps else agents
        pltpu.make_async_copy(self.src.at[own], self.dst.at[mine], self.recv).start()

    def wait(self):
        pltpu.make_async_copy(self.src, self.dst, self.recv).wait()

    def drain(self):
        pltpu.make_async_copy(self.src.at[0:127], self.dst.at[0:127], self.send).wait()


def block_kernel(
    tokens, cotangent, observed_in, time_qkv, time_out, agent_qkv, agent_out,
    grad_tokens, tq_ref, to_ref, aq_ref, ao_ref,
    w_tq, w_to, w_aq, w_ao,
    x_time, made, turned, x_agent, cot, tiles_out, first_in, back_in,
    merged_t, merged_a, gmix, gu, bias_t, bias_a, observed,
    units, gms, mixeds, g_time, g_agent,
    *rest,
):
    grad_a = rest[0]
    bufs = (rest[1:7], rest[7:13])
    load, spread_send, spread_recv, swap_send, swap_recv, twin_send, twin_recv, sc_send, sc_recv = rest[13:]
    place = Place()
    loads = [
        pltpu.make_async_copy(src, dst, load.at[i])
        for i, (src, dst) in enumerate(
            (
                (cotangent, cot),
                (observed_in, observed),
                (time_qkv, w_tq),
                (time_out, w_to),
                (agent_out, w_ao),
                (agent_qkv, w_aq),
            )
        )
    ]
    for copy in loads:
        copy.start()
    far = [
        (place.y * 4 + (1 - place.zlo) * 2 + place.core, (1 - place.zhi) * 4 + place.x),
    ]
    greet(
        [((place.ag + step) % 16, place.tm) for step in range(1, 16)]
        + [(place.ag, (place.tm + step) % 8) for step in range(1, 8)]
        + far
    )

    def swap(slot, axis, source, target):
        return Swap(place, axis, swap_send.at[slot], swap_recv.at[slot], source, target)

    def two(ref):
        return lambda i: ref.at[pl.ds(i * 2, 2)]

    def sixteen(ref):
        return lambda i: ref.at[0:2, span(i, 16), :]

    def rows16(ref):
        return lambda i: ref.at[span(i, 16), :]

    tokens_in = swap(0, "tm", two(tokens), sixteen(x_time))
    cot_in = swap(1, "ag", rows16(turned), rows16(g_agent))
    first = Spread(place, spread_send.at[0], spread_recv.at[0], tiles_out, first_in, True)
    back = Spread(place, spread_send.at[1], spread_recv.at[1], tiles_out, back_in, False)
    tokens_out = swap(2, "tm", sixteen(made), two(grad_tokens))
    twins = [Twin(place, twin_send.at[s], twin_recv.at[s]) for s in range(2)]

    def block_a(stream, slot):
        lo, hi, _ = STREAMS[stream]
        return grad_a.at[slot, :, lo:hi]

    def block_t(stream, slot):
        lo, hi, _ = STREAMS[stream]
        if stream < 2:
            return w_aq.at[span(slot, 128), lo:hi]
        return w_aq.at[span(slot + 4, 128), 0 : hi - lo]

    def second_a(stream):
        lo, hi, _ = STREAMS[stream]
        return w_aq.at[512 + stream * 128 : 640 + stream * 128, 1408 : 1408 + hi - lo]

    def second_t(stream):
        lo, hi, _ = STREAMS[stream]
        if stream < 2:
            return w_aq.at[384:512, lo:hi]
        return w_aq.at[896:1024, 0 : hi - lo]

    blocks, seconds = (block_a, block_t), (second_a, second_t)
    scatters = [Scatter(place, blocks[s], seconds[s], bufs[s], sc_send.at[s], sc_recv.at[s]) for s in range(2)]
    unit_a, unit_t = units.at[0], units.at[1]
    gm_a, gm_t = gms.at[0], gms.at[1]
    mixed_a, mixed_t = mixeds.at[0], mixeds.at[1]
    ut = [w_ao.at[0:512, 0:512], w_ao.at[0:512, 512:1024], w_ao.at[512:1024, 0:512]]
    ut_mixed = w_ao.at[512:1024, 512:1024]
    seqs = [slice(0, 128), slice(128, 256)]
    biases_t = [bias_t.at[0], bias_t.at[1]]

    with jax.named_scope("tokens_to_agents"):
        tokens_in.start()
        loads[0].wait()
        swap_rows(cot, turned)
        loads[1].wait()
        self_t = lax.broadcasted_iota(jnp.int32, (128, 128), 0) == lax.broadcasted_iota(jnp.int32, (128, 128), 1)
        for a in range(2):
            row = observed[pl.ds(place.ag * 16 + place.tm * 2 + a, 1), :]
            bias_t[a] = jnp.where((row > 0) | self_t, 0.0, masked_score)
        at_step = lax.broadcasted_iota(jnp.int32, (8, STEPS), 1) == place.tm * 16 + place.ag
        seen = matmul(jnp.where(at_step, 1.0, 0.0).astype(BF), observed[...].astype(F32).astype(BF), NT)
        self_a = lax.broadcasted_iota(jnp.int32, (256, 256), 0) == lax.broadcasted_iota(jnp.int32, (256, 256), 1)
        bias_a[...] = jnp.where((seen[0:1, :] > 0.5) | self_a, 0.0, masked_score)
        loads[2].wait()
        tokens_in.wait()
        cot_in.start()
    with jax.named_scope("time_forward"):
        project(x_time, unit_t, w_tq, merged_t)
        twins[1].copy(0, unit_t).start()
        attend(merged_t, mixed_t, seqs, biases_t, 4)
        twins[1].copy(2, mixed_t).start()
        loads[3].wait()
        add_residual(x_time, mixed_t, w_to, made, (2, 128))
        pack_time(made, tiles_out)
        first.start()
    with jax.named_scope("first_to_steps"):
        cot_in.wait()
        twins[0].copy(3, g_agent).start()
        loads[4].wait()
        grad_of_mixed(g_agent.at[0:256, :], w_ao, gmix)
        cot_in.drain()
        loads[5].wait()
        first.wait()
        unpack_agent(first_in, x_agent)
    with jax.named_scope("agent_backward"):
        project(x_agent, unit_a, w_aq, merged_a)
        twins[0].copy(0, unit_a).start()
        attend_back(merged_a, gmix, mixed_a, gm_a, [slice(0, 256)], [bias_a], 2)
        twins[0].copy(2, mixed_a).start()
        twins[0].copy(1, gm_a).start()
        grad_of_input(x_agent, g_agent.at[0:256, :], gm_a, w_aq, gu, cot, (256,))
        first.drain()
        pack_agent(cot, tiles_out)
        back.start()
    with jax.named_scope("agent_weights"):
        for slot, ref in enumerate((unit_a, gm_a, mixed_a, g_agent)):
            twins[0].copy(slot, ref).wait_recv()
        transposed(place, unit_a, mixed_a, ut, ut_mixed, gu)
        for stream in range(3):
            scatters[0].start(stream, ut, ut_mixed, gm_a, g_agent)
    with jax.named_scope("grad_first_to_agents"):
        for slot, ref in ((0, unit_t), (2, mixed_t)):
            twins[1].copy(slot, ref).wait_recv()
        transposed(place, unit_t, mixed_t, ut, ut_mixed, gu)
        back.wait()
        unpack_time(back_in, g_time)
        twins[1].copy_rows(3, g_time).start()
    with jax.named_scope("time_backward"):
        g_own = g_time.at[0:2]
        grad_of_mixed(g_own, w_to, gmix)
        attend_back(merged_t, gmix, None, gm_t, seqs, biases_t, 4)
        twins[1].copy(1, gm_t).start()
        for stream in range(3):
            scatters[0].pass_on(stream)
        grad_of_input(x_time, g_own, gm_t, w_tq, gu, made, (2, 128))
        tokens_out.start()
        for stream in range(3):
            scatters[0].second(stream)
    with jax.named_scope("time_weights"):
        twins[1].copy(1, gm_t).wait_recv()
        twins[1].copy_rows(3, g_time).wait_recv()
        for stream in range(3):
            scatters[1].start(stream, ut, ut_mixed, gm_t, g_time)
    with jax.named_scope("rings"):
        outs = ((aq_ref, ao_ref), (tq_ref, to_ref))
        for stream in range(3):
            scatters[0].third(stream)
        for stream in range(3):
            scatters[1].pass_on(stream)
        for stream in range(3):
            scatters[1].second(stream)
        for stream in range(3):
            scatters[0].last(stream, *outs[0])
        for stream in range(3):
            scatters[1].third(stream)
        for stream in range(3):
            scatters[1].last(stream, *outs[1])
        tokens_out.wait()
    with jax.named_scope("drain"):
        for s in range(2):
            scatters[s].drain()
        for slot, ref in enumerate((unit_a, gm_a, mixed_a, g_agent)):
            twins[0].copy(slot, ref).wait_send()
        for slot, ref in enumerate((unit_t, gm_t, mixed_t)):
            twins[1].copy(slot, ref).wait_send()
        twins[1].copy_rows(3, g_time).wait_send()
        for moved in (tokens_in, back, tokens_out):
            moved.drain()


def hand_on(*refs):
    for source, target in zip(refs[:5], refs[5:]):
        target[...] = source[...]


def local(tokens, cotangent, observed, time_qkv, time_out, agent_qkv, agent_out):
    shape = jax.ShapeDtypeStruct
    grad_tokens, *grads = pl.pallas_call(
        block_kernel,
        out_shape=[
            shape((16, 16, D), BF),
            shape((8, 3 * D), F32),
            shape((8, D), F32),
            shape((8, 3 * D), F32),
            shape((8, D), F32),
        ],
        in_specs=[
            pl.BlockSpec(memory_space=pl.ANY)
        ]
        * 7,
        out_specs=[pl.BlockSpec(memory_space=pl.ANY)] + [pl.BlockSpec(memory_space=pltpu.VMEM)] * 4,
        scratch_shapes=[
            pltpu.VMEM((D, 3 * D), BF),
            pltpu.VMEM((D, D), BF),
            pltpu.VMEM((D, 3 * D), BF),
            pltpu.VMEM((D, D), BF),
            pltpu.VMEM((2, 128, D), BF),
            pltpu.VMEM((2, 128, D), BF),
            pltpu.VMEM((256, D), BF),
            pltpu.VMEM((256, D), BF),
            pltpu.VMEM((256, D), BF),
            pltpu.VMEM((128, 16, 128), BF),
            pltpu.VMEM((128, 16, 128), BF),
            pltpu.VMEM((128, 16, 128), BF),
            pltpu.VMEM((256, 3 * D), BF),
            pltpu.VMEM((256, 3 * D), BF),
            pltpu.VMEM((256, D), BF),
            pltpu.VMEM((256, D), F32),
            pltpu.VMEM((2, 128, 128), F32),
            pltpu.VMEM((256, 256), F32),
            pltpu.VMEM((256, STEPS), jnp.int32),
            pltpu.VMEM((2, 512, D), BF),
            pltpu.VMEM((2, 512, 3 * D), BF),
            pltpu.VMEM((2, 512, D), BF),
            pltpu.VMEM((4, 128, D), BF),
            pltpu.VMEM((512, D), BF),
        ]
        + [pltpu.VMEM((3, 128, 4096), BF)]
        + scatter_bufs()
        + scatter_bufs()
        + [
            pltpu.SemaphoreType.DMA((6,)),
            pltpu.SemaphoreType.DMA((2,)),
            pltpu.SemaphoreType.DMA((2,)),
            pltpu.SemaphoreType.DMA((3, 16)),
            pltpu.SemaphoreType.DMA((3, 16)),
            pltpu.SemaphoreType.DMA((2, 4)),
            pltpu.SemaphoreType.DMA((2, 4)),
            pltpu.SemaphoreType.DMA((2, 3, 12)),
            pltpu.SemaphoreType.DMA((2, 3, 12)),
        ],
        compiler_params=pltpu.CompilerParams(
            collective_id=0, has_side_effects=True, vmem_limit_bytes=61 * 1024 * 1024
        ),
    )(
        tokens.reshape(16, 16, D),
        cotangent.reshape(256, D),
        observed.reshape(256, STEPS),
        time_qkv,
        time_out,
        agent_qkv,
        agent_out,
    )
    made = [grad_tokens, *grads]
    grad_tokens, *grads = pl.pallas_call(
        hand_on,
        out_shape=[shape(x.shape, x.dtype) for x in made],
        in_specs=[pl.BlockSpec(memory_space=pltpu.VMEM)] * 5,
        out_specs=[pl.BlockSpec(memory_space=pltpu.VMEM)] * 5,
    )(*made)
    return (grad_tokens.reshape(1, 16, 16, D), *grads)


def solution(mesh):
    in_specs = (P(None, "ag", "tm", None), P(None, "ag", "tm", None), P(), P(), P(), P(), P())
    out_specs = (
        P(None, "ag", "tm", None),
        P(("ag", "tm"), None),
        P(("ag", "tm"), None),
        P(("ag", "tm"), None),
        P(("ag", "tm"), None),
    )
    return jax.shard_map(local, mesh=mesh, in_specs=in_specs, out_specs=out_specs, check_vma=False)
```
